32 devices in a mesh: expert: 16 (over z, y, x), shard: 2 (over core).
Axes of the slice: x: 2, y: 2, z: 4, core: 2. Of those that a mesh axis runs over, the one named last changes fastest.
Arguments:
- tokens: bfloat16 [2, 2048, 2048], P('shard', 'expert'), may hold values from -6 to 6
- lengths: int32 [2, 2], P('shard'), may hold values from 0 to 2048, as said below
- routes: int32 [2, 2048, 6], P('shard', 'expert'), may hold values from 0 to 15, all different within a row; in each aligned block of 128 rows (0 to 127, 128 to 255, ..., all dimensions but the last counted through in order) at most 54 rows name the same one
- attn_gain: bfloat16 [2048], P('shard'), may hold values from 0.5 to 1.5
- query_weight: bfloat16 [2048, 3072], P('shard'), may hold values from -0.25 to 0.25
- latent_weight: bfloat16 [2048, 576], P('shard'), may hold values from -0.125 to 0.125
- latent_gain: bfloat16 [512], P('shard'), may hold values from 0.5 to 1.5
- expand_weight: bfloat16 [512, 4096], P('shard'), may hold values from -0.25 to 0.25
- output_weight: bfloat16 [2048, 2048], P('shard'), may hold values from -2 to 2
- ffn_gain: bfloat16 [2048], P('shard'), may hold values from 0.5 to 1.5
- router_weight: bfloat16 [2048, 16], P('shard'), may hold values from -0.0625 to 0.0625
- shared_in: bfloat16 [2048, 5632], P('shard'), may hold values from -0.125 to 0.125
- shared_out: bfloat16 [2816, 2048], P('shard'), may hold values from -0.21875 to 0.21875
- expert_in: bfloat16 [16, 2048, 2, 1408], P('expert', None, None, 'shard'), may hold values from -0.125 to 0.125
- expert_out: bfloat16 [16, 1408, 2048], P('expert', 'shard'), may hold values from -2.5 to 2.5
- cotangent: bfloat16 [2, 2048, 2048], P('shard', 'expert'), may hold values from -6 to 6
Outputs:
- block_out: bfloat16 [2, 2048, 2048], P('shard', 'expert')
- tokens_grad: bfloat16 [2, 2048, 2048], P('shard', 'expert')
- grad_attn_gain: float32 [2048], P(('expert', 'shard'))
- grad_query_weight: float32 [2048, 3072], P(('expert', 'shard'))
- grad_latent_weight: float32 [2048, 576], P(('expert', 'shard'))
- grad_latent_gain: float32 [512], P(('expert', 'shard'))
- grad_expand_weight: float32 [512, 4096], P(('expert', 'shard'))
- grad_output_weight: float32 [2048, 2048], P(('expert', 'shard'))
- grad_ffn_gain: float32 [2048], P(('expert', 'shard'))
- grad_router_weight: float32 [2048, 16], P(('expert', 'shard'))
- grad_shared_in: float32 [2048, 5632], P(('expert', 'shard'))
- grad_shared_out: float32 [2816, 2048], P(('expert', 'shard'))
- grad_expert_in: float32 [16, 2048, 2, 1408], P('expert', None, None, 'shard')
- grad_expert_out: float32 [16, 1408, 2048], P('expert', 'shard')
The draws below stay inside these ranges and needn't reach their ends.
Inputs may be any that keep to these rules, and one draw needn't show every extreme that they name: `lengths`: A slot holds either one sequence of 1024 to 2048 tokens, its second entry 0, or two sequences of 1024 and 1024 tokens; the first slot holds one sequence of 2048 tokens. `routes`: every token names 6 different experts; the 128 tokens of one device name any one expert at most 54 times, and in some devices' tokens one expert exactly 54 times.
All inputs are finite; a program needn't handle non-finite values.
Results may differ from the reference program's by a relative error of at most 0.025.
Values may be sent and summed in bfloat16 or wider, within the bound.
A program may use at most 384 MiB of HBM per device.

```python
import math
import jax
import jax.numpy as jnp
import numpy as np
from jax import lax

D = 2048
HEADS = 16
HEAD = 128
ROPE = 64
VHEAD = 128
RANK = 512
FF_E = 1408
FF_S = 2816
TOPK = 6
SLOT = 2048
EXPERTS = 16
SLOTS = 2
TOK_DEV = 128
CAP = 54
N_EXPERT = 16
N_SHARD = 2


def draw_lengths(key, part):
    keys = jax.random.split(key, 2)
    half_len = SLOT // 2
    single_len = jax.random.randint(keys[0], (SLOTS,), half_len, SLOT + 1).astype(jnp.int32)
    paired = jax.random.randint(keys[1], (SLOTS,), 0, 2).astype(jnp.int32)
    paired = paired.at[0].set(0)
    single_len = single_len.at[0].set(SLOT)
    first_len = jnp.where(paired == 1, half_len, single_len)
    second_len = jnp.where(paired == 1, SLOT - half_len, 0)
    return jnp.stack([first_len, second_len], -1).astype(jnp.int32)


def levels(own_key, dims, cuts, smallest, largest):
    def one(position, shards_of):
        draws = jax.random.uniform(jax.random.fold_in(jax.random.fold_in(own_key, 6), position), (shards_of,), jnp.float32, smallest / len(cuts), largest / len(cuts))
        return jnp.repeat(jnp.exp(draws), dims[position] // shards_of).reshape((-1,) + (1,) * (len(dims) - position - 1))

    level = one(*cuts[0])
    for cut in cuts[1:]:
        level = level * one(*cut)
    return level


def routed_block(key, own, number, rows, amount, top, limit, slope):
    ranking = jax.random.permutation(key, amount)
    crowded, usual = load_shares(amount, rows * top, limit, slope, True), load_shares(amount, rows * top, limit, slope, False)
    places = jnp.arange(amount)

    def named(sizes, offset_by):
        used = int((sizes > 0).sum())
        fixed = max(1, used // 4)
        moved = fixed + (places - fixed + offset_by * (used - fixed)) % max(1, amount - fixed)
        return jnp.zeros((amount,), jnp.int32).at[ranking[jnp.where(places < fixed, places, moved)]].set(jnp.asarray(sizes, jnp.int32))

    sizes = jnp.where(number % 4 == 0, named(crowded, number // 4), named(usual, number - number // 4 - 1))
    mixed = jax.random.permutation(jax.random.fold_in(own, 3), amount)
    giver, sink = mixed[0:amount // 2 * 2:2], mixed[1:amount // 2 * 2:2]
    slack = jnp.minimum(sizes[giver] - 1, limit - sizes[sink]) // 2
    slack = jnp.where((giver == ranking[0]) | (sink == ranking[0]) | (sizes[sink] == 0), 0, jnp.maximum(slack, 0))
    moved = jax.random.randint(jax.random.fold_in(own, 4), (amount // 2,), 0, 1 << 20) % (slack + 1)
    sizes = sizes.at[giver].add(-moved).at[sink].add(moved)
    members = jnp.searchsorted(jnp.cumsum(sizes), jnp.arange(rows * top), side="right").astype(jnp.int32)
    table = members.reshape(top, rows).T
    table = table[jax.random.permutation(jax.random.fold_in(own, 1), rows)]
    offset_by = jax.random.randint(jax.random.fold_in(own, 2), (rows, 1), 0, top)
    return jnp.take_along_axis(table, (jnp.arange(top)[None, :] + offset_by) % top, axis=1)


def load_shares(amount, total, limit, lean, full):
    weights = [(1 << 20) // math.isqrt(grade ** lean) + 1 for grade in range(1, amount + 1)]
    largest = limit if full else min(limit, max(-(-total // amount), total * weights[0] // sum(weights)))
    least = 1 if total - largest >= amount - 1 else 0
    holding, spare = [largest] + [least] * (amount - 1), total - largest - least * (amount - 1)
    while spare > 0:
        free = [i for i in range(1, amount) if holding[i] < largest] or [i for i in range(1, amount) if holding[i] < limit]
        whole, left = sum([weights[i] for i in free]), spare
        for i in free:
            addition = min(limit - holding[i], max(1, left * weights[i] // whole), spare)
            holding[i] = holding[i] + addition
            spare = spare - addition
    return np.array(holding)


def noise(key, extent, scale, limit, cuts=(), held_as=jnp.bfloat16):
    values = jax.random.normal(key, extent, jnp.float32) * scale
    if len(cuts) > 0:
        values = levels(key, extent, cuts, -0.22, 0.18) * values
    return jnp.clip(values, min=-limit, max=limit).astype(held_as)


def setup_inputs(seed: int = 0) -> dict:
    key_of = jax.random.split(jax.random.key(seed), 17)
    tokens = noise(key_of[0], (SLOTS, SLOT, D), 1.0, 6.0, ((0, 2), (1, 16)))
    lengths = draw_lengths(jax.random.fold_in(key_of[16], 71), 0)
    routes_keys = jax.random.split(jax.random.fold_in(key_of[2], 1), SLOTS * SLOT // TOK_DEV)
    routes_turns = jax.random.permutation(jax.random.fold_in(key_of[2], 3), SLOTS * SLOT // TOK_DEV)
    routes = jax.vmap(lambda own, number: routed_block(jax.random.fold_in(key_of[2], 2), own, number, TOK_DEV, EXPERTS, TOPK, CAP, 1))(routes_keys, routes_turns).reshape((SLOTS, SLOT, TOPK))
    attn_gain = jnp.clip(1.0 + 0.1 * jax.random.normal(key_of[3], (D,), jnp.float32), 0.5, 1.5).astype(jnp.bfloat16)
    query_weight = noise(key_of[4], (D, HEADS * (HEAD + ROPE)), (D // 4) ** -0.5, 0.25, ((0, 2),))
    latent_weight = noise(key_of[5], (D, RANK + ROPE), D ** -0.5, 0.125, ((0, 2),))
    latent_gain = jnp.clip(1.0 + 0.1 * jax.random.normal(key_of[6], (RANK,), jnp.float32), 0.5, 1.5).astype(jnp.bfloat16)
    expand_weight = noise(key_of[7], (RANK, HEADS * (HEAD + VHEAD)), RANK ** -0.5, 0.25, ((0, 2),))
    output_weight = noise(key_of[8], (HEADS * VHEAD, D), (max(1, HEADS * VHEAD // 256)) ** -0.5, 2.0, ((0, 2),))
    ffn_gain = jnp.clip(1.0 + 0.1 * jax.random.normal(key_of[9], (D,), jnp.float32), 0.5, 1.5).astype(jnp.bfloat16)
    router_weight = noise(key_of[10], (D, EXPERTS), (4 * D) ** -0.5, 0.0625, ((0, 2),))
    shared_in = noise(key_of[11], (D, 2 * FF_S), D ** -0.5, 0.125, ((0, 2),))
    shared_out = noise(key_of[12], (FF_S, D), (max(1, FF_S // 4)) ** -0.5, 0.21875, ((0, 2),))
    expert_in = noise(key_of[13], (EXPERTS, D, 2, FF_E), D ** -0.5, 0.125, ((0, 16), (3, 2)))
    expert_out = noise(key_of[14], (EXPERTS, FF_E, D), (max(1, FF_E // 256)) ** -0.5, 2.5, ((0, 16), (1, 2)))
    cotangent = noise(key_of[15], (SLOTS, SLOT, D), 1.0, 6.0, ((0, 2), (1, 16)))
    return dict(tokens=tokens, lengths=lengths, routes=routes, attn_gain=attn_gain, query_weight=query_weight, latent_weight=latent_weight, latent_gain=latent_gain, expand_weight=expand_weight, output_weight=output_weight, ffn_gain=ffn_gain, router_weight=router_weight, shared_in=shared_in, shared_out=shared_out, expert_in=expert_in, expert_out=expert_out, cotangent=cotangent)


EPS = 1e-06
MASK_FILL = -1e+30
EXACT_PRECISION = lax.Precision.HIGHEST

@jax.custom_vjp
def low(v):
    return lax.optimization_barrier(v.astype(jnp.bfloat16)).astype(jnp.float32)

@jax.custom_vjp
def low_back(v):
    return v

def low_keep(v):
    return (low(v), None)

def low_pass(kept, grad):
    return (grad,)

def back_keep(v):
    return (v, None)

def back_low(kept, grad):
    return (low(grad),)
low.defvjp(low_keep, low_pass)
low_back.defvjp(back_keep, back_low)

def layout(lengths_slot):
    slot_index = jnp.arange(SLOT, dtype=jnp.int32)
    first_len = lengths_slot[0]
    second_end = first_len + lengths_slot[1]
    segment = (slot_index >= first_len).astype(jnp.int32) + (slot_index >= second_end).astype(jnp.int32)
    seq_start = jnp.where(segment == 0, 0, jnp.where(segment == 1, first_len, second_end))
    return (segment, slot_index - seq_start, slot_index < second_end)

def rope_tables(positions):
    half_width = ROPE // 2
    inverse = 10000.0 ** (-jnp.arange(half_width, dtype=jnp.float32) / half_width)
    angles = positions.astype(jnp.float32)[:, None] * inverse[None, :]
    return (jnp.cos(angles), jnp.sin(angles))

def rotate(values, cosine, sine_table):
    half_width = values.shape[-1] // 2
    first_half = values[..., :half_width]
    second_half = values[..., half_width:]
    return jnp.concatenate([first_half * cosine - second_half * sine_table, second_half * cosine + first_half * sine_table], -1)

def softmax_last(scores):
    shifted = jnp.exp(scores - lax.optimization_barrier(jnp.max(scores, -1, keepdims=True)))
    return shifted / lax.optimization_barrier(jnp.sum(shifted, -1, keepdims=True))

def rms_scale(values):
    return lax.rsqrt(lax.optimization_barrier(jnp.mean(values * values, -1, keepdims=True)) + EPS)

def silu_of(values):
    return values * jax.nn.sigmoid(values)

def attend(normed, lengths_slot, query_weight, latent_weight, latent_gain, expand_weight):
    segment, positions, valid_rows = layout(lengths_slot)
    cosine, sine_table = rope_tables(positions)
    query_raw = low_back(jnp.dot(normed, query_weight, precision=EXACT_PRECISION)).reshape(SLOT, HEADS, HEAD + ROPE)
    query_rot = rotate(query_raw[..., HEAD:], cosine[:, None, :], sine_table[:, None, :])
    queries = low(jnp.concatenate([query_raw[..., :HEAD], query_rot], -1))
    latent_raw = low_back(jnp.dot(normed, latent_weight, precision=EXACT_PRECISION))
    latent = latent_raw[:, :RANK]
    latent_norm = low(latent * rms_scale(latent) * latent_gain)
    key_rot = low(rotate(latent_raw[:, RANK:], cosine, sine_table))
    expanded = low(jnp.dot(latent_norm, expand_weight, precision=EXACT_PRECISION)).reshape(SLOT, HEADS, HEAD + VHEAD)
    keys = jnp.concatenate([expanded[..., :HEAD], jnp.broadcast_to(key_rot[:, None, :], (SLOT, HEADS, ROPE))], -1)
    score_scale = (HEAD + ROPE) ** (-0.5)
    scores = low_back(jnp.einsum('qhc,khc->hqk', queries, keys, precision=EXACT_PRECISION) * score_scale)
    slot_index = jnp.arange(SLOT, dtype=jnp.int32)
    allowed = (segment[:, None] == segment[None, :]) & (slot_index[None, :] <= slot_index[:, None])
    scores = jnp.where(allowed[None], scores, MASK_FILL)
    attention = softmax_last(scores)
    mixed_heads = jnp.einsum('hqk,khv->qhv', low(attention), expanded[..., HEAD:], precision=EXACT_PRECISION)
    return low(low_back(mixed_heads)).reshape(SLOT, HEADS * VHEAD)

def expert(ffn_in, expert_in_one, expert_out_one, token_rows):
    rows_in = ffn_in[token_rows]
    gate_up = low_back(jnp.einsum('rd,dgf->rgf', rows_in, expert_in_one, precision=EXACT_PRECISION))
    hidden_units = low(silu_of(gate_up[:, 0]) * gate_up[:, 1])
    return low(low_back(jnp.dot(hidden_units, expert_out_one, precision=EXACT_PRECISION)))

def reference(tokens, lengths, routes, attn_gain, query_weight, latent_weight, latent_gain, expand_weight, output_weight, ffn_gain, router_weight, shared_in, shared_out, expert_in, expert_out, cotangent):
    slot_count = tokens.shape[0]
    model_width = tokens.shape[2]
    total_rows = slot_count * SLOT
    most_rows = N_EXPERT * N_SHARD * CAP
    experts_all = router_weight.shape[1]
    route_flat = routes.reshape(-1)
    member = (route_flat[:, None] == jnp.arange(experts_all, dtype=jnp.int32)[None, :]).astype(jnp.int32)
    slot_rank = lax.optimization_barrier(jnp.sum((jnp.cumsum(member, 0) - 1) * member, -1))
    target_slot = route_flat * most_rows + slot_rank
    pair_at = jnp.zeros((experts_all * most_rows,), jnp.int32).at[target_slot].set(jnp.arange(route_flat.shape[0], dtype=jnp.int32))
    occupied = jnp.zeros((experts_all * most_rows,), jnp.float32).at[target_slot].set(1.0)
    token_at = pair_at // TOPK
    valid_rows = jax.vmap(layout)(lengths)[2]
    attend_block = jax.checkpoint(attend)
    expert_block = jax.checkpoint(expert)

    def forward(inputs, attn_gain, query_weight, latent_weight, latent_gain, expand_weight, output_weight, ffn_gain, router_weight, shared_in, shared_out, expert_in, expert_out):
        carry_zero = jnp.zeros((), jnp.float32)
        normed = low(inputs * rms_scale(inputs) * attn_gain)

        def attn_step(carried, pieces):
            return (carried, attend_block(pieces[0], pieces[1], query_weight, latent_weight, latent_gain, expand_weight))
        mixed_heads = lax.scan(attn_step, carry_zero, (normed, lengths))[1]
        hidden_state = inputs + low_back(jnp.einsum('stv,vd->std', mixed_heads, output_weight, precision=EXACT_PRECISION))
        flat_hidden = hidden_state.reshape(total_rows, model_width)
        ffn_in = low(flat_hidden * rms_scale(flat_hidden) * ffn_gain)
        logits = low_back(jnp.dot(ffn_in, router_weight, precision=EXACT_PRECISION))
        gate_weights = jnp.take_along_axis(softmax_last(logits), routes.reshape(total_rows, TOPK), -1)
        shared_both = low_back(jnp.dot(ffn_in, shared_in, precision=EXACT_PRECISION))
        shared_hidden = low(silu_of(shared_both[:, :FF_S]) * shared_both[:, FF_S:])
        shared_result = jnp.dot(shared_hidden, shared_out, precision=EXACT_PRECISION)

        def expert_step(carried, pieces):
            return (carried, expert_block(ffn_in, pieces[0], pieces[1], pieces[2]))
        expert_result = lax.scan(expert_step, carry_zero, (expert_in, expert_out, token_at.reshape(experts_all, most_rows)))[1]
        weight_at = gate_weights.reshape(-1)[pair_at] * occupied
        routed = jnp.zeros((total_rows, model_width), jnp.float32).at[token_at].add(expert_result.reshape(-1, model_width) * weight_at[:, None])
        return hidden_state + (shared_result + routed).reshape(slot_count, SLOT, model_width)
    params = (attn_gain, query_weight, latent_weight, latent_gain, expand_weight, output_weight, ffn_gain, router_weight, shared_in, shared_out, expert_in, expert_out)
    params_wide = tuple((piece.astype(jnp.float32) for piece in params))
    result, pullback = jax.vjp(forward, tokens.astype(jnp.float32), *params_wide)
    gradients = pullback(cotangent.astype(jnp.float32) * valid_rows[..., None].astype(jnp.float32))
    return (result.astype(jnp.bfloat16), gradients[0].astype(jnp.bfloat16), gradients[1], gradients[2], gradients[3], gradients[4], gradients[5], gradients[6], gradients[7], gradients[8], gradients[9], gradients[10], gradients[11], gradients[12])
```

```python
import functools

import jax
import jax.numpy as jnp
from jax import lax
from jax.experimental import pallas as pl
from jax.experimental.pallas import tpu as pltpu
from jax.sharding import PartitionSpec as P

HEADS = 16
HEAD = 128
ROPE = 64
VHEAD = 128
RANK = 512
FF_S = 2816
SLOT = 2048

EPS = 1e-06
MASK_FILL = -1e30
BF = jnp.bfloat16
F32 = jnp.float32


def layout(lengths_slot, slot_index):
    first_len = lengths_slot[0]
    second_end = first_len + lengths_slot[1]
    segment = (slot_index >= first_len).astype(jnp.int32) + (slot_index >= second_end).astype(
        jnp.int32
    )
    seq_start = jnp.where(segment == 0, 0, jnp.where(segment == 1, first_len, second_end))
    return (segment, slot_index - seq_start, slot_index < second_end)


def rope_tables(positions):
    half_width = ROPE // 2
    inverse = 10000.0 ** (-jnp.arange(half_width, dtype=F32) / half_width)
    angles = positions.astype(F32)[:, None] * inverse[None, :]
    return (jnp.cos(angles), jnp.sin(angles))


def rotate(values, cosine, sine_table):
    half_width = values.shape[-1] // 2
    first_half = values[..., :half_width]
    second_half = values[..., half_width:]
    return jnp.concatenate(
        [
            first_half * cosine - second_half * sine_table,
            second_half * cosine + first_half * sine_table,
        ],
        -1,
    )


def rotate_back(grads_in, cosine, sine_table):
    return rotate(grads_in, cosine, -sine_table)


def silu_parts(gate_in):
    sigma = jax.nn.sigmoid(gate_in)
    return (gate_in * sigma, sigma * (1.0 + gate_in * (1.0 - sigma)))


def rms_scale(values):
    return lax.rsqrt(jnp.mean(values * values, -1, keepdims=True) + EPS)


def norm_back(grad_in, normed, inverse):
    return inverse * (grad_in - normed * jnp.mean(grad_in * normed, -1, keepdims=True))


def dot(left, right):
    return jnp.dot(left, right, preferred_element_type=F32)


def dot_t(left, right):
    return lax.dot_general(left, right, (((1,), (1,)), ((), ())), preferred_element_type=F32)


def t_dot(left, right):
    return lax.dot_general(left, right, (((0,), (0,)), ((), ())), preferred_element_type=F32)


def cross(values, bit):
    count = lax.axis_size("expert")
    return lax.ppermute(values, "expert", [(i, i ^ bit) for i in range(count)])


def swap(values):
    return lax.ppermute(values, "shard", [(0, 1), (1, 0)])


def whole_rows(weight):
    if lax.axis_size("shard") != 2:
        return lax.all_gather(weight, "shard", axis=0, tiled=True)
    other = swap(weight)
    first = lax.axis_index("shard") == 0
    return jnp.where(
        first, jnp.concatenate([weight, other], 0), jnp.concatenate([other, weight], 0)
    )


def row_blocks(weight):
    count = lax.axis_size("shard")
    if count == 2:
        own = lax.axis_index("shard")
        return [(own, weight), (1 - own, swap(weight))]
    blocks = lax.all_gather(weight, "shard", axis=0)
    return [(j, blocks[j]) for j in range(count)]


def times(values, blocks):
    rows = blocks[0][1].shape[0]
    return sum(
        dot(lax.dynamic_slice_in_dim(values, place * rows, rows, 1), block)
        for place, block in blocks
    )


def times_back(grads, blocks):
    pieces = [dot_t(grads, block) for _, block in blocks]
    if len(pieces) != 2:
        return jnp.concatenate(pieces, 1)
    first = lax.axis_index("shard") == 0
    return jnp.where(first, jnp.concatenate(pieces, 1), jnp.concatenate(pieces[::-1], 1))


def group_rows(values):
    if lax.axis_size("shard") == 2:
        return jnp.concatenate([values, swap(values)], 0)
    return lax.all_gather(values, "shard", axis=0, tiled=True)


def collect(values, bits):
    places = [0]
    for bit in bits:
        values = jnp.concatenate([values, cross(values, bit)], 0)
        places = places + [place ^ bit for place in places]
    return values, places


def fold(pieces, bits, rows):
    count = rows << len(bits)
    for bit in bits:
        count = count // 2
        sent = sum(p[count:].astype(F32) for p in pieces).astype(BF)
        pieces = [p[:count] for p in pieces] + [cross(sent, bit)]
    return sum(p.astype(F32) for p in pieces)


def fold_order(bits):
    places = [0]
    for bit in reversed(bits):
        places = places + [place ^ bit for place in places]
    return places


def differing(blocks, bits):
    count = len(bits)
    here = lax.axis_index("expert")
    blocks = blocks.reshape((2,) * count + blocks.shape[1:])
    for k in range(count):
        odd = (here >> (count - 1 - k)) % 2 == 1
        blocks = jnp.where(odd, jnp.flip(blocks, k), blocks)
    axes = [count - bit.bit_length() for bit in bits]
    blocks = blocks.transpose(axes + list(range(count, blocks.ndim)))
    return blocks.reshape((1 << count,) + blocks.shape[count:])


def gradient_kernel(rows, order_ref, left_ref, right_ref, kept_ref, sent_ref, picked_ref):
    count = picked_ref.shape[0] // rows

    @pl.when(pl.program_id(0) == 0)
    def _():
        for j in range(count):
            start = pl.multiple_of(order_ref[j] * rows, rows)
            picked_ref[j * rows : (j + 1) * rows, :] = left_ref[pl.ds(start, rows), :]

    half = kept_ref.shape[0]
    right = right_ref[...]
    kept_ref[...] = dot(picked_ref[:half, :].astype(BF), right).astype(kept_ref.dtype)
    sent_ref[...] = dot(picked_ref[half:, :].astype(BF), right).astype(sent_ref.dtype)


def gradient_halves(left, right, bits):
    experts, shards = lax.axis_size("expert"), lax.axis_size("shard")
    tokens, rows_all = left.shape
    columns = right.shape[1]
    rows = rows_all // (experts * shards)
    blocks = (
        lax.axis_index("expert") ^ jnp.array(fold_order(bits), jnp.int32)
    ) * shards + lax.axis_index("shard")
    left = left.T
    half = rows * experts // 2
    if rows % 8:
        picked = lax.dynamic_index_in_dim(
            left.reshape(experts, shards, rows, tokens), lax.axis_index("shard"), 1, keepdims=False
        )
        picked = differing(picked, bits).reshape(-1, tokens)
        product = dot(picked, right).astype(BF)
        return product[:half], product[half:]
    if rows % 16:
        left = left.astype(F32)
    tile = next(t for t in (512, 384, 256, 128, columns) if columns % t == 0)
    return pl.pallas_call(
        functools.partial(gradient_kernel, rows),
        grid_spec=pltpu.PrefetchScalarGridSpec(
            num_scalar_prefetch=1,
            grid=(columns // tile,),
            in_specs=[
                pl.BlockSpec((rows_all, tokens), lambda i, order: (0, 0)),
                pl.BlockSpec((tokens, tile), lambda i, order: (0, i)),
            ],
            out_specs=[
                pl.BlockSpec((half, tile), lambda i, order: (0, i)),
                pl.BlockSpec((half, tile), lambda i, order: (0, i)),
            ],
            scratch_shapes=[pltpu.VMEM((rows * experts, tokens), left.dtype)],
        ),
        out_shape=[jax.ShapeDtypeStruct((half, columns), BF)] * 2,
        compiler_params=pltpu.CompilerParams(vmem_limit_bytes=40 << 20),
        cost_estimate=pl.CostEstimate(
            flops=4 * half * tokens * columns,
            bytes_accessed=4 * half * columns + 2 * tokens * (rows_all + columns),
            transcendentals=0,
        ),
    )(blocks, left, right)


def reduce_product(left, right, bits):
    kept, sent = gradient_halves(left, right, bits)
    rows = 2 * kept.shape[0] >> len(bits)
    arrived = cross(sent, bits[0])
    return fold([kept, arrived], bits[1:], rows)


def reduce_partial(partial, bits):
    experts, shards = lax.axis_size("expert"), lax.axis_size("shard")
    rows = partial.shape[0] // (experts * shards)
    if shards != 2:
        return lax.psum_scatter(partial, ("expert", "shard"), scatter_dimension=0, tiled=True)
    own = lax.axis_index("shard")
    blocks = partial.reshape(experts, 2, rows, partial.shape[1])
    kept = lax.dynamic_index_in_dim(blocks, own, 1, keepdims=False)
    sent = lax.dynamic_index_in_dim(blocks, 1 - own, 1, keepdims=False)
    total = (kept.astype(F32) + swap(sent).astype(F32)).astype(partial.dtype)
    return fold([differing(total, bits).reshape(experts * rows, -1)], bits, rows)


def per_device(
    tokens,
    lengths,
    routes,
    attn_gain,
    query_weight,
    latent_weight,
    latent_gain,
    expand_weight,
    output_weight,
    ffn_gain,
    router_weight,
    shared_in,
    shared_out,
    expert_in,
    expert_out,
    cotangent,
):
    local_rows = tokens.shape[1]
    model_width = tokens.shape[2]
    owners, shards = lax.axis_size("expert"), lax.axis_size("shard")
    experts_all = router_weight.shape[1]
    assert experts_all == owners
    topk_count = routes.shape[2]
    capacity = max(2, 9 * local_rows * topk_count // (8 * experts_all))
    capacity = -(-capacity // 8) * 8
    score_scale = (HEAD + ROPE) ** (-0.5)
    here = lax.axis_index("expert")
    bits = [1 << k for k in range(owners.bit_length() - 1)]
    first_x = tuple(bits)
    first_y = tuple(bits[1:2] + bits[:1] + bits[2:])

    query_blocks = row_blocks(query_weight)
    latent_blocks = row_blocks(latent_weight)
    gains = jnp.concatenate([attn_gain, ffn_gain, latent_gain])[None]
    gains = (
        jnp.where(
            lax.axis_index("shard") == 0,
            jnp.concatenate([gains, swap(gains)], 0),
            jnp.concatenate([swap(gains), gains], 0),
        )
        if shards == 2
        else lax.all_gather(gains, "shard", axis=0, tiled=True)
    ).astype(F32)
    cut = attn_gain.shape[0]
    gain_attn = gains[:, :cut].reshape(-1)
    gain_ffn = gains[:, cut : 2 * cut].reshape(-1)
    gain_latent = gains[:, 2 * cut :].reshape(-1)
    expand = whole_rows(expand_weight).reshape(RANK, HEADS, HEAD + VHEAD)
    expand_key, expand_value = expand[..., :HEAD], expand[..., HEAD:]
    output_blocks = row_blocks(output_weight)
    router = whole_rows(router_weight)
    shared_out_blocks = row_blocks(shared_out)
    shared_in_blocks = row_blocks(shared_in)
    expert_out_blocks = row_blocks(expert_out[0])
    gate_blocks = row_blocks(expert_in[0, :, 0, :])
    up_blocks = row_blocks(expert_in[0, :, 1, :])

    here_index = here * local_rows + jnp.arange(local_rows, dtype=jnp.int32)
    query_segment, query_position, query_valid = layout(lengths[0], here_index)
    cosine, sine_table = rope_tables(query_position)
    live_rows = query_valid.astype(F32)[:, None]
    grad_out = cotangent[0].astype(F32) * live_rows
    grad_out_low = grad_out.astype(BF)

    expert_ids = jnp.arange(experts_all, dtype=jnp.int32)
    member = jnp.any(routes[0][:, :, None] == expert_ids[None, None, :], 1)
    token_ids = jnp.arange(local_rows, dtype=jnp.int32)
    earlier = (token_ids[None, :] < token_ids[:, None]).astype(BF)
    rank = dot(earlier, member.astype(BF)).astype(jnp.int32)
    place_ids = jnp.arange(capacity, dtype=jnp.int32)
    spread = (
        member.T[:, None, :] & (rank.T[:, None, :] == place_ids[None, :, None])
    ).reshape(experts_all * capacity, local_rows).astype(BF)

    def exchange(rows):
        return lax.all_to_all(
            rows.reshape(owners, capacity, model_width),
            "expert",
            split_axis=0,
            concat_axis=0,
            tiled=True,
        ).reshape(owners * capacity, model_width)

    inputs = tokens[0].astype(F32)
    inverse_attn = rms_scale(inputs)
    normed_attn = inputs * inverse_attn
    attn_in = (normed_attn * gain_attn).astype(BF)
    latent_raw = times(attn_in, latent_blocks)
    latent = latent_raw[:, :RANK]
    inverse_latent = rms_scale(latent)
    normed_latent = latent * inverse_latent
    latent_in = (normed_latent * gain_latent).astype(BF)
    key_rope = rotate(latent_raw[:, RANK:], cosine, sine_table).astype(BF)
    own_keys = jnp.concatenate([latent_in, key_rope], -1)
    part = local_rows // 2
    collect_bits = (tuple(reversed(first_x)), tuple(reversed(first_y)))
    keys, key_index = [], []
    for k in range(2):
        gathered, places = collect(own_keys[k * part : (k + 1) * part], collect_bits[k])
        keys.append(gathered)
        key_index.append(
            (
                (here ^ jnp.array(places, jnp.int32))[:, None] * local_rows
                + k * part
                + jnp.arange(part, dtype=jnp.int32)[None, :]
            ).reshape(-1)
        )
    keys = jnp.concatenate(keys, 0)
    key_index = jnp.concatenate(key_index)

    received_grads = exchange(dot(spread, grad_out_low).astype(BF))

    query_raw = times(attn_in, query_blocks).reshape(local_rows, HEADS, HEAD + ROPE)
    query_nope = query_raw[..., :HEAD].astype(BF)
    query_rope = rotate(
        query_raw[..., HEAD:], cosine[:, None, :], sine_table[:, None, :]
    ).astype(BF)
    query_latent = jnp.einsum(
        "qhc,rhc->hqr", query_nope, expand_key, preferred_element_type=F32
    ).astype(BF)
    queries = jnp.concatenate([query_latent, query_rope.transpose(1, 0, 2)], -1).reshape(
        HEADS * local_rows, RANK + ROPE
    )
    key_segment = layout(lengths[0], key_index)[0]
    allowed = (query_segment[:, None] == key_segment[None, :]) & (
        key_index[None, :] <= here_index[:, None]
    )
    scores = dot_t(queries, keys).reshape(HEADS, local_rows, SLOT)
    scores = jnp.where(allowed[None], scores * score_scale, MASK_FILL)
    shifted = jnp.exp(scores - jnp.max(scores, -1, keepdims=True))
    attention = (shifted / jnp.sum(shifted, -1, keepdims=True)).reshape(HEADS * local_rows, SLOT)
    attention_low = attention.astype(BF)
    mixed_latent = dot(attention_low, keys[:, :RANK]).astype(BF).reshape(HEADS, local_rows, RANK)
    mixed_heads = (
        jnp.einsum("hqr,rhv->qhv", mixed_latent, expand_value, preferred_element_type=F32)
        .astype(BF)
        .reshape(local_rows, HEADS * VHEAD)
    )
    hidden_state = inputs + times(mixed_heads, output_blocks)
    inverse_ffn = rms_scale(hidden_state)
    normed_ffn = hidden_state * inverse_ffn
    ffn_in = (normed_ffn * gain_ffn).astype(BF)

    received = exchange(dot(spread, ffn_in).astype(BF))
    slopes_in = [dot_t(received_grads, block) for _, block in expert_out_blocks]
    row_logits = dot(received, router)
    row_exp = jnp.exp(row_logits - jnp.max(row_logits, -1, keepdims=True))
    row_probs = row_exp / jnp.sum(row_exp, -1, keepdims=True)
    own_expert = (expert_ids == here).astype(F32)[None, :]
    row_gate = jnp.sum(row_probs * own_expert, -1, keepdims=True)
    row_gate_grad = 0.0
    hidden, grads_gate, grads_up = [], [], []
    for j in range(shards):
        gate = dot(received, gate_blocks[j][1])
        up = dot(received, up_blocks[j][1])
        act, slope = silu_parts(gate)
        units = (act * up).astype(BF)
        row_gate_grad = row_gate_grad + jnp.sum(slopes_in[j] * units.astype(F32), -1, keepdims=True)
        grad_units = row_gate * slopes_in[j]
        hidden.append(units)
        grads_gate.append((grad_units * up * slope).astype(BF))
        grads_up.append((grad_units * act).astype(BF))
    row_grad_logits = (row_probs * (own_expert - row_gate) * row_gate_grad).astype(BF)
    row_grads = dot_t(row_grad_logits, router)
    for j in range(shards):
        row_grads = row_grads + dot_t(grads_gate[j], gate_blocks[j][1])
        row_grads = row_grads + dot_t(grads_up[j], up_blocks[j][1])
    returned_grads = exchange(row_grads.astype(BF))
    row_out = sum(dot(hidden[j], expert_out_blocks[j][1]) for j in range(shards))
    returned = exchange((row_gate * row_out).astype(BF))
    routed = t_dot(spread, returned)
    grad_routed = t_dot(spread, returned_grads)
    weighted_grads = (row_gate * received_grads.astype(F32)).astype(BF)
    grad_expert_parts = [
        (
            t_dot(received, grads_gate[j]),
            t_dot(received, grads_up[j]),
            t_dot(hidden[j], weighted_grads),
        )
        for j in range(shards)
    ]
    if shards == 2:
        own_parts, other_parts = grad_expert_parts
        own_parts = [
            own + swap(other.astype(BF)).astype(F32)
            for own, other in zip(own_parts, other_parts)
        ]
    else:
        own_parts = [
            lax.psum_scatter(
                jnp.stack([p[k].astype(BF) for p in grad_expert_parts]), "shard", tiled=True
            )[0].astype(F32)
            for k in range(3)
        ]
    grad_expert_in = jnp.stack(own_parts[:2], 1)[None]
    grad_expert_out = own_parts[2][None]
    grad_router = t_dot(received, row_grad_logits)

    shared_both = times(ffn_in, shared_in_blocks)
    shared_act, shared_slope = silu_parts(shared_both[:, :FF_S])
    shared_up = shared_both[:, FF_S:]
    shared_hidden = (shared_act * shared_up).astype(BF)
    shared_result = times(shared_hidden, shared_out_blocks)
    block_result = hidden_state + shared_result + routed
    grad_shared_hidden = times_back(grad_out_low, shared_out_blocks)
    grad_shared_gate = (grad_shared_hidden * shared_up * shared_slope).astype(BF)
    grad_shared_up = (grad_shared_hidden * shared_act).astype(BF)
    grad_shared_both = jnp.concatenate([grad_shared_gate, grad_shared_up], -1)
    group_ffn_in = group_rows(ffn_in)
    grad_shared_out = reduce_product(
        group_rows(shared_hidden), group_rows(grad_out_low), first_x
    )
    grad_shared_in = jnp.concatenate(
        [
            reduce_product(group_ffn_in, group_rows(grad_shared_gate), first_y),
            reduce_product(group_ffn_in, group_rows(grad_shared_up), first_x),
        ],
        -1,
    )
    grad_ffn_in = times_back(grad_shared_both, shared_in_blocks) + grad_routed
    grad_gain_ffn = jnp.sum(grad_ffn_in * normed_ffn, 0)
    grad_hidden_state = grad_out + norm_back(grad_ffn_in * gain_ffn, normed_ffn, inverse_ffn)

    grad_attn_out = grad_hidden_state.astype(BF)
    grad_output = reduce_product(group_rows(mixed_heads), group_rows(grad_attn_out), first_y)
    grad_mixed = times_back(grad_attn_out, output_blocks).astype(BF).reshape(
        local_rows, HEADS, VHEAD
    )
    grad_mixed_latent = (
        jnp.einsum("qhv,rhv->hqr", grad_mixed, expand_value, preferred_element_type=F32)
        .astype(BF)
        .reshape(HEADS * local_rows, RANK)
    )
    grad_attention = dot_t(grad_mixed_latent, keys[:, :RANK])
    grad_scores = (
        attention
        * (grad_attention - jnp.sum(attention * grad_attention, -1, keepdims=True))
        * score_scale
    ).astype(BF)
    grad_queries = dot(grad_scores, keys).reshape(HEADS, local_rows, RANK + ROPE)
    grad_query_latent = grad_queries[..., :RANK].astype(BF)
    grad_query_rope = grad_queries[..., RANK:].transpose(1, 0, 2)
    grad_keys = t_dot(grad_scores, queries)
    grad_keys = jnp.concatenate(
        [
            grad_keys[:, :RANK] + t_dot(attention_low, grad_mixed_latent),
            grad_keys[:, RANK:],
        ],
        -1,
    ).astype(BF)
    slot_half = SLOT // 2
    grad_own_keys = jnp.concatenate(
        [
            fold(
                [grad_keys[k * slot_half : (k + 1) * slot_half]],
                tuple(reversed(collect_bits[k])),
                part,
            )
            for k in range(2)
        ],
        0,
    )
    grad_expand = jnp.concatenate(
        [
            jnp.einsum("hqr,qhc->rhc", grad_query_latent, query_nope, preferred_element_type=F32),
            jnp.einsum("hqr,qhv->rhv", mixed_latent, grad_mixed, preferred_element_type=F32),
        ],
        -1,
    ).reshape(RANK, HEADS * (HEAD + VHEAD))
    grad_expand = reduce_partial(grad_expand.astype(BF), first_x).astype(F32)
    grad_latent_in = grad_own_keys[:, :RANK]
    grad_gain_latent = jnp.sum(grad_latent_in * normed_latent, 0)
    grad_latent = norm_back(grad_latent_in * gain_latent, normed_latent, inverse_latent)
    grad_latent_raw = jnp.concatenate(
        [grad_latent, rotate_back(grad_own_keys[:, RANK:], cosine, sine_table)], -1
    ).astype(BF)
    grad_query_nope = jnp.einsum(
        "hqr,rhc->qhc", grad_query_latent, expand_key, preferred_element_type=F32
    )
    grad_query_raw = (
        jnp.concatenate(
            [
                grad_query_nope,
                rotate_back(grad_query_rope, cosine[:, None, :], sine_table[:, None, :]),
            ],
            -1,
        )
        .reshape(local_rows, HEADS * (HEAD + ROPE))
        .astype(BF)
    )
    group_attn_in = group_rows(attn_in)
    group_grad_query = group_rows(grad_query_raw)
    query_half = group_grad_query.shape[1] // 2
    grad_query = jnp.concatenate(
        [
            reduce_product(group_attn_in, group_grad_query[:, :query_half], first_x),
            reduce_product(group_attn_in, group_grad_query[:, query_half:], first_y),
        ],
        -1,
    )
    grad_latent_weight = reduce_product(group_attn_in, group_rows(grad_latent_raw), first_y)
    grad_attn_in = times_back(grad_latent_raw, latent_blocks) + times_back(
        grad_query_raw, query_blocks
    )
    grad_gain_attn = jnp.sum(grad_attn_in * normed_attn, 0)
    tokens_grad = grad_hidden_state + norm_back(grad_attn_in * gain_attn, normed_attn, inverse_attn)

    devices = owners * shards
    rows = model_width // devices
    latent_column = jnp.pad(
        grad_gain_latent.reshape(devices, -1), ((0, 0), (0, rows - RANK // devices))
    ).reshape(-1, 1)
    small = jnp.concatenate(
        [grad_router, grad_gain_attn[:, None], grad_gain_ffn[:, None], latent_column], 1
    )
    small = reduce_partial(small, first_x).astype(F32)
    return (
        block_result.astype(BF)[None],
        tokens_grad.astype(BF)[None],
        small[:, experts_all],
        grad_query,
        grad_latent_weight,
        small[: RANK // devices, experts_all + 2],
        grad_expand,
        grad_output,
        small[:, experts_all + 1],
        small[:, :experts_all],
        grad_shared_in,
        grad_shared_out,
        grad_expert_in,
        grad_expert_out,
    )


def solution(mesh):
    return jax.shard_map(
        per_device,
        mesh=mesh,
        in_specs=(
            P("shard", "expert", None),
            P("shard", None),
            P("shard", "expert", None),
            P("shard"),
            P("shard", None),
            P("shard", None),
            P("shard"),
            P("shard", None),
            P("shard", None),
            P("shard"),
            P("shard", None),
            P("shard", None),
            P("shard", None),
            P("expert", None, None, "shard"),
            P("expert", "shard", None),
            P("shard", "expert", None),
        ),
        out_specs=(
            P("shard", "expert", None),
            P("shard", "expert", None),
            P(("expert", "shard")),
            P(("expert", "shard"), None),
            P(("expert", "shard"), None),
            P(("expert", "shard")),
            P(("expert", "shard"), None),
            P(("expert", "shard"), None),
            P(("expert", "shard")),
            P(("expert", "shard"), None),
            P(("expert", "shard"), None),
            P(("expert", "shard"), None),
            P("expert", None, None, "shard"),
            P("expert", "shard", None),
        ),
        check_vma=False,
    )
```

```python
import functools

import jax
import jax.numpy as jnp
from jax import lax
from jax.experimental import pallas as pl
from jax.experimental.pallas import tpu as pltpu
from jax.sharding import PartitionSpec as P

HEADS = 16
HEAD = 128
ROPE = 64
VHEAD = 128
RANK = 512
FF_S = 2816
SLOT = 2048

EPS = 1e-06
MASK_FILL = -1e30
BF = jnp.bfloat16
F32 = jnp.float32


def layout(lengths_slot, slot_index):
    first_len = lengths_slot[0]
    second_end = first_len + lengths_slot[1]
    segment = (slot_index >= first_len).astype(jnp.int32) + (slot_index >= second_end).astype(
        jnp.int32
    )
    seq_start = jnp.where(segment == 0, 0, jnp.where(segment == 1, first_len, second_end))
    return (segment, slot_index - seq_start, slot_index < second_end)


def rope_tables(positions):
    half_width = ROPE // 2
    inverse = 10000.0 ** (-jnp.arange(half_width, dtype=F32) / half_width)
    angles = positions.astype(F32)[:, None] * inverse[None, :]
    return (jnp.cos(angles), jnp.sin(angles))


def rotate(values, cosine, sine_table):
    half_width = values.shape[-1] // 2
    first_half = values[..., :half_width]
    second_half = values[..., half_width:]
    return jnp.concatenate(
        [
            first_half * cosine - second_half * sine_table,
            second_half * cosine + first_half * sine_table,
        ],
        -1,
    )


def rotate_back(grads_in, cosine, sine_table):
    return rotate(grads_in, cosine, -sine_table)


def silu_parts(gate_in):
    sigma = jax.nn.sigmoid(gate_in)
    return (gate_in * sigma, sigma * (1.0 + gate_in * (1.0 - sigma)))


def rms_scale(values):
    return lax.rsqrt(jnp.mean(values * values, -1, keepdims=True) + EPS)


def norm_back(grad_in, normed, inverse):
    return inverse * (grad_in - normed * jnp.mean(grad_in * normed, -1, keepdims=True))


def dot(left, right):
    return jnp.dot(left, right, preferred_element_type=F32)


def dot_t(left, right):
    return lax.dot_general(left, right, (((1,), (1,)), ((), ())), preferred_element_type=F32)


def t_dot(left, right):
    return lax.dot_general(left, right, (((0,), (0,)), ((), ())), preferred_element_type=F32)


def cross(values, bit):
    count = lax.axis_size("expert")
    return lax.ppermute(values, "expert", [(i, i ^ bit) for i in range(count)])


def swap(values):
    return lax.ppermute(values, "shard", [(0, 1), (1, 0)])


def whole_rows(weight):
    if lax.axis_size("shard") != 2:
        return lax.all_gather(weight, "shard", axis=0, tiled=True)
    other = swap(weight)
    first = lax.axis_index("shard") == 0
    return jnp.where(
        first, jnp.concatenate([weight, other], 0), jnp.concatenate([other, weight], 0)
    )


def row_blocks(weight):
    count = lax.axis_size("shard")
    if count == 2:
        own = lax.axis_index("shard")
        return [(own, weight), (1 - own, swap(weight))]
    blocks = lax.all_gather(weight, "shard", axis=0)
    return [(j, blocks[j]) for j in range(count)]


def times(values, blocks):
    rows = blocks[0][1].shape[0]
    return sum(
        dot(lax.dynamic_slice_in_dim(values, place * rows, rows, 1), block)
        for place, block in blocks
    )


def times_back(grads, blocks):
    pieces = [dot_t(grads, block) for _, block in blocks]
    if len(pieces) != 2:
        return jnp.concatenate(pieces, 1)
    first = lax.axis_index("shard") == 0
    return jnp.where(first, jnp.concatenate(pieces, 1), jnp.concatenate(pieces[::-1], 1))


def collect(values, bits):
    places = [0]
    for bit in bits:
        values = jnp.concatenate([values, cross(values, bit)], 0)
        places = places + [place ^ bit for place in places]
    return values, places


def fold(pieces, bits, rows):
    count = rows << len(bits)
    for bit in bits:
        count = count // 2
        sent = sum(p[count:].astype(F32) for p in pieces).astype(BF)
        pieces = [p[:count] for p in pieces] + [cross(sent, bit)]
    return sum(p.astype(F32) for p in pieces)


def fold_order(bits):
    places = [0]
    for bit in reversed(bits):
        places = places + [place ^ bit for place in places]
    return places


def differing(blocks, bits, here):
    count = len(bits)
    blocks = blocks.reshape((2,) * count + blocks.shape[1:])
    ranked = sorted(bits, reverse=True)
    for k, bit in enumerate(ranked):
        blocks = jnp.where(here // bit % 2 == 1, jnp.flip(blocks, k), blocks)
    axes = [ranked.index(bit) for bit in bits]
    blocks = blocks.transpose(axes + list(range(count, blocks.ndim)))
    return blocks.reshape((1 << count,) + blocks.shape[count:])


def gradient_kernel(rows, order_ref, left_ref, right_ref, kept_ref, sent_ref, picked_ref):
    count = picked_ref.shape[0] // rows

    @pl.when(pl.program_id(0) == 0)
    def _():
        for j in range(count):
            start = pl.multiple_of(order_ref[j] * rows, rows)
            picked_ref[j * rows : (j + 1) * rows, :] = left_ref[pl.ds(start, rows), :]

    half = kept_ref.shape[0]
    right = right_ref[...]
    kept_ref[...] = dot(picked_ref[:half, :].astype(BF), right).astype(kept_ref.dtype)
    sent_ref[...] = dot(picked_ref[half:, :].astype(BF), right).astype(sent_ref.dtype)


def gradient_halves(left, right, blocks, bits):
    count = 1 << len(bits)
    rows_all, tokens = left.shape
    columns = right.shape[1]
    rows = rows_all // count
    half = rows_all // 2
    if rows % 8:
        picked = differing(left.reshape(count, rows, tokens), bits, blocks).reshape(-1, tokens)
        product = dot(picked, right).astype(BF)
        return product[:half], product[half:]
    order = []
    for place in fold_order(bits):
        block = 0
        for k, bit in enumerate(sorted(bits)):
            flipped = (blocks >> bit.bit_length() - 1) & 1
            block = block + ((flipped ^ (place // bit & 1)) << k)
        order.append(block)
    if rows % 16:
        left = left.astype(F32)
    tile = next(t for t in (512, 384, 256, 128, columns) if columns % t == 0)
    return pl.pallas_call(
        functools.partial(gradient_kernel, rows),
        grid_spec=pltpu.PrefetchScalarGridSpec(
            num_scalar_prefetch=1,
            grid=(columns // tile,),
            in_specs=[
                pl.BlockSpec((rows_all, tokens), lambda i, order: (0, 0)),
                pl.BlockSpec((tokens, tile), lambda i, order: (0, i)),
            ],
            out_specs=[
                pl.BlockSpec((half, tile), lambda i, order: (0, i)),
                pl.BlockSpec((half, tile), lambda i, order: (0, i)),
            ],
            scratch_shapes=[pltpu.VMEM((rows_all, tokens), left.dtype)],
        ),
        out_shape=[jax.ShapeDtypeStruct((half, columns), BF)] * 2,
        compiler_params=pltpu.CompilerParams(vmem_limit_bytes=40 << 20),
        cost_estimate=pl.CostEstimate(
            flops=4 * half * tokens * columns,
            bytes_accessed=4 * half * columns + 2 * tokens * (rows_all + columns),
            transcendentals=0,
        ),
    )(jnp.stack(order).astype(jnp.int32), left, right)


def group_left(left, bit):
    experts, shards = lax.axis_size("expert"), lax.axis_size("shard")
    tokens, columns = left.shape
    own = lax.axis_index("expert") // bit % 2
    blocks = left.T.reshape(experts // (2 * bit), 2, bit, shards, -1, tokens)
    kept = lax.dynamic_index_in_dim(blocks, own, 1, keepdims=False)
    sent = lax.dynamic_index_in_dim(blocks, 1 - own, 1, keepdims=False)
    blocks = jnp.concatenate([kept, cross(sent, bit)], -1).reshape(
        experts // 2, shards, -1, 2 * tokens
    )
    if shards != 2:
        blocks = lax.all_to_all(blocks, "shard", split_axis=1, concat_axis=3, tiled=True)
        return blocks.reshape(columns // (2 * shards), -1)
    own = lax.axis_index("shard")
    kept = lax.dynamic_index_in_dim(blocks, own, 1, keepdims=False)
    sent = lax.dynamic_index_in_dim(blocks, 1 - own, 1, keepdims=False)
    return jnp.concatenate([kept, swap(sent)], -1).reshape(columns // 4, -1)


def group_right(right, bit):
    right = jnp.concatenate([right, cross(right, bit)], 0)
    if lax.axis_size("shard") != 2:
        return lax.all_gather(right, "shard", axis=0, tiled=True)
    return jnp.concatenate([right, swap(right)], 0)


def reduce_product(left, right, bits):
    kept, sent = gradient_halves(left, right, lax.axis_index("expert"), bits[1:])
    rows = 2 * kept.shape[0] >> len(bits) - 1
    arrived = cross(sent, bits[1])
    return fold([kept, arrived], bits[2:], rows)


def reduce_partial(partial, bits):
    experts, shards = lax.axis_size("expert"), lax.axis_size("shard")
    rows = partial.shape[0] // (experts * shards)
    if shards != 2:
        return lax.psum_scatter(partial, ("expert", "shard"), scatter_dimension=0, tiled=True)
    own = lax.axis_index("shard")
    blocks = partial.reshape(experts, 2, rows, partial.shape[1])
    kept = lax.dynamic_index_in_dim(blocks, own, 1, keepdims=False)
    sent = lax.dynamic_index_in_dim(blocks, 1 - own, 1, keepdims=False)
    total = (kept.astype(F32) + swap(sent).astype(F32)).astype(partial.dtype)
    return fold([differing(total, bits, lax.axis_index("expert")).reshape(experts * rows, -1)], bits, rows)


def attend_kernel(
    raw_ref, cosine_ref, sine_ref, expand_ref, keys_ref, bias_ref,
    nope_ref, queries_ref, weights_ref, mixed_ref, out_ref,
):
    rows = raw_ref.shape[0]
    width = HEAD + ROPE
    cosine, sine = cosine_ref[...], sine_ref[...]
    for h in range(2):
        raw = raw_ref[:, h * width : (h + 1) * width]
        nope = raw[:, :HEAD].astype(BF)
        first = raw[:, HEAD : HEAD + ROPE // 2]
        second = raw[:, HEAD + ROPE // 2 :]
        turned = jnp.concatenate(
            [first * cosine - second * sine, second * cosine + first * sine], -1
        )
        nope_ref[:, h * HEAD : (h + 1) * HEAD] = nope
        latent = dot_t(nope, expand_ref[:, 2 * h * HEAD : (2 * h + 1) * HEAD])
        queries_ref[h * rows : (h + 1) * rows, :RANK] = latent.astype(BF)
        queries_ref[h * rows : (h + 1) * rows, RANK:] = turned.astype(BF)
    bias = bias_ref[...]
    for h in range(2):
        part = slice(h * rows, (h + 1) * rows)
        scores = dot_t(queries_ref[part, :], keys_ref[...]) * (HEAD + ROPE) ** -0.5 + bias
        shifted = jnp.exp(scores - jnp.max(scores, -1, keepdims=True))
        total = jnp.sum(shifted, -1, keepdims=True)
        weights_ref[part, :] = (shifted * (1.0 / total)).astype(BF)
    mixed_ref[...] = dot(weights_ref[...], keys_ref[:, :RANK]).astype(BF)
    for h in range(2):
        out_ref[:, h * VHEAD : (h + 1) * VHEAD] = dot(
            mixed_ref[h * rows : (h + 1) * rows, :],
            expand_ref[:, (2 * h + 1) * HEAD : (2 * h + 2) * HEAD],
        ).astype(BF)


def attend(query_raw, cosine, sine, expand, keys, bias):
    rows, slot = bias.shape
    steps = HEADS // 2
    whole = lambda *shape: pl.BlockSpec(shape, lambda i: (0,) * len(shape))
    return pl.pallas_call(
        attend_kernel,
        grid=(steps,),
        in_specs=[
            pl.BlockSpec((rows, 2 * (HEAD + ROPE)), lambda i: (0, i)),
            whole(rows, ROPE // 2),
            whole(rows, ROPE // 2),
            pl.BlockSpec((RANK, 4 * HEAD), lambda i: (0, i)),
            whole(slot, RANK + ROPE),
            whole(rows, slot),
        ],
        out_specs=[
            pl.BlockSpec((rows, 2 * HEAD), lambda i: (0, i)),
            pl.BlockSpec((2 * rows, RANK + ROPE), lambda i: (i, 0)),
            pl.BlockSpec((2 * rows, slot), lambda i: (i, 0)),
            pl.BlockSpec((2 * rows, RANK), lambda i: (i, 0)),
            pl.BlockSpec((rows, 2 * VHEAD), lambda i: (0, i)),
        ],
        out_shape=[
            jax.ShapeDtypeStruct((rows, HEADS * HEAD), BF),
            jax.ShapeDtypeStruct((HEADS * rows, RANK + ROPE), BF),
            jax.ShapeDtypeStruct((HEADS * rows, slot), BF),
            jax.ShapeDtypeStruct((HEADS * rows, RANK), BF),
            jax.ShapeDtypeStruct((rows, HEADS * VHEAD), BF),
        ],
        compiler_params=pltpu.CompilerParams(vmem_limit_bytes=40 << 20),
        cost_estimate=pl.CostEstimate(
            flops=2 * HEADS * rows * slot * (2 * RANK + ROPE),
            bytes_accessed=2 * HEADS * rows * slot,
            transcendentals=HEADS * rows * slot,
        ),
    )(query_raw, cosine, sine, expand, keys, bias)


def attend_back_kernel(
    grad_ref, expand_ref, keys_ref, weights_ref, queries_ref, mixed_ref, nope_ref, cosine_ref,
    sine_ref, query_grad_ref, expand_grad_ref, key_grad_ref, latent_ref, scores_ref,
):
    rows = grad_ref.shape[0]
    width = HEAD + ROPE
    scale = (HEAD + ROPE) ** -0.5

    @pl.when(pl.program_id(0) == 0)
    def _():
        key_grad_ref[...] = jnp.zeros_like(key_grad_ref)

    for h in range(2):
        part = slice(h * rows, (h + 1) * rows)
        grad = grad_ref[:, h * VHEAD : (h + 1) * VHEAD]
        latent_ref[part, :] = dot_t(
            grad, expand_ref[:, (2 * h + 1) * HEAD : (2 * h + 2) * HEAD]
        ).astype(BF)
        arrived = dot_t(latent_ref[part, :], keys_ref[:, :RANK])
        weights = weights_ref[part, :].astype(F32)
        mean = jnp.sum(weights * arrived, -1, keepdims=True)
        scores_ref[part, :] = (weights * (arrived - mean) * scale).astype(BF)
    key_grad_ref[...] += t_dot(queries_ref[...], scores_ref[...])
    key_grad_ref[:RANK, :] += t_dot(latent_ref[...], weights_ref[...])
    cosine, sine = cosine_ref[...], sine_ref[...]
    for h in range(2):
        part = slice(h * rows, (h + 1) * rows)
        query_grad = dot(scores_ref[part, :], keys_ref[...])
        latent = query_grad[:, :RANK].astype(BF)
        key_part = slice(2 * h * HEAD, (2 * h + 1) * HEAD)
        value_part = slice((2 * h + 1) * HEAD, (2 * h + 2) * HEAD)
        nope = dot(latent, expand_ref[:, key_part])
        first = query_grad[:, RANK : RANK + ROPE // 2]
        second = query_grad[:, RANK + ROPE // 2 :]
        query_grad_ref[:, h * width : (h + 1) * width] = jnp.concatenate(
            [nope, first * cosine + second * sine, second * cosine - first * sine], -1
        ).astype(BF)
        expand_grad_ref[:, key_part] = t_dot(
            latent, nope_ref[:, h * HEAD : (h + 1) * HEAD]
        ).astype(BF)
        expand_grad_ref[:, value_part] = t_dot(
            mixed_ref[part, :], grad_ref[:, h * VHEAD : (h + 1) * VHEAD]
        ).astype(BF)


def attend_back(grad_out, expand, keys, weights, queries, mixed, nope, cosine, sine):
    rows = grad_out.shape[0]
    slot = keys.shape[0]
    whole = lambda *shape: pl.BlockSpec(shape, lambda i: (0,) * len(shape))
    return pl.pallas_call(
        attend_back_kernel,
        grid=(HEADS // 2,),
        in_specs=[
            pl.BlockSpec((rows, 2 * VHEAD), lambda i: (0, i)),
            pl.BlockSpec((RANK, 4 * HEAD), lambda i: (0, i)),
            whole(slot, RANK + ROPE),
            pl.BlockSpec((2 * rows, slot), lambda i: (i, 0)),
            pl.BlockSpec((2 * rows, RANK + ROPE), lambda i: (i, 0)),
            pl.BlockSpec((2 * rows, RANK), lambda i: (i, 0)),
            pl.BlockSpec((rows, 2 * HEAD), lambda i: (0, i)),
            whole(rows, ROPE // 2),
            whole(rows, ROPE // 2),
        ],
        out_specs=[
            pl.BlockSpec((rows, 2 * (HEAD + ROPE)), lambda i: (0, i)),
            pl.BlockSpec((RANK, 4 * HEAD), lambda i: (0, i)),
            whole(RANK + ROPE, slot),
        ],
        out_shape=[
            jax.ShapeDtypeStruct((rows, HEADS * (HEAD + ROPE)), BF),
            jax.ShapeDtypeStruct((RANK, 2 * HEADS * HEAD), BF),
            jax.ShapeDtypeStruct((RANK + ROPE, slot), F32),
        ],
        scratch_shapes=[pltpu.VMEM((2 * rows, RANK), BF), pltpu.VMEM((2 * rows, slot), BF)],
        compiler_params=pltpu.CompilerParams(vmem_limit_bytes=48 << 20),
        cost_estimate=pl.CostEstimate(
            flops=2 * HEADS * rows * slot * (3 * RANK + 2 * (RANK + ROPE)),
            bytes_accessed=2 * HEADS * rows * slot,
            transcendentals=0,
        ),
    )(grad_out, expand, keys, weights, queries, mixed, nope, cosine, sine)


def expert_kernel(sources, here_ref, rows_ref, grads_ref, router_ref, *refs):
    weights = refs[: 2 * sources]
    (
        row_grad_ref, units_ref, back_ref, gate_ref, logit_grad_ref, total_ref, probs_ref, share_ref,
    ) = refs[2 * sources :]
    step = pl.program_id(0)
    chunks = pl.num_programs(0) // sources

    @pl.when(step == 0)
    def _():
        logits = dot_t(router_ref[...], rows_ref[...])
        powers = jnp.exp(logits - jnp.max(logits, 0, keepdims=True))
        probs = powers / jnp.sum(powers, 0, keepdims=True)
        own = lax.broadcasted_iota(jnp.int32, probs.shape, 0) == here_ref[0]
        probs_ref[...] = probs
        gate_ref[...] = jnp.sum(jnp.where(own, probs, 0.0), 0, keepdims=True)
        share_ref[...] = jnp.zeros_like(share_ref)
        total_ref[...] = jnp.zeros_like(total_ref)

    def work(in_ref, out_ref):
        gate = dot_t(in_ref[0], rows_ref[...])
        up = dot_t(in_ref[1], rows_ref[...])
        back = dot_t(out_ref[...], grads_ref[...])
        sigma = 1.0 / (1.0 + jnp.exp(-gate))
        act = gate * sigma
        units = (act * up).astype(BF)
        units_ref[...] = units
        share_ref[...] += jnp.sum(back * units.astype(F32), 0, keepdims=True)
        back = back * gate_ref[...]
        back_ref[0] = (back * up * (sigma * (1.0 + gate * (1.0 - sigma)))).astype(BF)
        back_ref[1] = (back * act).astype(BF)
        total_ref[...] += t_dot(back_ref[0], in_ref[0])
        total_ref[...] += t_dot(back_ref[1], in_ref[1])

    for k in range(sources):

        @pl.when(step // chunks == k)
        def _(k=k):
            work(weights[2 * k], weights[2 * k + 1])

    @pl.when(step == pl.num_programs(0) - 1)
    def _():
        probs = probs_ref[...]
        own = lax.broadcasted_iota(jnp.int32, probs.shape, 0) == here_ref[0]
        grad = probs * (own.astype(F32) - gate_ref[...]) * share_ref[...]
        logit_grad_ref[...] = grad.astype(BF)
        row_grad_ref[...] = (
            total_ref[...] + t_dot(logit_grad_ref[...], router_ref[...])
        ).astype(BF)


def expert_pass(here, rows, grads, router, weights):
    count, width = rows.shape
    experts = router.shape[0]
    sources = len(weights)
    units = weights[0][1].shape[0]
    tile = next(t for t in (352, 176, 88, 64, 32, 16, units) if units % t == 0)
    chunks = units // tile
    once = pl.Buffered(1)
    in_specs = [
        pl.BlockSpec((count, width), lambda i, h: (0, 0), pipeline_mode=once),
        pl.BlockSpec((count, width), lambda i, h: (0, 0), pipeline_mode=once),
        pl.BlockSpec((experts, width), lambda i, h: (0, 0)),
    ]
    for k in range(sources):
        at = lambda i, k=k: jnp.clip(i - k * chunks, 0, chunks - 1)
        in_specs.append(pl.BlockSpec((2, tile, width), lambda i, h, at=at: (0, at(i), 0)))
        in_specs.append(pl.BlockSpec((tile, width), lambda i, h, at=at: (at(i), 0)))
    return pl.pallas_call(
        functools.partial(expert_kernel, sources),
        grid_spec=pltpu.PrefetchScalarGridSpec(
            num_scalar_prefetch=1,
            grid=(sources * chunks,),
            in_specs=in_specs,
            out_specs=[
                pl.BlockSpec((count, width), lambda i, h: (0, 0), pipeline_mode=once),
                pl.BlockSpec((tile, count), lambda i, h: (i, 0)),
                pl.BlockSpec(
                    (None, 2, tile, count), lambda i, h: (i // chunks, 0, i % chunks, 0)
                ),
                pl.BlockSpec((1, count), lambda i, h: (0, 0)),
                pl.BlockSpec((experts, count), lambda i, h: (0, 0)),
            ],
            scratch_shapes=[
                pltpu.VMEM((count, width), F32),
                pltpu.VMEM((experts, count), F32),
                pltpu.VMEM((1, count), F32),
            ],
        ),
        out_shape=[
            jax.ShapeDtypeStruct((count, width), BF),
            jax.ShapeDtypeStruct((sources * units, count), BF),
            jax.ShapeDtypeStruct((sources, 2, units, count), BF),
            jax.ShapeDtypeStruct((1, count), F32),
            jax.ShapeDtypeStruct((experts, count), BF),
        ],
        compiler_params=pltpu.CompilerParams(vmem_limit_bytes=58 << 20),
        cost_estimate=pl.CostEstimate(
            flops=10 * count * width * sources * units,
            bytes_accessed=6 * (count + sources * units) * width,
            transcendentals=count * sources * units,
        ),
    )(here, rows, grads, router, *[piece for pair in weights for piece in pair])


def per_device(
    tokens,
    lengths,
    routes,
    attn_gain,
    query_weight,
    latent_weight,
    latent_gain,
    expand_weight,
    output_weight,
    ffn_gain,
    router_weight,
    shared_in,
    shared_out,
    expert_in,
    expert_out,
    cotangent,
):
    local_rows = tokens.shape[1]
    model_width = tokens.shape[2]
    owners, shards = lax.axis_size("expert"), lax.axis_size("shard")
    experts_all = router_weight.shape[1]
    assert experts_all == owners
    topk_count = routes.shape[2]
    capacity = max(2, 9 * local_rows * topk_count // (8 * experts_all))
    capacity = -(-capacity // 8) * 8
    here = lax.axis_index("expert")
    bits = [1 << k for k in range(owners.bit_length() - 1)]
    first_x = tuple(bits)
    first_y = tuple(bits[1:2] + bits[:1] + bits[2:])

    query_blocks = row_blocks(query_weight)
    latent_blocks = row_blocks(latent_weight)
    gains = jnp.concatenate([attn_gain, ffn_gain, latent_gain])[None]
    gains = (
        jnp.where(
            lax.axis_index("shard") == 0,
            jnp.concatenate([gains, swap(gains)], 0),
            jnp.concatenate([swap(gains), gains], 0),
        )
        if shards == 2
        else lax.all_gather(gains, "shard", axis=0, tiled=True)
    ).astype(F32)
    cut = attn_gain.shape[0]
    gain_attn = gains[:, :cut].reshape(-1)
    gain_ffn = gains[:, cut : 2 * cut].reshape(-1)
    gain_latent = gains[:, 2 * cut :].reshape(-1)
    expand = whole_rows(expand_weight)
    output_blocks = row_blocks(output_weight)
    router = whole_rows(router_weight)
    shared_out_blocks = row_blocks(shared_out)
    shared_in_blocks = row_blocks(shared_in)
    expert_in_rows = expert_in[0].transpose(1, 2, 0)
    if shards == 2:
        expert_weights = [
            (expert_in_rows, expert_out[0]),
            (swap(expert_in_rows), swap(expert_out[0])),
        ]
    else:
        expert_weights = [
            (
                lax.all_gather(expert_in_rows, "shard", axis=1, tiled=True),
                lax.all_gather(expert_out[0], "shard", axis=0, tiled=True),
            )
        ]

    here_index = here * local_rows + jnp.arange(local_rows, dtype=jnp.int32)
    query_segment, query_position, query_valid = layout(lengths[0], here_index)
    cosine, sine_table = rope_tables(query_position)
    live_rows = query_valid.astype(F32)[:, None]
    grad_out = cotangent[0].astype(F32) * live_rows
    grad_out_low = grad_out.astype(BF)

    expert_ids = jnp.arange(experts_all, dtype=jnp.int32)
    member = jnp.any(routes[0][:, :, None] == expert_ids[None, None, :], 1)
    token_ids = jnp.arange(local_rows, dtype=jnp.int32)
    earlier = (token_ids[None, :] < token_ids[:, None]).astype(BF)
    rank = dot(earlier, member.astype(BF)).astype(jnp.int32)
    place_ids = jnp.arange(capacity, dtype=jnp.int32)
    spread = (
        member.T[:, None, :] & (rank.T[:, None, :] == place_ids[None, :, None])
    ).reshape(experts_all * capacity, local_rows).astype(BF)

    def exchange(rows):
        return lax.all_to_all(
            rows.reshape(owners, capacity, model_width),
            "expert",
            split_axis=0,
            concat_axis=0,
            tiled=True,
        ).reshape(owners * capacity, model_width)

    inputs = tokens[0].astype(F32)
    inverse_attn = rms_scale(inputs)
    normed_attn = inputs * inverse_attn
    attn_in = (normed_attn * gain_attn).astype(BF)
    latent_raw = times(attn_in, latent_blocks)
    latent = latent_raw[:, :RANK]
    inverse_latent = rms_scale(latent)
    normed_latent = latent * inverse_latent
    latent_in = (normed_latent * gain_latent).astype(BF)
    key_rope = rotate(latent_raw[:, RANK:], cosine, sine_table).astype(BF)
    own_keys = jnp.concatenate([latent_in, key_rope], -1)
    part = local_rows // 2
    collect_bits = (tuple(reversed(first_x)), tuple(reversed(first_y)))
    keys, key_index = [], []
    for k in range(2):
        gathered, places = collect(own_keys[k * part : (k + 1) * part], collect_bits[k])
        keys.append(gathered)
        key_index.append(
            (
                (here ^ jnp.array(places, jnp.int32))[:, None] * local_rows
                + k * part
                + jnp.arange(part, dtype=jnp.int32)[None, :]
            ).reshape(-1)
        )
    keys = jnp.concatenate(keys, 0)
    key_index = jnp.concatenate(key_index)

    sent_grads, keys = lax.optimization_barrier((dot(spread, grad_out_low).astype(BF), keys))
    received_grads = exchange(sent_grads)

    query_raw = times(attn_in, query_blocks)
    key_segment = layout(lengths[0], key_index)[0]
    allowed = (query_segment[:, None] == key_segment[None, :]) & (
        key_index[None, :] <= here_index[:, None]
    )
    bias = jnp.where(allowed, 0.0, MASK_FILL).astype(F32)
    query_nope, queries, attention, mixed_latent, mixed_heads = attend(
        query_raw, cosine, sine_table, expand, keys, bias
    )
    mixed_heads, received_grads = lax.optimization_barrier((mixed_heads, received_grads))
    hidden_state = inputs + times(mixed_heads, output_blocks)
    inverse_ffn = rms_scale(hidden_state)
    normed_ffn = hidden_state * inverse_ffn
    ffn_in = (normed_ffn * gain_ffn).astype(BF)

    received = exchange(dot(spread, ffn_in).astype(BF))
    row_grads, hidden, hidden_grads, row_gate, row_grad_logits = expert_pass(
        here[None], received, received_grads, router.T, expert_weights
    )
    returned_grads = exchange(row_grads)
    row_gate = row_gate.reshape(-1, 1)
    row_out = 0.0
    units = expert_weights[0][1].shape[0]
    for j, (_, weight) in enumerate(expert_weights):
        row_out = row_out + t_dot(hidden[j * units : (j + 1) * units], weight)
    returned = exchange((row_gate * row_out).astype(BF))
    routed = t_dot(spread, returned)
    grad_routed = t_dot(spread, returned_grads)
    weighted_grads = (row_gate * received_grads.astype(F32)).astype(BF)
    grad_expert_parts = [
        (
            dot(hidden_grads[j].reshape(2 * units, -1), received).reshape(2, units, -1),
            dot(hidden[j * units : (j + 1) * units], weighted_grads),
        )
        for j in range(len(expert_weights))
    ]
    if shards == 2:
        grad_expert_in, grad_expert_out = [
            own + swap(other.astype(BF)).astype(F32) for own, other in zip(*grad_expert_parts)
        ]
    else:
        grad_expert_in, grad_expert_out = [
            lax.psum_scatter(
                part.astype(BF), "shard", scatter_dimension=part.ndim - 2, tiled=True
            ).astype(F32)
            for part in grad_expert_parts[0]
        ]
    grad_expert_in = grad_expert_in.transpose(2, 0, 1)[None]
    grad_expert_out = grad_expert_out[None]
    grad_router = dot(row_grad_logits, received).T

    shared_both = times(ffn_in, shared_in_blocks)
    shared_act, shared_slope = silu_parts(shared_both[:, :FF_S])
    shared_up = shared_both[:, FF_S:]
    shared_hidden = (shared_act * shared_up).astype(BF)
    shared_result = times(shared_hidden, shared_out_blocks)
    block_result = hidden_state + shared_result + routed
    grad_shared_hidden = times_back(grad_out_low, shared_out_blocks)
    grad_shared_gate = (grad_shared_hidden * shared_up * shared_slope).astype(BF)
    grad_shared_up = (grad_shared_hidden * shared_act).astype(BF)
    grad_shared_both = jnp.concatenate([grad_shared_gate, grad_shared_up], -1)
    grad_shared_out = reduce_product(
        group_left(shared_hidden, first_x[0]), group_right(grad_out_low, first_x[0]), first_x
    )
    grad_shared_in = jnp.concatenate(
        [
            reduce_product(
                group_left(ffn_in, order[0]), group_right(grads_in, order[0]), order
            )
            for order, grads_in in ((first_y, grad_shared_gate), (first_x, grad_shared_up))
        ],
        -1,
    )
    grad_ffn_in = times_back(grad_shared_both, shared_in_blocks) + grad_routed
    grad_gain_ffn = jnp.sum(grad_ffn_in * normed_ffn, 0)
    grad_hidden_state = grad_out + norm_back(grad_ffn_in * gain_ffn, normed_ffn, inverse_ffn)

    grad_attn_out = grad_hidden_state.astype(BF)
    grad_output = reduce_product(
        group_left(mixed_heads, first_y[0]), group_right(grad_attn_out, first_y[0]), first_y
    )
    grad_mixed = times_back(grad_attn_out, output_blocks).astype(BF)
    grad_query_raw, grad_expand, grad_keys = attend_back(
        grad_mixed,
        expand,
        keys,
        attention,
        queries,
        mixed_latent,
        query_nope,
        cosine,
        sine_table,
    )
    grad_keys = grad_keys.T.astype(BF)
    slot_half = SLOT // 2
    grad_own_keys = jnp.concatenate(
        [
            fold(
                [grad_keys[k * slot_half : (k + 1) * slot_half]],
                tuple(reversed(collect_bits[k])),
                part,
            )
            for k in range(2)
        ],
        0,
    )
    grad_expand = reduce_partial(grad_expand, first_x).astype(F32)
    grad_latent_in = grad_own_keys[:, :RANK]
    grad_gain_latent = jnp.sum(grad_latent_in * normed_latent, 0)
    grad_latent = norm_back(grad_latent_in * gain_latent, normed_latent, inverse_latent)
    grad_latent_raw = jnp.concatenate(
        [grad_latent, rotate_back(grad_own_keys[:, RANK:], cosine, sine_table)], -1
    ).astype(BF)
    left_x, left_y = group_left(attn_in, first_x[0]), group_left(attn_in, first_y[0])
    query_half = grad_query_raw.shape[1] // 2
    grad_query = jnp.concatenate(
        [
            reduce_product(
                left_x, group_right(grad_query_raw[:, :query_half], first_x[0]), first_x
            ),
            reduce_product(
                left_y, group_right(grad_query_raw[:, query_half:], first_y[0]), first_y
            ),
        ],
        -1,
    )
    grad_latent_weight = reduce_product(
        left_y, group_right(grad_latent_raw, first_y[0]), first_y
    )
    grad_attn_in = times_back(grad_latent_raw, latent_blocks) + times_back(
        grad_query_raw, query_blocks
    )
    grad_gain_attn = jnp.sum(grad_attn_in * normed_attn, 0)
    tokens_grad = grad_hidden_state + norm_back(grad_attn_in * gain_attn, normed_attn, inverse_attn)

    devices = owners * shards
    rows = model_width // devices
    latent_column = jnp.pad(
        grad_gain_latent.reshape(devices, -1), ((0, 0), (0, rows - RANK // devices))
    ).reshape(-1, 1)
    small = jnp.concatenate(
        [grad_router, grad_gain_attn[:, None], grad_gain_ffn[:, None], latent_column], 1
    )
    small = reduce_partial(small, first_x).astype(F32)
    return (
        block_result.astype(BF)[None],
        tokens_grad.astype(BF)[None],
        small[:, experts_all],
        grad_query,
        grad_latent_weight,
        small[: RANK // devices, experts_all + 2],
        grad_expand,
        grad_output,
        small[:, experts_all + 1],
        small[:, :experts_all],
        grad_shared_in,
        grad_shared_out,
        grad_expert_in,
        grad_expert_out,
    )


def solution(mesh):
    return jax.shard_map(
        per_device,
        mesh=mesh,
        in_specs=(
            P("shard", "expert", None),
            P("shard", None),
            P("shard", "expert", None),
            P("shard"),
            P("shard", None),
            P("shard", None),
            P("shard"),
            P("shard", None),
            P("shard", None),
            P("shard"),
            P("shard", None),
            P("shard", None),
            P("shard", None),
            P("expert", None, None, "shard"),
            P("expert", "shard", None),
            P("shard", "expert", None),
        ),
        out_specs=(
            P("shard", "expert", None),
            P("shard", "expert", None),
            P(("expert", "shard")),
            P(("expert", "shard"), None),
            P(("expert", "shard"), None),
            P(("expert", "shard")),
            P(("expert", "shard"), None),
            P(("expert", "shard"), None),
            P(("expert", "shard")),
            P(("expert", "shard"), None),
            P(("expert", "shard"), None),
            P(("expert", "shard"), None),
            P("expert", None, None, "shard"),
            P("expert", "shard", None),
        ),
        check_vma=False,
    )
```

```python
import functools

import jax
import jax.numpy as jnp
from jax import lax
from jax.experimental import pallas as pl
from jax.experimental.pallas import tpu as pltpu
from jax.sharding import PartitionSpec as P

HEADS = 16
HEAD = 128
ROPE = 64
VHEAD = 128
RANK = 512
FF_S = 2816
SLOT = 2048

EPS = 1e-06
MASK_FILL = -1e30
BF = jnp.bfloat16
F32 = jnp.float32


def layout(lengths_slot, slot_index):
    first_len = lengths_slot[0]
    second_end = first_len + lengths_slot[1]
    segment = (slot_index >= first_len).astype(jnp.int32) + (slot_index >= second_end).astype(
        jnp.int32
    )
    seq_start = jnp.where(segment == 0, 0, jnp.where(segment == 1, first_len, second_end))
    return (segment, slot_index - seq_start, slot_index < second_end)


def rope_tables(positions):
    half_width = ROPE // 2
    inverse = 10000.0 ** (-jnp.arange(half_width, dtype=F32) / half_width)
    angles = positions.astype(F32)[:, None] * inverse[None, :]
    return (jnp.cos(angles), jnp.sin(angles))


def rotate(values, cosine, sine_table):
    half_width = values.shape[-1] // 2
    first_half = values[..., :half_width]
    second_half = values[..., half_width:]
    return jnp.concatenate(
        [
            first_half * cosine - second_half * sine_table,
            second_half * cosine + first_half * sine_table,
        ],
        -1,
    )


def rotate_back(grads_in, cosine, sine_table):
    return rotate(grads_in, cosine, -sine_table)


def silu_parts(gate_in):
    sigma = jax.nn.sigmoid(gate_in)
    return (gate_in * sigma, sigma * (1.0 + gate_in * (1.0 - sigma)))


def rms_scale(values):
    return lax.rsqrt(jnp.mean(values * values, -1, keepdims=True) + EPS)


def norm_back(grad_in, normed, inverse):
    return inverse * (grad_in - normed * jnp.mean(grad_in * normed, -1, keepdims=True))


def dot(left, right):
    return jnp.dot(left, right, preferred_element_type=F32)


def dot_t(left, right):
    return lax.dot_general(left, right, (((1,), (1,)), ((), ())), preferred_element_type=F32)


def t_dot(left, right):
    return lax.dot_general(left, right, (((0,), (0,)), ((), ())), preferred_element_type=F32)


def cross(values, bit):
    count = lax.axis_size("expert")
    return lax.ppermute(values, "expert", [(i, i ^ bit) for i in range(count)])


def swap(values):
    return lax.ppermute(values, "shard", [(0, 1), (1, 0)])


def whole_rows(weight):
    if lax.axis_size("shard") != 2:
        return lax.all_gather(weight, "shard", axis=0, tiled=True)
    other = swap(weight)
    first = lax.axis_index("shard") == 0
    return jnp.where(
        first, jnp.concatenate([weight, other], 0), jnp.concatenate([other, weight], 0)
    )


def row_blocks(weight):
    count = lax.axis_size("shard")
    if count == 2:
        own = lax.axis_index("shard")
        return [(own, weight), (1 - own, swap(weight))]
    blocks = lax.all_gather(weight, "shard", axis=0)
    return [(j, blocks[j]) for j in range(count)]


def times(values, blocks):
    rows = blocks[0][1].shape[0]
    return sum(
        dot(lax.dynamic_slice_in_dim(values, place * rows, rows, 1), block)
        for place, block in blocks
    )


def times_back(grads, blocks):
    pieces = [dot_t(grads, block) for _, block in blocks]
    if len(pieces) != 2:
        return jnp.concatenate(pieces, 1)
    first = lax.axis_index("shard") == 0
    return jnp.where(first, jnp.concatenate(pieces, 1), jnp.concatenate(pieces[::-1], 1))


def collect(values, bits):
    places = [0]
    for bit in bits:
        values = jnp.concatenate([values, cross(values, bit)], 0)
        places = places + [place ^ bit for place in places]
    return values, places


def after(value, *gates):
    leaves, tree = jax.tree.flatten(value)
    fenced = lax.optimization_barrier((*leaves, *jax.tree.leaves(gates)))
    return jax.tree.unflatten(tree, fenced[: len(leaves)])


def fold_step(pieces, bit, *gates):
    count = pieces[0].shape[0] // 2
    sent = sum(p[count:].astype(F32) for p in pieces).astype(BF)
    return [p[:count] for p in pieces] + [cross(after(sent, *gates), bit)]


def fold_end(pieces):
    return sum(p.astype(F32) for p in pieces)


def fold(pieces, bits):
    for bit in bits:
        pieces = fold_step(pieces, bit)
    return fold_end(pieces)


def fold_order(bits):
    places = [0]
    for bit in reversed(bits):
        places = places + [place ^ bit for place in places]
    return places


def differing(blocks, bits, here):
    count = len(bits)
    blocks = blocks.reshape((2,) * count + blocks.shape[1:])
    ranked = sorted(bits, reverse=True)
    for k, bit in enumerate(ranked):
        blocks = jnp.where(here // bit % 2 == 1, jnp.flip(blocks, k), blocks)
    axes = [ranked.index(bit) for bit in bits]
    blocks = blocks.transpose(axes + list(range(count, blocks.ndim)))
    return blocks.reshape((1 << count,) + blocks.shape[count:])


def gradient_kernel(rows, order_ref, left_ref, right_ref, kept_ref, sent_ref, picked_ref):
    count = picked_ref.shape[0] // rows

    @pl.when(pl.program_id(0) == 0)
    def _():
        for j in range(count):
            start = pl.multiple_of(order_ref[j] * rows, rows)
            picked_ref[j * rows : (j + 1) * rows, :] = left_ref[pl.ds(start, rows), :]

    half = kept_ref.shape[0]
    right = right_ref[...]
    kept_ref[...] = dot(picked_ref[:half, :].astype(BF), right).astype(kept_ref.dtype)
    sent_ref[...] = dot(picked_ref[half:, :].astype(BF), right).astype(sent_ref.dtype)


def gradient_halves(left, right, blocks, bits):
    count = 1 << len(bits)
    rows_all, tokens = left.shape
    columns = right.shape[1]
    rows = rows_all // count
    half = rows_all // 2
    if rows % 8:
        picked = differing(left.reshape(count, rows, tokens), bits, blocks).reshape(-1, tokens)
        product = dot(picked, right).astype(BF)
        return product[:half], product[half:]
    order = []
    for place in fold_order(bits):
        block = 0
        for k, bit in enumerate(sorted(bits)):
            flipped = (blocks >> bit.bit_length() - 1) & 1
            block = block + ((flipped ^ (place // bit & 1)) << k)
        order.append(block)
    if rows % 16:
        left = left.astype(F32)
    tile = next(t for t in (512, 384, 256, 128, columns) if columns % t == 0)
    return pl.pallas_call(
        functools.partial(gradient_kernel, rows),
        grid_spec=pltpu.PrefetchScalarGridSpec(
            num_scalar_prefetch=1,
            grid=(columns // tile,),
            in_specs=[
                pl.BlockSpec((rows_all, tokens), lambda i, order: (0, 0)),
                pl.BlockSpec((tokens, tile), lambda i, order: (0, i)),
            ],
            out_specs=[
                pl.BlockSpec((half, tile), lambda i, order: (0, i)),
                pl.BlockSpec((half, tile), lambda i, order: (0, i)),
            ],
            scratch_shapes=[pltpu.VMEM((rows_all, tokens), left.dtype)],
        ),
        out_shape=[jax.ShapeDtypeStruct((half, columns), BF)] * 2,
        compiler_params=pltpu.CompilerParams(vmem_limit_bytes=40 << 20),
        cost_estimate=pl.CostEstimate(
            flops=4 * half * tokens * columns,
            bytes_accessed=4 * half * columns + 2 * tokens * (rows_all + columns),
            transcendentals=0,
        ),
    )(jnp.stack(order).astype(jnp.int32), left, right)


def group_left(left, bit):
    experts, shards = lax.axis_size("expert"), lax.axis_size("shard")
    tokens, columns = left.shape
    own = lax.axis_index("expert") // bit % 2
    blocks = left.T.reshape(experts // (2 * bit), 2, bit, shards, -1, tokens)
    kept = lax.dynamic_index_in_dim(blocks, own, 1, keepdims=False)
    sent = lax.dynamic_index_in_dim(blocks, 1 - own, 1, keepdims=False)
    blocks = jnp.concatenate([kept, cross(sent, bit)], -1).reshape(
        experts // 2, shards, -1, 2 * tokens
    )
    if shards != 2:
        blocks = lax.all_to_all(blocks, "shard", split_axis=1, concat_axis=3, tiled=True)
        return blocks.reshape(columns // (2 * shards), -1)
    own = lax.axis_index("shard")
    kept = lax.dynamic_index_in_dim(blocks, own, 1, keepdims=False)
    sent = lax.dynamic_index_in_dim(blocks, 1 - own, 1, keepdims=False)
    return jnp.concatenate([kept, swap(sent)], -1).reshape(columns // 4, -1)


def group_right(right, bit):
    right = jnp.concatenate([right, cross(right, bit)], 0)
    if lax.axis_size("shard") != 2:
        return lax.all_gather(right, "shard", axis=0, tiled=True)
    return jnp.concatenate([right, swap(right)], 0)


def product_group(left, right, bit):
    return group_left(left, bit), group_right(right, bit)


def product_halves(group, bits):
    return gradient_halves(*group, lax.axis_index("expert"), bits)


def product_sum(group, bits):
    kept, sent = product_halves(group, bits[1:])
    return fold([kept, cross(sent, bits[1])], bits[2:])


def reduce_partial(partial, bits):
    experts, shards = lax.axis_size("expert"), lax.axis_size("shard")
    rows = partial.shape[0] // (experts * shards)
    if shards != 2:
        return lax.psum_scatter(partial, ("expert", "shard"), scatter_dimension=0, tiled=True)
    own = lax.axis_index("shard")
    blocks = partial.reshape(experts, 2, rows, partial.shape[1])
    kept = lax.dynamic_index_in_dim(blocks, own, 1, keepdims=False)
    sent = lax.dynamic_index_in_dim(blocks, 1 - own, 1, keepdims=False)
    total = (kept.astype(F32) + swap(sent).astype(F32)).astype(partial.dtype)
    return fold([differing(total, bits, lax.axis_index("expert")).reshape(experts * rows, -1)], bits)


def attend_kernel(
    raw_ref, cosine_ref, sine_ref, expand_ref, keys_ref, bias_ref,
    nope_ref, queries_ref, weights_ref, mixed_ref, out_ref,
):
    rows = raw_ref.shape[0]
    width = HEAD + ROPE
    cosine, sine = cosine_ref[...], sine_ref[...]
    for h in range(2):
        raw = raw_ref[:, h * width : (h + 1) * width]
        nope = raw[:, :HEAD].astype(BF)
        first = raw[:, HEAD : HEAD + ROPE // 2]
        second = raw[:, HEAD + ROPE // 2 :]
        turned = jnp.concatenate(
            [first * cosine - second * sine, second * cosine + first * sine], -1
        )
        nope_ref[:, h * HEAD : (h + 1) * HEAD] = nope
        latent = dot_t(nope, expand_ref[:, 2 * h * HEAD : (2 * h + 1) * HEAD])
        queries_ref[h * rows : (h + 1) * rows, :RANK] = latent.astype(BF)
        queries_ref[h * rows : (h + 1) * rows, RANK:] = turned.astype(BF)
    bias = bias_ref[...]
    for h in range(2):
        part = slice(h * rows, (h + 1) * rows)
        scores = dot_t(queries_ref[part, :], keys_ref[...]) * (HEAD + ROPE) ** -0.5 + bias
        shifted = jnp.exp(scores - jnp.max(scores, -1, keepdims=True))
        total = jnp.sum(shifted, -1, keepdims=True)
        weights_ref[part, :] = (shifted * (1.0 / total)).astype(BF)
    mixed_ref[...] = dot(weights_ref[...], keys_ref[:, :RANK]).astype(BF)
    for h in range(2):
        out_ref[:, h * VHEAD : (h + 1) * VHEAD] = dot(
            mixed_ref[h * rows : (h + 1) * rows, :],
            expand_ref[:, (2 * h + 1) * HEAD : (2 * h + 2) * HEAD],
        ).astype(BF)


def attend(query_raw, cosine, sine, expand, keys, bias):
    rows, slot = bias.shape
    steps = HEADS // 2
    whole = lambda *shape: pl.BlockSpec(shape, lambda i: (0,) * len(shape))
    return pl.pallas_call(
        attend_kernel,
        grid=(steps,),
        in_specs=[
            pl.BlockSpec((rows, 2 * (HEAD + ROPE)), lambda i: (0, i)),
            whole(rows, ROPE // 2),
            whole(rows, ROPE // 2),
            pl.BlockSpec((RANK, 4 * HEAD), lambda i: (0, i)),
            whole(slot, RANK + ROPE),
            whole(rows, slot),
        ],
        out_specs=[
            pl.BlockSpec((rows, 2 * HEAD), lambda i: (0, i)),
            pl.BlockSpec((2 * rows, RANK + ROPE), lambda i: (i, 0)),
            pl.BlockSpec((2 * rows, slot), lambda i: (i, 0)),
            pl.BlockSpec((2 * rows, RANK), lambda i: (i, 0)),
            pl.BlockSpec((rows, 2 * VHEAD), lambda i: (0, i)),
        ],
        out_shape=[
            jax.ShapeDtypeStruct((rows, HEADS * HEAD), BF),
            jax.ShapeDtypeStruct((HEADS * rows, RANK + ROPE), BF),
            jax.ShapeDtypeStruct((HEADS * rows, slot), BF),
            jax.ShapeDtypeStruct((HEADS * rows, RANK), BF),
            jax.ShapeDtypeStruct((rows, HEADS * VHEAD), BF),
        ],
        compiler_params=pltpu.CompilerParams(vmem_limit_bytes=40 << 20),
        cost_estimate=pl.CostEstimate(
            flops=2 * HEADS * rows * slot * (2 * RANK + ROPE),
            bytes_accessed=2 * HEADS * rows * slot,
            transcendentals=HEADS * rows * slot,
        ),
    )(query_raw, cosine, sine, expand, keys, bias)


def attend_back_kernel(
    grad_ref, expand_ref, keys_ref, weights_ref, queries_ref, mixed_ref, nope_ref, cosine_ref,
    sine_ref, query_grad_ref, expand_grad_ref, key_grad_ref, latent_ref, scores_ref,
):
    rows = grad_ref.shape[0]
    width = HEAD + ROPE
    scale = (HEAD + ROPE) ** -0.5

    @pl.when(pl.program_id(0) == 0)
    def _():
        key_grad_ref[...] = jnp.zeros_like(key_grad_ref)

    for h in range(2):
        part = slice(h * rows, (h + 1) * rows)
        grad = grad_ref[:, h * VHEAD : (h + 1) * VHEAD]
        latent_ref[part, :] = dot_t(
            grad, expand_ref[:, (2 * h + 1) * HEAD : (2 * h + 2) * HEAD]
        ).astype(BF)
        arrived = dot_t(latent_ref[part, :], keys_ref[:, :RANK])
        weights = weights_ref[part, :].astype(F32)
        mean = jnp.sum(weights * arrived, -1, keepdims=True)
        scores_ref[part, :] = (weights * (arrived - mean) * scale).astype(BF)
    key_grad_ref[...] += t_dot(queries_ref[...], scores_ref[...])
    key_grad_ref[:RANK, :] += t_dot(latent_ref[...], weights_ref[...])
    cosine, sine = cosine_ref[...], sine_ref[...]
    for h in range(2):
        part = slice(h * rows, (h + 1) * rows)
        query_grad = dot(scores_ref[part, :], keys_ref[...])
        latent = query_grad[:, :RANK].astype(BF)
        key_part = slice(2 * h * HEAD, (2 * h + 1) * HEAD)
        value_part = slice((2 * h + 1) * HEAD, (2 * h + 2) * HEAD)
        nope = dot(latent, expand_ref[:, key_part])
        first = query_grad[:, RANK : RANK + ROPE // 2]
        second = query_grad[:, RANK + ROPE // 2 :]
        query_grad_ref[:, h * width : (h + 1) * width] = jnp.concatenate(
            [nope, first * cosine + second * sine, second * cosine - first * sine], -1
        ).astype(BF)
        expand_grad_ref[:, key_part] = t_dot(
            latent, nope_ref[:, h * HEAD : (h + 1) * HEAD]
        ).astype(BF)
        expand_grad_ref[:, value_part] = t_dot(
            mixed_ref[part, :], grad_ref[:, h * VHEAD : (h + 1) * VHEAD]
        ).astype(BF)


def attend_back(grad_out, expand, keys, weights, queries, mixed, nope, cosine, sine):
    rows = grad_out.shape[0]
    slot = keys.shape[0]
    whole = lambda *shape: pl.BlockSpec(shape, lambda i: (0,) * len(shape))
    return pl.pallas_call(
        attend_back_kernel,
        grid=(HEADS // 2,),
        in_specs=[
            pl.BlockSpec((rows, 2 * VHEAD), lambda i: (0, i)),
            pl.BlockSpec((RANK, 4 * HEAD), lambda i: (0, i)),
            whole(slot, RANK + ROPE),
            pl.BlockSpec((2 * rows, slot), lambda i: (i, 0)),
            pl.BlockSpec((2 * rows, RANK + ROPE), lambda i: (i, 0)),
            pl.BlockSpec((2 * rows, RANK), lambda i: (i, 0)),
            pl.BlockSpec((rows, 2 * HEAD), lambda i: (0, i)),
            whole(rows, ROPE // 2),
            whole(rows, ROPE // 2),
        ],
        out_specs=[
            pl.BlockSpec((rows, 2 * (HEAD + ROPE)), lambda i: (0, i)),
            pl.BlockSpec((RANK, 4 * HEAD), lambda i: (0, i)),
            whole(RANK + ROPE, slot),
        ],
        out_shape=[
            jax.ShapeDtypeStruct((rows, HEADS * (HEAD + ROPE)), BF),
            jax.ShapeDtypeStruct((RANK, 2 * HEADS * HEAD), BF),
            jax.ShapeDtypeStruct((RANK + ROPE, slot), F32),
        ],
        scratch_shapes=[pltpu.VMEM((2 * rows, RANK), BF), pltpu.VMEM((2 * rows, slot), BF)],
        compiler_params=pltpu.CompilerParams(vmem_limit_bytes=48 << 20),
        cost_estimate=pl.CostEstimate(
            flops=2 * HEADS * rows * slot * (3 * RANK + 2 * (RANK + ROPE)),
            bytes_accessed=2 * HEADS * rows * slot,
            transcendentals=0,
        ),
    )(grad_out, expand, keys, weights, queries, mixed, nope, cosine, sine)


def pick_kernel(spread_ref, tokens_ref, *out_refs):
    for m, out_ref in enumerate(out_refs):
        out_ref[...] = dot(spread_ref[m], tokens_ref[...]).astype(BF)


def pick_rows(spread, tokens):
    planes, lines, capacity, count = spread.shape
    width = tokens.shape[-1]
    return pl.pallas_call(
        pick_kernel,
        grid=(lines,),
        in_specs=[
            pl.BlockSpec((planes, None, capacity, count), lambda j: (0, j, 0, 0)),
            pl.BlockSpec((None, count, width), lambda j: (j, 0, 0)),
        ],
        out_specs=[pl.BlockSpec((None, capacity, width), lambda j: (j, 0, 0))] * planes,
        out_shape=[jax.ShapeDtypeStruct((lines, capacity, width), BF)] * planes,
        compiler_params=pltpu.CompilerParams(vmem_limit_bytes=24 << 20),
        cost_estimate=pl.CostEstimate(
            flops=2 * planes * lines * capacity * count * width,
            bytes_accessed=2 * lines * (count + planes * capacity) * width,
            transcendentals=0,
        ),
    )(spread, tokens)


def put_kernel(spread_ref, *refs):
    refs[-1][...] = sum(t_dot(spread_ref[m], ref[...]) for m, ref in enumerate(refs[:-1]))


def put_rows(spread, rows):
    planes, lines, capacity, count = spread.shape
    width = rows[0].shape[-1]
    return pl.pallas_call(
        put_kernel,
        grid=(lines,),
        in_specs=[pl.BlockSpec((planes, None, capacity, count), lambda j: (0, j, 0, 0))]
        + [pl.BlockSpec((None, capacity, width), lambda j: (j, 0, 0))] * planes,
        out_specs=pl.BlockSpec((None, count, width), lambda j: (j, 0, 0)),
        out_shape=jax.ShapeDtypeStruct((lines, count, width), F32),
        compiler_params=pltpu.CompilerParams(vmem_limit_bytes=24 << 20),
        cost_estimate=pl.CostEstimate(
            flops=2 * planes * lines * capacity * count * width,
            bytes_accessed=2 * lines * (2 * count + planes * capacity) * width,
            transcendentals=0,
        ),
    )(spread, *rows)


def expert_kernel(sources, here_ref, rows_ref, grads_ref, router_ref, *refs):
    weights = refs[: 2 * sources]
    (
        row_grad_refs, units_ref, back_ref, gate_ref, logit_grad_ref, total_ref, probs_ref, share_ref,
    ) = (refs[2 * sources : 2 * sources + 2], *refs[2 * sources + 2 :])
    step = pl.program_id(0)
    chunks = pl.num_programs(0) // sources

    @pl.when(step == 0)
    def _():
        logits = dot_t(router_ref[...], rows_ref[...])
        powers = jnp.exp(logits - jnp.max(logits, 0, keepdims=True))
        probs = powers / jnp.sum(powers, 0, keepdims=True)
        own = lax.broadcasted_iota(jnp.int32, probs.shape, 0) == here_ref[0]
        probs_ref[...] = probs
        gate_ref[...] = jnp.sum(jnp.where(own, probs, 0.0), 0, keepdims=True)
        share_ref[...] = jnp.zeros_like(share_ref)
        total_ref[...] = jnp.zeros_like(total_ref)

    def work(in_ref, out_ref):
        gate = dot_t(in_ref[0], rows_ref[...])
        up = dot_t(in_ref[1], rows_ref[...])
        back = dot_t(out_ref[...], grads_ref[...])
        sigma = 1.0 / (1.0 + jnp.exp(-gate))
        act = gate * sigma
        units = (act * up).astype(BF)
        units_ref[...] = units
        share_ref[...] += jnp.sum(back * units.astype(F32), 0, keepdims=True)
        back = back * gate_ref[...]
        back_ref[0] = (back * up * (sigma * (1.0 + gate * (1.0 - sigma)))).astype(BF)
        back_ref[1] = (back * act).astype(BF)
        total_ref[...] += t_dot(back_ref[0], in_ref[0])
        total_ref[...] += t_dot(back_ref[1], in_ref[1])

    for k in range(sources):

        @pl.when(step // chunks == k)
        def _(k=k):
            work(weights[2 * k], weights[2 * k + 1])

    @pl.when(step == pl.num_programs(0) - 1)
    def _():
        probs = probs_ref[...]
        own = lax.broadcasted_iota(jnp.int32, probs.shape, 0) == here_ref[0]
        grad = probs * (own.astype(F32) - gate_ref[...]) * share_ref[...]
        logit_grad_ref[...] = grad.astype(BF)
        half = row_grad_refs[0].shape[1]
        for k, row_grad_ref in enumerate(row_grad_refs):
            part = slice(k * half, (k + 1) * half)
            row_grad_ref[...] = (
                total_ref[:, part] + t_dot(logit_grad_ref[...], router_ref[:, part])
            ).astype(BF)


def expert_pass(here, rows, grads, router, weights):
    count, width = rows.shape
    experts = router.shape[0]
    sources = len(weights)
    units = weights[0][1].shape[0]
    tile = next(t for t in (352, 176, 88, 64, 32, 16, units) if units % t == 0)
    chunks = units // tile
    once = pl.Buffered(1)
    in_specs = [
        pl.BlockSpec((count, width), lambda i, h: (0, 0), pipeline_mode=once),
        pl.BlockSpec((count, width), lambda i, h: (0, 0), pipeline_mode=once),
        pl.BlockSpec((experts, width), lambda i, h: (0, 0)),
    ]
    for k in range(sources):
        at = lambda i, k=k: jnp.clip(i - k * chunks, 0, chunks - 1)
        in_specs.append(pl.BlockSpec((2, tile, width), lambda i, h, at=at: (0, at(i), 0)))
        in_specs.append(pl.BlockSpec((tile, width), lambda i, h, at=at: (at(i), 0)))
    return pl.pallas_call(
        functools.partial(expert_kernel, sources),
        grid_spec=pltpu.PrefetchScalarGridSpec(
            num_scalar_prefetch=1,
            grid=(sources * chunks,),
            in_specs=in_specs,
            out_specs=[
                pl.BlockSpec((count, width // 2), lambda i, h: (0, 0), pipeline_mode=once),
                pl.BlockSpec((count, width // 2), lambda i, h: (0, 0), pipeline_mode=once),
                pl.BlockSpec((tile, count), lambda i, h: (i, 0)),
                pl.BlockSpec(
                    (None, 2, tile, count), lambda i, h: (i // chunks, 0, i % chunks, 0)
                ),
                pl.BlockSpec((1, count), lambda i, h: (0, 0)),
                pl.BlockSpec((experts, count), lambda i, h: (0, 0)),
            ],
            scratch_shapes=[
                pltpu.VMEM((count, width), F32),
                pltpu.VMEM((experts, count), F32),
                pltpu.VMEM((1, count), F32),
            ],
        ),
        out_shape=[
            jax.ShapeDtypeStruct((count, width // 2), BF),
            jax.ShapeDtypeStruct((count, width // 2), BF),
            jax.ShapeDtypeStruct((sources * units, count), BF),
            jax.ShapeDtypeStruct((sources, 2, units, count), BF),
            jax.ShapeDtypeStruct((1, count), F32),
            jax.ShapeDtypeStruct((experts, count), BF),
        ],
        compiler_params=pltpu.CompilerParams(vmem_limit_bytes=58 << 20),
        cost_estimate=pl.CostEstimate(
            flops=10 * count * width * sources * units,
            bytes_accessed=6 * (count + sources * units) * width,
            transcendentals=count * sources * units,
        ),
    )(here, rows, grads, router, *[piece for pair in weights for piece in pair])


def per_device(
    tokens,
    lengths,
    routes,
    attn_gain,
    query_weight,
    latent_weight,
    latent_gain,
    expand_weight,
    output_weight,
    ffn_gain,
    router_weight,
    shared_in,
    shared_out,
    expert_in,
    expert_out,
    cotangent,
):
    local_rows = tokens.shape[1]
    model_width = tokens.shape[2]
    owners, shards = lax.axis_size("expert"), lax.axis_size("shard")
    experts_all = router_weight.shape[1]
    assert experts_all == owners
    topk_count = routes.shape[2]
    capacity = max(2, 9 * local_rows * topk_count // (8 * experts_all))
    capacity = -(-capacity // 8) * 8
    here = lax.axis_index("expert")
    bits = [1 << k for k in range(owners.bit_length() - 1)]
    first_x = tuple(bits)
    first_y = tuple(bits[1:2] + bits[:1] + bits[2:])

    query_blocks = row_blocks(query_weight)
    latent_blocks = row_blocks(latent_weight)
    gains = jnp.concatenate([attn_gain, ffn_gain, latent_gain])[None]
    gains = (
        jnp.where(
            lax.axis_index("shard") == 0,
            jnp.concatenate([gains, swap(gains)], 0),
            jnp.concatenate([swap(gains), gains], 0),
        )
        if shards == 2
        else lax.all_gather(gains, "shard", axis=0, tiled=True)
    ).astype(F32)
    cut = attn_gain.shape[0]
    gain_attn = gains[:, :cut].reshape(-1)
    gain_ffn = gains[:, cut : 2 * cut].reshape(-1)
    gain_latent = gains[:, 2 * cut :].reshape(-1)
    expand = whole_rows(expand_weight)
    output_blocks = row_blocks(output_weight)
    router = whole_rows(router_weight)
    shared_out_blocks = row_blocks(shared_out)
    shared_in_blocks = row_blocks(shared_in)
    expert_in_rows = expert_in[0].transpose(1, 2, 0)
    if shards == 2:
        expert_weights = [
            (expert_in_rows, expert_out[0]),
            (swap(expert_in_rows), swap(expert_out[0])),
        ]
    else:
        expert_weights = [
            (
                lax.all_gather(expert_in_rows, "shard", axis=1, tiled=True),
                lax.all_gather(expert_out[0], "shard", axis=0, tiled=True),
            )
        ]

    here_index = here * local_rows + jnp.arange(local_rows, dtype=jnp.int32)
    query_segment, query_position, query_valid = layout(lengths[0], here_index)
    cosine, sine_table = rope_tables(query_position)
    live_rows = query_valid.astype(F32)[:, None]
    grad_out = cotangent[0].astype(F32) * live_rows
    grad_out_low = grad_out.astype(BF)

    plane = range(4)
    line_bits = tuple(reversed(bits[2:]))
    line_routes, line_places = collect(routes[0].T, line_bits)
    lines = len(line_places)
    line_routes = line_routes.reshape(lines, 1, topk_count, local_rows)
    expert_ids = (here ^ jnp.arange(len(plane), dtype=jnp.int32))[:, None, None, None]
    member = jnp.any(line_routes[None, :, 0] == expert_ids, 2).reshape(-1, local_rows)
    token_ids = jnp.arange(local_rows, dtype=jnp.int32)
    earlier = (token_ids[:, None] < token_ids[None, :]).astype(BF)
    rank = dot(member.astype(BF), earlier).astype(jnp.int32)
    place_ids = jnp.arange(capacity, dtype=jnp.int32)
    spread = (
        (member[:, None, :] & (rank[:, None, :] == place_ids[None, :, None]))
        .reshape(len(plane), lines, capacity, local_rows)
        .astype(BF)
    )

    def dispatch(values):
        gathered, _ = collect(values, line_bits)
        rows = pick_rows(spread, gathered.reshape(lines, local_rows, -1))
        rows = [rows[0]] + [cross(rows[m], m) for m in plane[1:]]
        return jnp.stack(rows).reshape(-1, values.shape[1])

    def in_plane(values):
        rows = values.reshape(len(plane), lines, capacity, -1)
        return [rows[0]] + [cross(rows[m], m) for m in plane[1:]]

    def along_line(rows):
        sums = put_rows(spread, rows).reshape(lines * local_rows, -1)
        return fold([sums], tuple(reversed(line_bits)))

    inputs = tokens[0].astype(F32)
    inverse_attn = rms_scale(inputs)
    normed_attn = inputs * inverse_attn
    attn_in = (normed_attn * gain_attn).astype(BF)
    latent_raw = times(attn_in, latent_blocks)
    latent = latent_raw[:, :RANK]
    inverse_latent = rms_scale(latent)
    normed_latent = latent * inverse_latent
    latent_in = (normed_latent * gain_latent).astype(BF)
    key_rope = rotate(latent_raw[:, RANK:], cosine, sine_table).astype(BF)
    own_keys = jnp.concatenate([latent_in, key_rope], -1)
    part = local_rows // 2
    collect_bits = (tuple(reversed(first_x)), tuple(reversed(first_y)))
    own_parts = [collect(own_keys[k * part : (k + 1) * part], line_bits)[0] for k in range(2)]
    grads_sent, *own_parts = lax.optimization_barrier((grad_out_low, *own_parts))
    keys, key_index = [], []
    for k in range(2):
        keys.append(collect(own_parts[k], collect_bits[k][len(line_bits) :])[0])
        places = [0]
        for bit in collect_bits[k]:
            places = places + [place ^ bit for place in places]
        key_index.append(
            (
                (here ^ jnp.array(places, jnp.int32))[:, None] * local_rows
                + k * part
                + jnp.arange(part, dtype=jnp.int32)[None, :]
            ).reshape(-1)
        )
    keys = jnp.concatenate(keys, 0)
    key_index = jnp.concatenate(key_index)
    received_grads = dispatch(grads_sent)

    query_raw = times(attn_in, query_blocks)
    key_segment = layout(lengths[0], key_index)[0]
    allowed = (query_segment[:, None] == key_segment[None, :]) & (
        key_index[None, :] <= here_index[:, None]
    )
    bias = jnp.where(allowed, 0.0, MASK_FILL).astype(F32)
    query_nope, queries, attention, mixed_latent, mixed_heads = attend(
        query_raw, cosine, sine_table, expand, keys, bias
    )
    mixed_heads = after(
        mixed_heads, received_grads, output_blocks, shared_in_blocks, shared_out_blocks, expert_weights
    )
    hidden_state = inputs + times(mixed_heads, output_blocks)
    inverse_ffn = rms_scale(hidden_state)
    normed_ffn = hidden_state * inverse_ffn
    ffn_in = (normed_ffn * gain_ffn).astype(BF)

    half_width = model_width // 2
    received = jnp.concatenate(
        [dispatch(ffn_in[:, k * half_width : (k + 1) * half_width]) for k in range(2)], 1
    )
    shared_both = times(ffn_in, shared_in_blocks)
    shared_act, shared_slope = silu_parts(shared_both[:, :FF_S])
    shared_up = shared_both[:, FF_S:]
    shared_hidden = (shared_act * shared_up).astype(BF)
    shared_result = times(shared_hidden, shared_out_blocks)
    grad_shared_hidden = times_back(grad_out_low, shared_out_blocks)
    grad_shared_gate = (grad_shared_hidden * shared_up * shared_slope).astype(BF)
    grad_shared_up = (grad_shared_hidden * shared_act).astype(BF)
    grad_ffn_in = times_back(
        jnp.concatenate([grad_shared_gate, grad_shared_up], -1), shared_in_blocks
    )
    shared_hidden, grad_shared_gate, grad_shared_up, received, shared_result, grad_ffn_in = after(
        (shared_hidden, grad_shared_gate, grad_shared_up, received, shared_result, grad_ffn_in)
    )

    shared_orders = (first_x, first_y, first_x)
    shared_groups = [
        product_group(shared_hidden, grad_out_low, shared_orders[0][0]),
        product_group(ffn_in, grad_shared_gate, shared_orders[1][0]),
        product_group(ffn_in, grad_shared_up, shared_orders[2][0]),
    ]
    expert_results = expert_pass(
        here[None], received, received_grads, router.T, expert_weights
    )
    *row_grads, hidden, hidden_grads, row_gate, row_grad_logits = after(
        expert_results, shared_groups
    )

    halves = [
        product_halves(group, order[1:]) for group, order in zip(shared_groups, shared_orders)
    ]
    row_grads = after([in_plane(part) for part in row_grads], halves)
    grad_routed = jnp.concatenate([along_line(part) for part in row_grads], 1)
    shared_sums = [
        [kept, cross(after(sent, row_grads), order[1])]
        for (kept, sent), order in zip(halves, shared_orders)
    ]
    grad_ffn_in = grad_ffn_in + grad_routed
    grad_gain_ffn = jnp.sum(grad_ffn_in * normed_ffn, 0)
    grad_hidden_state = grad_out + norm_back(grad_ffn_in * gain_ffn, normed_ffn, inverse_ffn)
    grad_attn_out = grad_hidden_state.astype(BF)
    grad_mixed = times_back(grad_attn_out, output_blocks).astype(BF)
    row_gate = row_gate.reshape(-1, 1)
    row_out = 0.0
    units = expert_weights[0][1].shape[0]
    for j, (_, weight) in enumerate(expert_weights):
        row_out = row_out + t_dot(hidden[j * units : (j + 1) * units], weight)
    row_out = (row_gate * row_out).astype(BF)

    grad_mixed, shared_sums, row_out = after((grad_mixed, shared_sums, row_out))
    shared_sums = [
        fold_step(pieces, order[2]) for pieces, order in zip(shared_sums, shared_orders)
    ]
    row_out = in_plane(row_out)
    attention_grads = attend_back(
        grad_mixed,
        expand,
        keys,
        attention,
        queries,
        mixed_latent,
        query_nope,
        cosine,
        sine_table,
    )
    (grad_query_raw, grad_expand, grad_keys), shared_sums, row_out = after(
        (attention_grads, shared_sums, row_out)
    )
    routed = along_line(row_out)
    block_result = hidden_state + shared_result + routed
    grad_shared_out, *grad_shared_in = [
        fold_end(fold_step(pieces, order[3])) for pieces, order in zip(shared_sums, shared_orders)
    ]
    grad_shared_in = jnp.concatenate(grad_shared_in, -1)
    grad_output = product_sum(
        product_group(after(mixed_heads, grad_attn_out), grad_attn_out, first_y[0]), first_y
    )

    weighted_grads = (row_gate * received_grads.astype(F32)).astype(BF)
    grad_expert_parts = [
        (
            dot(hidden_grads[j].reshape(2 * units, -1), received).reshape(2, units, -1),
            dot(hidden[j * units : (j + 1) * units], weighted_grads),
        )
        for j in range(len(expert_weights))
    ]
    if shards == 2:
        grad_expert_in, grad_expert_out = [
            own + swap(other.astype(BF)).astype(F32) for own, other in zip(*grad_expert_parts)
        ]
    else:
        grad_expert_in, grad_expert_out = [
            lax.psum_scatter(
                part.astype(BF), "shard", scatter_dimension=part.ndim - 2, tiled=True
            ).astype(F32)
            for part in grad_expert_parts[0]
        ]
    grad_expert_in = grad_expert_in.transpose(2, 0, 1)[None]
    grad_expert_out = grad_expert_out[None]
    grad_router = dot(row_grad_logits, received).T

    grad_keys = grad_keys.T.astype(BF)
    slot_half = SLOT // 2
    grad_own_keys = jnp.concatenate(
        [
            fold(
                [grad_keys[k * slot_half : (k + 1) * slot_half]],
                tuple(reversed(collect_bits[k])),
            )
            for k in range(2)
        ],
        0,
    )
    grad_expand = reduce_partial(grad_expand, first_x).astype(F32)
    grad_latent_in = grad_own_keys[:, :RANK]
    grad_gain_latent = jnp.sum(grad_latent_in * normed_latent, 0)
    grad_latent = norm_back(grad_latent_in * gain_latent, normed_latent, inverse_latent)
    grad_latent_raw = jnp.concatenate(
        [grad_latent, rotate_back(grad_own_keys[:, RANK:], cosine, sine_table)], -1
    ).astype(BF)
    late_attn_in = after(attn_in, grad_attn_out)
    left_x, left_y = [group_left(late_attn_in, order[0]) for order in (first_x, first_y)]
    query_half = grad_query_raw.shape[1] // 2
    grad_query = jnp.concatenate(
        [
            product_sum(
                (left_x, group_right(grad_query_raw[:, :query_half], first_x[0])), first_x
            ),
            product_sum(
                (left_y, group_right(grad_query_raw[:, query_half:], first_y[0])), first_y
            ),
        ],
        -1,
    )
    grad_latent_weight = product_sum(
        (left_y, group_right(grad_latent_raw, first_y[0])), first_y
    )
    grad_attn_in = times_back(grad_latent_raw, latent_blocks) + times_back(
        grad_query_raw, query_blocks
    )
    grad_gain_attn = jnp.sum(grad_attn_in * normed_attn, 0)
    tokens_grad = grad_hidden_state + norm_back(grad_attn_in * gain_attn, normed_attn, inverse_attn)

    devices = owners * shards
    rows = model_width // devices
    latent_column = jnp.pad(
        grad_gain_latent.reshape(devices, -1), ((0, 0), (0, rows - RANK // devices))
    ).reshape(-1, 1)
    small = jnp.concatenate(
        [grad_router, grad_gain_attn[:, None], grad_gain_ffn[:, None], latent_column], 1
    )
    small = reduce_partial(small, first_x).astype(F32)
    return (
        block_result.astype(BF)[None],
        tokens_grad.astype(BF)[None],
        small[:, experts_all],
        grad_query,
        grad_latent_weight,
        small[: RANK // devices, experts_all + 2],
        grad_expand,
        grad_output,
        small[:, experts_all + 1],
        small[:, :experts_all],
        grad_shared_in,
        grad_shared_out,
        grad_expert_in,
        grad_expert_out,
    )


def solution(mesh):
    return jax.shard_map(
        per_device,
        mesh=mesh,
        in_specs=(
            P("shard", "expert", None),
            P("shard", None),
            P("shard", "expert", None),
            P("shard"),
            P("shard", None),
            P("shard", None),
            P("shard"),
            P("shard", None),
            P("shard", None),
            P("shard"),
            P("shard", None),
            P("shard", None),
            P("shard", None),
            P("expert", None, None, "shard"),
            P("expert", "shard", None),
            P("shard", "expert", None),
        ),
        out_specs=(
            P("shard", "expert", None),
            P("shard", "expert", None),
            P(("expert", "shard")),
            P(("expert", "shard"), None),
            P(("expert", "shard"), None),
            P(("expert", "shard")),
            P(("expert", "shard"), None),
            P(("expert", "shard"), None),
            P(("expert", "shard")),
            P(("expert", "shard"), None),
            P(("expert", "shard"), None),
            P(("expert", "shard"), None),
            P("expert", None, None, "shard"),
            P("expert", "shard", None),
        ),
        check_vma=False,
    )
```

```python
import functools

import jax
import jax.numpy as jnp
from jax import lax
from jax.experimental import pallas as pl
from jax.experimental.pallas import tpu as pltpu
from jax.sharding import PartitionSpec as P

HEADS = 16
HEAD = 128
ROPE = 64
VHEAD = 128
RANK = 512
FF_S = 2816
SLOT = 2048

EPS = 1e-06
MASK_FILL = -1e30
BF = jnp.bfloat16
F32 = jnp.float32


def layout(lengths_slot, slot_index):
    first_len = lengths_slot[0]
    second_end = first_len + lengths_slot[1]
    segment = (slot_index >= first_len).astype(jnp.int32) + (slot_index >= second_end).astype(
        jnp.int32
    )
    seq_start = jnp.where(segment == 0, 0, jnp.where(segment == 1, first_len, second_end))
    return (segment, slot_index - seq_start, slot_index < second_end)


def rope_tables(positions):
    half_width = ROPE // 2
    inverse = 10000.0 ** (-jnp.arange(half_width, dtype=F32) / half_width)
    angles = positions.astype(F32)[:, None] * inverse[None, :]
    return (jnp.cos(angles), jnp.sin(angles))


def rotate(values, cosine, sine_table):
    half_width = values.shape[-1] // 2
    first_half = values[..., :half_width]
    second_half = values[..., half_width:]
    return jnp.concatenate(
        [
            first_half * cosine - second_half * sine_table,
            second_half * cosine + first_half * sine_table,
        ],
        -1,
    )


def rotate_back(grads_in, cosine, sine_table):
    return rotate(grads_in, cosine, -sine_table)


def silu_parts(gate_in):
    sigma = jax.nn.sigmoid(gate_in)
    return (gate_in * sigma, sigma * (1.0 + gate_in * (1.0 - sigma)))


def rms_scale(values):
    return lax.rsqrt(jnp.mean(values * values, -1, keepdims=True) + EPS)


def norm_back(grad_in, normed, inverse):
    return inverse * (grad_in - normed * jnp.mean(grad_in * normed, -1, keepdims=True))


def dot(left, right):
    return jnp.dot(left, right, preferred_element_type=F32)


def dot_t(left, right):
    return lax.dot_general(left, right, (((1,), (1,)), ((), ())), preferred_element_type=F32)


def t_dot(left, right):
    return lax.dot_general(left, right, (((0,), (0,)), ((), ())), preferred_element_type=F32)


def cross(values, bit):
    count = lax.axis_size("expert")
    return lax.ppermute(values, "expert", [(i, i ^ bit) for i in range(count)])


def swap(values):
    return lax.ppermute(values, "shard", [(0, 1), (1, 0)])


def whole_rows(weight):
    if lax.axis_size("shard") != 2:
        return lax.all_gather(weight, "shard", axis=0, tiled=True)
    other = swap(weight)
    first = lax.axis_index("shard") == 0
    return jnp.where(
        first, jnp.concatenate([weight, other], 0), jnp.concatenate([other, weight], 0)
    )


def row_blocks(weight):
    count = lax.axis_size("shard")
    if count == 2:
        own = lax.axis_index("shard")
        return [(own, weight), (1 - own, swap(weight))]
    blocks = lax.all_gather(weight, "shard", axis=0)
    return [(j, blocks[j]) for j in range(count)]


def times(values, blocks):
    rows = blocks[0][1].shape[0]
    return sum(
        dot(lax.dynamic_slice_in_dim(values, place * rows, rows, 1), block)
        for place, block in blocks
    )


def times_back(grads, blocks):
    pieces = [dot_t(grads, block) for _, block in blocks]
    if len(pieces) != 2:
        return jnp.concatenate(pieces, 1)
    first = lax.axis_index("shard") == 0
    return jnp.where(first, jnp.concatenate(pieces, 1), jnp.concatenate(pieces[::-1], 1))


def collect(values, bits):
    places = [0]
    for bit in bits:
        values = jnp.concatenate([values, cross(values, bit)], 0)
        places = places + [place ^ bit for place in places]
    return values, places


def together(*values):
    leaves, tree = jax.tree.flatten(values)
    return jax.tree.unflatten(tree, lax.optimization_barrier(leaves))


def fold_step(pieces, bit):
    count = pieces[0].shape[0] // 2
    sent = sum(p[count:].astype(F32) for p in pieces).astype(BF)
    return [p[:count] for p in pieces] + [cross(sent, bit)]


def fold_end(pieces):
    return sum(p.astype(F32) for p in pieces)


def fold(pieces, bits):
    for bit in bits:
        pieces = fold_step(pieces, bit)
    return fold_end(pieces)


def fold_order(bits):
    places = [0]
    for bit in reversed(bits):
        places = places + [place ^ bit for place in places]
    return places


def differing(blocks, bits, here):
    count = len(bits)
    blocks = blocks.reshape((2,) * count + blocks.shape[1:])
    ranked = sorted(bits, reverse=True)
    for k, bit in enumerate(ranked):
        blocks = jnp.where(here // bit % 2 == 1, jnp.flip(blocks, k), blocks)
    axes = [ranked.index(bit) for bit in bits]
    blocks = blocks.transpose(axes + list(range(count, blocks.ndim)))
    return blocks.reshape((1 << count,) + blocks.shape[count:])


def gradient_kernel(rows, order_ref, left_ref, right_ref, kept_ref, sent_ref, picked_ref):
    count = picked_ref.shape[0] // rows

    @pl.when(pl.program_id(0) == 0)
    def _():
        for j in range(count):
            start = pl.multiple_of(order_ref[j] * rows, rows)
            picked_ref[j * rows : (j + 1) * rows, :] = left_ref[pl.ds(start, rows), :]

    half = kept_ref.shape[0]
    right = right_ref[...]
    kept_ref[...] = dot(picked_ref[:half, :].astype(BF), right).astype(kept_ref.dtype)
    sent_ref[...] = dot(picked_ref[half:, :].astype(BF), right).astype(sent_ref.dtype)


def gradient_halves(left, right, blocks, bits):
    count = 1 << len(bits)
    rows_all, tokens = left.shape
    columns = right.shape[1]
    rows = rows_all // count
    half = rows_all // 2
    if rows % 8:
        picked = differing(left.reshape(count, rows, tokens), bits, blocks).reshape(-1, tokens)
        product = dot(picked, right).astype(BF)
        return product[:half], product[half:]
    order = []
    for place in fold_order(bits):
        block = 0
        for k, bit in enumerate(sorted(bits)):
            flipped = (blocks >> bit.bit_length() - 1) & 1
            block = block + ((flipped ^ (place // bit & 1)) << k)
        order.append(block)
    if rows % 16:
        left = left.astype(F32)
    tile = next(t for t in (512, 384, 256, 128, columns) if columns % t == 0)
    return pl.pallas_call(
        functools.partial(gradient_kernel, rows),
        grid_spec=pltpu.PrefetchScalarGridSpec(
            num_scalar_prefetch=1,
            grid=(columns // tile,),
            in_specs=[
                pl.BlockSpec((rows_all, tokens), lambda i, order: (0, 0)),
                pl.BlockSpec((tokens, tile), lambda i, order: (0, i)),
            ],
            out_specs=[
                pl.BlockSpec((half, tile), lambda i, order: (0, i)),
                pl.BlockSpec((half, tile), lambda i, order: (0, i)),
            ],
            scratch_shapes=[pltpu.VMEM((rows_all, tokens), left.dtype)],
        ),
        out_shape=[jax.ShapeDtypeStruct((half, columns), BF)] * 2,
        compiler_params=pltpu.CompilerParams(vmem_limit_bytes=40 << 20),
        cost_estimate=pl.CostEstimate(
            flops=4 * half * tokens * columns,
            bytes_accessed=4 * half * columns + 2 * tokens * (rows_all + columns),
            transcendentals=0,
        ),
    )(jnp.stack(order).astype(jnp.int32), left, right)


def cross_left(left, bit):
    experts, shards = lax.axis_size("expert"), lax.axis_size("shard")
    own = lax.axis_index("expert") // bit % 2
    blocks = left.T.reshape(experts // (2 * bit), 2, bit, shards, -1, left.shape[0])
    kept = lax.dynamic_index_in_dim(blocks, own, 1, keepdims=False)
    sent = lax.dynamic_index_in_dim(blocks, 1 - own, 1, keepdims=False)
    return kept, cross(sent, bit)


def pair_left(halves):
    experts, shards = lax.axis_size("expert"), lax.axis_size("shard")
    blocks = jnp.concatenate(halves, -1)
    blocks = blocks.reshape(experts // 2, shards, *blocks.shape[-2:])
    if shards != 2:
        blocks = lax.all_to_all(blocks, "shard", split_axis=1, concat_axis=3, tiled=True)
        return blocks.reshape(-1, blocks.shape[-1])
    own = lax.axis_index("shard")
    kept = lax.dynamic_index_in_dim(blocks, own, 1, keepdims=False)
    sent = lax.dynamic_index_in_dim(blocks, 1 - own, 1, keepdims=False)
    blocks = jnp.concatenate([kept, swap(sent)], -1)
    return blocks.reshape(-1, blocks.shape[-1])


def pair_right(halves):
    right = jnp.concatenate(halves, 0)
    if lax.axis_size("shard") != 2:
        return lax.all_gather(right, "shard", axis=0, tiled=True)
    return jnp.concatenate([right, swap(right)], 0)


def group_left(left, bit):
    return pair_left(cross_left(left, bit))


def group_right(right, bit):
    return pair_right((right, cross(right, bit)))


def product_group(left, right, bit):
    return group_left(left, bit), group_right(right, bit)


def product_halves(group, bits):
    return gradient_halves(*group, lax.axis_index("expert"), bits)


def product_sum(group, bits):
    kept, sent = product_halves(group, bits[1:])
    return fold([kept, cross(sent, bits[1])], bits[2:])


def pair_partial(partial, bits):
    experts, shards = lax.axis_size("expert"), lax.axis_size("shard")
    rows = partial.shape[0] // (experts * shards)
    if shards != 2:
        blocks = partial.reshape(experts, shards, rows, -1)
        total = lax.psum_scatter(blocks, "shard", scatter_dimension=1, tiled=True)[:, 0]
    else:
        own = lax.axis_index("shard")
        blocks = partial.reshape(experts, 2, rows, -1)
        kept = lax.dynamic_index_in_dim(blocks, own, 1, keepdims=False)
        sent = lax.dynamic_index_in_dim(blocks, 1 - own, 1, keepdims=False)
        total = (kept.astype(F32) + swap(sent).astype(F32)).astype(partial.dtype)
    return [differing(total, bits, lax.axis_index("expert")).reshape(experts * rows, -1)]


def attend_kernel(
    raw_ref, cosine_ref, sine_ref, expand_ref, keys_ref, bias_ref,
    nope_ref, queries_ref, weights_ref, mixed_ref, out_ref,
):
    rows = raw_ref.shape[0]
    width = HEAD + ROPE
    cosine, sine = cosine_ref[...], sine_ref[...]
    for h in range(2):
        raw = raw_ref[:, h * width : (h + 1) * width]
        nope = raw[:, :HEAD].astype(BF)
        first = raw[:, HEAD : HEAD + ROPE // 2]
        second = raw[:, HEAD + ROPE // 2 :]
        turned = jnp.concatenate(
            [first * cosine - second * sine, second * cosine + first * sine], -1
        )
        nope_ref[:, h * HEAD : (h + 1) * HEAD] = nope
        latent = dot_t(nope, expand_ref[:, 2 * h * HEAD : (2 * h + 1) * HEAD])
        queries_ref[h * rows : (h + 1) * rows, :RANK] = latent.astype(BF)
        queries_ref[h * rows : (h + 1) * rows, RANK:] = turned.astype(BF)
    bias = bias_ref[...]
    for h in range(2):
        part = slice(h * rows, (h + 1) * rows)
        scores = dot_t(queries_ref[part, :], keys_ref[...]) * (HEAD + ROPE) ** -0.5 + bias
        shifted = jnp.exp(scores - jnp.max(scores, -1, keepdims=True))
        total = jnp.sum(shifted, -1, keepdims=True)
        weights_ref[part, :] = (shifted * (1.0 / total)).astype(BF)
    mixed_ref[...] = dot(weights_ref[...], keys_ref[:, :RANK]).astype(BF)
    for h in range(2):
        out_ref[:, h * VHEAD : (h + 1) * VHEAD] = dot(
            mixed_ref[h * rows : (h + 1) * rows, :],
            expand_ref[:, (2 * h + 1) * HEAD : (2 * h + 2) * HEAD],
        ).astype(BF)


def attend(query_raw, cosine, sine, expand, keys, bias):
    rows, slot = bias.shape
    steps = HEADS // 2
    whole = lambda *shape: pl.BlockSpec(shape, lambda i: (0,) * len(shape))
    return pl.pallas_call(
        attend_kernel,
        grid=(steps,),
        in_specs=[
            pl.BlockSpec((rows, 2 * (HEAD + ROPE)), lambda i: (0, i)),
            whole(rows, ROPE // 2),
            whole(rows, ROPE // 2),
            pl.BlockSpec((RANK, 4 * HEAD), lambda i: (0, i)),
            whole(slot, RANK + ROPE),
            whole(rows, slot),
        ],
        out_specs=[
            pl.BlockSpec((rows, 2 * HEAD), lambda i: (0, i)),
            pl.BlockSpec((2 * rows, RANK + ROPE), lambda i: (i, 0)),
            pl.BlockSpec((2 * rows, slot), lambda i: (i, 0)),
            pl.BlockSpec((2 * rows, RANK), lambda i: (i, 0)),
            pl.BlockSpec((rows, 2 * VHEAD), lambda i: (0, i)),
        ],
        out_shape=[
            jax.ShapeDtypeStruct((rows, HEADS * HEAD), BF),
            jax.ShapeDtypeStruct((HEADS * rows, RANK + ROPE), BF),
            jax.ShapeDtypeStruct((HEADS * rows, slot), BF),
            jax.ShapeDtypeStruct((HEADS * rows, RANK), BF),
            jax.ShapeDtypeStruct((rows, HEADS * VHEAD), BF),
        ],
        compiler_params=pltpu.CompilerParams(vmem_limit_bytes=40 << 20),
        cost_estimate=pl.CostEstimate(
            flops=2 * HEADS * rows * slot * (2 * RANK + ROPE),
            bytes_accessed=2 * HEADS * rows * slot,
            transcendentals=HEADS * rows * slot,
        ),
    )(query_raw, cosine, sine, expand, keys, bias)


def attend_back_kernel(
    grad_ref, expand_ref, keys_ref, weights_ref, queries_ref, mixed_ref, nope_ref, cosine_ref,
    sine_ref, query_grad_ref, expand_grad_ref, key_out_ref, key_grad_ref, latent_ref, scores_ref,
):
    rows = grad_ref.shape[0]
    width = HEAD + ROPE
    scale = (HEAD + ROPE) ** -0.5

    @pl.when(pl.program_id(0) == 0)
    def _():
        key_grad_ref[...] = jnp.zeros_like(key_grad_ref)

    for h in range(2):
        part = slice(h * rows, (h + 1) * rows)
        grad = grad_ref[:, h * VHEAD : (h + 1) * VHEAD]
        latent_ref[part, :] = dot_t(
            grad, expand_ref[:, (2 * h + 1) * HEAD : (2 * h + 2) * HEAD]
        ).astype(BF)
        arrived = dot_t(latent_ref[part, :], keys_ref[:, :RANK])
        weights = weights_ref[part, :].astype(F32)
        mean = jnp.sum(weights * arrived, -1, keepdims=True)
        scores_ref[part, :] = (weights * (arrived - mean) * scale).astype(BF)
    key_grad_ref[...] += t_dot(queries_ref[...], scores_ref[...])
    key_grad_ref[:RANK, :] += t_dot(latent_ref[...], weights_ref[...])
    cosine, sine = cosine_ref[...], sine_ref[...]
    for h in range(2):
        part = slice(h * rows, (h + 1) * rows)
        query_grad = dot(scores_ref[part, :], keys_ref[...])
        latent = query_grad[:, :RANK].astype(BF)
        key_part = slice(2 * h * HEAD, (2 * h + 1) * HEAD)
        value_part = slice((2 * h + 1) * HEAD, (2 * h + 2) * HEAD)
        nope = dot(latent, expand_ref[:, key_part])
        first = query_grad[:, RANK : RANK + ROPE // 2]
        second = query_grad[:, RANK + ROPE // 2 :]
        query_grad_ref[:, h * width : (h + 1) * width] = jnp.concatenate(
            [nope, first * cosine + second * sine, second * cosine - first * sine], -1
        ).astype(BF)
        expand_grad_ref[:, key_part] = t_dot(
            latent, nope_ref[:, h * HEAD : (h + 1) * HEAD]
        ).astype(BF)
        expand_grad_ref[:, value_part] = t_dot(
            mixed_ref[part, :], grad_ref[:, h * VHEAD : (h + 1) * VHEAD]
        ).astype(BF)

    @pl.when(pl.program_id(0) == pl.num_programs(0) - 1)
    def _():
        key_out_ref[...] = key_grad_ref[...].T.astype(BF)


def attend_back(grad_out, expand, keys, weights, queries, mixed, nope, cosine, sine):
    rows = grad_out.shape[0]
    slot = keys.shape[0]
    whole = lambda *shape: pl.BlockSpec(shape, lambda i: (0,) * len(shape))
    return pl.pallas_call(
        attend_back_kernel,
        grid=(HEADS // 2,),
        in_specs=[
            pl.BlockSpec((rows, 2 * VHEAD), lambda i: (0, i)),
            pl.BlockSpec((RANK, 4 * HEAD), lambda i: (0, i)),
            whole(slot, RANK + ROPE),
            pl.BlockSpec((2 * rows, slot), lambda i: (i, 0)),
            pl.BlockSpec((2 * rows, RANK + ROPE), lambda i: (i, 0)),
            pl.BlockSpec((2 * rows, RANK), lambda i: (i, 0)),
            pl.BlockSpec((rows, 2 * HEAD), lambda i: (0, i)),
            whole(rows, ROPE // 2),
            whole(rows, ROPE // 2),
        ],
        out_specs=[
            pl.BlockSpec((rows, 2 * (HEAD + ROPE)), lambda i: (0, i)),
            pl.BlockSpec((RANK, 4 * HEAD), lambda i: (0, i)),
            whole(slot, RANK + ROPE),
        ],
        out_shape=[
            jax.ShapeDtypeStruct((rows, HEADS * (HEAD + ROPE)), BF),
            jax.ShapeDtypeStruct((RANK, 2 * HEADS * HEAD), BF),
            jax.ShapeDtypeStruct((slot, RANK + ROPE), BF),
        ],
        scratch_shapes=[
            pltpu.VMEM((RANK + ROPE, slot), F32),
            pltpu.VMEM((2 * rows, RANK), BF),
            pltpu.VMEM((2 * rows, slot), BF),
        ],
        compiler_params=pltpu.CompilerParams(vmem_limit_bytes=48 << 20),
        cost_estimate=pl.CostEstimate(
            flops=2 * HEADS * rows * slot * (3 * RANK + 2 * (RANK + ROPE)),
            bytes_accessed=2 * HEADS * rows * slot,
            transcendentals=0,
        ),
    )(grad_out, expand, keys, weights, queries, mixed, nope, cosine, sine)


def expert_kernel(sources, here_ref, rows_ref, grads_ref, router_ref, *refs):
    weights = refs[: 2 * sources]
    (
        row_grad_ref, units_ref, back_ref, gate_ref, logit_grad_ref, total_ref, probs_ref, share_ref,
    ) = refs[2 * sources :]
    step = pl.program_id(0)
    chunks = pl.num_programs(0) // sources

    @pl.when(step == 0)
    def _():
        logits = dot_t(router_ref[...], rows_ref[...])
        powers = jnp.exp(logits - jnp.max(logits, 0, keepdims=True))
        probs = powers / jnp.sum(powers, 0, keepdims=True)
        own = lax.broadcasted_iota(jnp.int32, probs.shape, 0) == here_ref[0]
        probs_ref[...] = probs
        gate_ref[...] = jnp.sum(jnp.where(own, probs, 0.0), 0, keepdims=True)
        share_ref[...] = jnp.zeros_like(share_ref)
        total_ref[...] = jnp.zeros_like(total_ref)

    def work(in_ref, out_ref):
        gate = dot_t(in_ref[0], rows_ref[...])
        up = dot_t(in_ref[1], rows_ref[...])
        back = dot_t(out_ref[...], grads_ref[...])
        sigma = 1.0 / (1.0 + jnp.exp(-gate))
        act = gate * sigma
        units = (act * up).astype(BF)
        units_ref[...] = units
        share_ref[...] += jnp.sum(back * units.astype(F32), 0, keepdims=True)
        back = back * gate_ref[...]
        back_ref[0] = (back * up * (sigma * (1.0 + gate * (1.0 - sigma)))).astype(BF)
        back_ref[1] = (back * act).astype(BF)
        total_ref[...] += t_dot(back_ref[0], in_ref[0])
        total_ref[...] += t_dot(back_ref[1], in_ref[1])

    for k in range(sources):

        @pl.when(step // chunks == k)
        def _(k=k):
            work(weights[2 * k], weights[2 * k + 1])

    @pl.when(step == pl.num_programs(0) - 1)
    def _():
        probs = probs_ref[...]
        own = lax.broadcasted_iota(jnp.int32, probs.shape, 0) == here_ref[0]
        grad = probs * (own.astype(F32) - gate_ref[...]) * share_ref[...]
        logit_grad_ref[...] = grad.astype(BF)
        row_grad_ref[...] = (
            total_ref[...] + t_dot(logit_grad_ref[...], router_ref[...])
        ).astype(BF)


def expert_pass(here, rows, grads, router, weights):
    count, width = rows.shape
    experts = router.shape[0]
    sources = len(weights)
    units = weights[0][1].shape[0]
    tile = next(t for t in (352, 176, 88, 64, 32, 16, units) if units % t == 0)
    chunks = units // tile
    once = pl.Buffered(1)
    in_specs = [
        pl.BlockSpec((count, width), lambda i, h: (0, 0), pipeline_mode=once),
        pl.BlockSpec((count, width), lambda i, h: (0, 0), pipeline_mode=once),
        pl.BlockSpec((experts, width), lambda i, h: (0, 0)),
    ]
    for k in range(sources):
        at = lambda i, k=k: jnp.clip(i - k * chunks, 0, chunks - 1)
        in_specs.append(pl.BlockSpec((2, tile, width), lambda i, h, at=at: (0, at(i), 0)))
        in_specs.append(pl.BlockSpec((tile, width), lambda i, h, at=at: (at(i), 0)))
    return pl.pallas_call(
        functools.partial(expert_kernel, sources),
        grid_spec=pltpu.PrefetchScalarGridSpec(
            num_scalar_prefetch=1,
            grid=(sources * chunks,),
            in_specs=in_specs,
            out_specs=[
                pl.BlockSpec((count, width), lambda i, h: (0, 0), pipeline_mode=once),
                pl.BlockSpec((tile, count), lambda i, h: (i, 0)),
                pl.BlockSpec(
                    (None, 2, tile, count), lambda i, h: (i // chunks, 0, i % chunks, 0)
                ),
                pl.BlockSpec((1, count), lambda i, h: (0, 0)),
                pl.BlockSpec((experts, count), lambda i, h: (0, 0)),
            ],
            scratch_shapes=[
                pltpu.VMEM((count, width), F32),
                pltpu.VMEM((experts, count), F32),
                pltpu.VMEM((1, count), F32),
            ],
        ),
        out_shape=[
            jax.ShapeDtypeStruct((count, width), BF),
            jax.ShapeDtypeStruct((sources * units, count), BF),
            jax.ShapeDtypeStruct((sources, 2, units, count), BF),
            jax.ShapeDtypeStruct((1, count), F32),
            jax.ShapeDtypeStruct((experts, count), BF),
        ],
        compiler_params=pltpu.CompilerParams(vmem_limit_bytes=58 << 20),
        cost_estimate=pl.CostEstimate(
            flops=10 * count * width * sources * units,
            bytes_accessed=6 * (count + sources * units) * width,
            transcendentals=count * sources * units,
        ),
    )(here, rows, grads, router, *[piece for pair in weights for piece in pair])


def per_device(
    tokens,
    lengths,
    routes,
    attn_gain,
    query_weight,
    latent_weight,
    latent_gain,
    expand_weight,
    output_weight,
    ffn_gain,
    router_weight,
    shared_in,
    shared_out,
    expert_in,
    expert_out,
    cotangent,
):
    local_rows = tokens.shape[1]
    model_width = tokens.shape[2]
    owners, shards = lax.axis_size("expert"), lax.axis_size("shard")
    experts_all = router_weight.shape[1]
    assert experts_all == owners
    topk_count = routes.shape[2]
    capacity = max(2, 9 * local_rows * topk_count // (8 * experts_all))
    capacity = -(-capacity // 8) * 8
    here = lax.axis_index("expert")
    bits = [1 << k for k in range(owners.bit_length() - 1)]
    first_x = tuple(bits)
    first_y = tuple(bits[1:2] + bits[:1] + bits[2:])

    query_blocks = row_blocks(query_weight)
    latent_blocks = row_blocks(latent_weight)
    gains = jnp.concatenate([attn_gain, ffn_gain, latent_gain])[None]
    gains = (
        jnp.where(
            lax.axis_index("shard") == 0,
            jnp.concatenate([gains, swap(gains)], 0),
            jnp.concatenate([swap(gains), gains], 0),
        )
        if shards == 2
        else lax.all_gather(gains, "shard", axis=0, tiled=True)
    ).astype(F32)
    cut = attn_gain.shape[0]
    gain_attn = gains[:, :cut].reshape(-1)
    gain_ffn = gains[:, cut : 2 * cut].reshape(-1)
    gain_latent = gains[:, 2 * cut :].reshape(-1)
    expand = whole_rows(expand_weight)
    output_blocks = row_blocks(output_weight)
    router = whole_rows(router_weight)
    shared_out_blocks = row_blocks(shared_out)
    shared_in_blocks = row_blocks(shared_in)
    expert_in_rows = expert_in[0].transpose(1, 2, 0)
    if shards == 2:
        expert_weights = [
            (expert_in_rows, expert_out[0]),
            (swap(expert_in_rows), swap(expert_out[0])),
        ]
    else:
        expert_weights = [
            (
                lax.all_gather(expert_in_rows, "shard", axis=1, tiled=True),
                lax.all_gather(expert_out[0], "shard", axis=0, tiled=True),
            )
        ]

    here_index = here * local_rows + jnp.arange(local_rows, dtype=jnp.int32)
    query_segment, query_position, query_valid = layout(lengths[0], here_index)
    cosine, sine_table = rope_tables(query_position)
    live_rows = query_valid.astype(F32)[:, None]
    grad_out = cotangent[0].astype(F32) * live_rows
    grad_out_low = grad_out.astype(BF)

    expert_ids = jnp.arange(experts_all, dtype=jnp.int32)
    member = jnp.any(routes[0].T[None] == expert_ids[:, None, None], 1)
    token_ids = jnp.arange(local_rows, dtype=jnp.int32)
    earlier = (token_ids[:, None] < token_ids[None, :]).astype(BF)
    rank = dot(member.astype(BF), earlier).astype(jnp.int32)
    place_ids = jnp.arange(capacity, dtype=jnp.int32)
    spread = (
        (member[:, None, :] & (rank[:, None, :] == place_ids[None, :, None]))
        .reshape(experts_all * capacity, local_rows)
        .astype(BF)
    )

    def exchange(rows):
        return lax.all_to_all(
            rows.reshape(owners, capacity, model_width),
            "expert",
            split_axis=0,
            concat_axis=0,
            tiled=True,
        ).reshape(owners * capacity, model_width)

    received_grads = exchange(dot(spread, grad_out_low).astype(BF))

    inputs = tokens[0].astype(F32)
    inverse_attn = rms_scale(inputs)
    normed_attn = inputs * inverse_attn
    attn_in = (normed_attn * gain_attn).astype(BF)
    latent_raw = times(attn_in, latent_blocks)
    latent = latent_raw[:, :RANK]
    inverse_latent = rms_scale(latent)
    normed_latent = latent * inverse_latent
    latent_in = (normed_latent * gain_latent).astype(BF)
    key_rope = rotate(latent_raw[:, RANK:], cosine, sine_table).astype(BF)
    own_keys = jnp.concatenate([latent_in, key_rope], -1)
    part = local_rows // 2
    collect_bits = (tuple(reversed(first_x)), tuple(reversed(first_y)))
    keys, key_index = [], []
    for k in range(2):
        gathered, places = collect(own_keys[k * part : (k + 1) * part], collect_bits[k])
        keys.append(gathered)
        key_index.append(
            (
                (here ^ jnp.array(places, jnp.int32))[:, None] * local_rows
                + k * part
                + jnp.arange(part, dtype=jnp.int32)[None, :]
            ).reshape(-1)
        )
    keys = jnp.concatenate(keys, 0)
    key_index = jnp.concatenate(key_index)

    query_raw = times(attn_in, query_blocks)
    key_segment = layout(lengths[0], key_index)[0]
    allowed = (query_segment[:, None] == key_segment[None, :]) & (
        key_index[None, :] <= here_index[:, None]
    )
    bias = jnp.where(allowed, 0.0, MASK_FILL).astype(F32)
    query_nope, queries, attention, mixed_latent, mixed_heads = attend(
        query_raw, cosine, sine_table, expand, keys, bias
    )
    (
        mixed_heads, received_grads, output_blocks, router, shared_in_blocks, shared_out_blocks,
        expert_weights,
    ) = together(
        mixed_heads, received_grads, output_blocks, router, shared_in_blocks, shared_out_blocks,
        expert_weights,
    )
    hidden_state = inputs + times(mixed_heads, output_blocks)
    inverse_ffn = rms_scale(hidden_state)
    normed_ffn = hidden_state * inverse_ffn
    ffn_in = (normed_ffn * gain_ffn).astype(BF)

    received = exchange(dot(spread, ffn_in).astype(BF))
    shared_both = times(ffn_in, shared_in_blocks)
    shared_act, shared_slope = silu_parts(shared_both[:, :FF_S])
    shared_up = shared_both[:, FF_S:]
    shared_hidden = (shared_act * shared_up).astype(BF)
    shared_result = times(shared_hidden, shared_out_blocks)
    grad_shared_hidden = times_back(grad_out_low, shared_out_blocks)
    grad_shared_gate = (grad_shared_hidden * shared_up * shared_slope).astype(BF)
    grad_shared_up = (grad_shared_hidden * shared_act).astype(BF)
    grad_ffn_in = times_back(
        jnp.concatenate([grad_shared_gate, grad_shared_up], -1), shared_in_blocks
    )
    (
        shared_hidden, grad_shared_gate, grad_shared_up, received, shared_result, grad_ffn_in,
        shared_in, late_grad_out,
    ) = together(
        shared_hidden, grad_shared_gate, grad_shared_up, received, shared_result, grad_ffn_in,
        ffn_in, grad_out_low,
    )

    shared_orders = ((4, 1, 2, 8), (4, 2, 1, 8), (4, 1, 2, 8))
    shared_lefts = [
        cross_left(left, order[0])
        for left, order in zip((shared_hidden, shared_in, shared_in), shared_orders)
    ]
    shared_rights = [
        (right, cross(right, order[0]))
        for right, order in zip((late_grad_out, grad_shared_gate, grad_shared_up), shared_orders)
    ]
    expert_results = expert_pass(
        here[None], received, received_grads, router.T, expert_weights
    )
    expert_results, shared_lefts, shared_rights = together(
        expert_results, shared_lefts, shared_rights
    )
    shared_groups = [
        (pair_left(left), pair_right(right)) for left, right in zip(shared_lefts, shared_rights)
    ]
    row_grads, hidden, hidden_grads, row_gate, row_grad_logits = expert_results

    returned_grads = exchange(row_grads)
    halves = [
        product_halves(group, order[1:]) for group, order in zip(shared_groups, shared_orders)
    ]
    shared_sums = [[kept, cross(sent, order[1])] for (kept, sent), order in zip(halves, shared_orders)]
    row_gate = row_gate.reshape(-1, 1)
    row_out = 0.0
    units = expert_weights[0][1].shape[0]
    for j, (_, weight) in enumerate(expert_weights):
        row_out = row_out + t_dot(hidden[j * units : (j + 1) * units], weight)
    row_out = (row_gate * row_out).astype(BF)
    weighted_grads = (row_gate * received_grads.astype(F32)).astype(BF)
    grad_expert_parts = [
        (
            dot(hidden_grads[j].reshape(2 * units, -1), received).reshape(2, units, -1),
            dot(hidden[j * units : (j + 1) * units], weighted_grads),
        )
        for j in range(len(expert_weights))
    ]
    if shards == 2:
        grad_expert_in, grad_expert_out = [
            own + swap(other.astype(BF)).astype(F32) for own, other in zip(*grad_expert_parts)
        ]
    else:
        grad_expert_in, grad_expert_out = [
            lax.psum_scatter(
                part.astype(BF), "shard", scatter_dimension=part.ndim - 2, tiled=True
            ).astype(F32)
            for part in grad_expert_parts[0]
        ]
    grad_router = dot(row_grad_logits, received)
    returned_grads, row_out, grad_expert_in, grad_expert_out, grad_router, shared_sums = together(
        returned_grads, row_out, grad_expert_in, grad_expert_out, grad_router, shared_sums
    )
    grad_expert_in = grad_expert_in.transpose(2, 0, 1)[None]
    grad_expert_out = grad_expert_out[None]
    returned = exchange(row_out)
    grad_ffn_in = grad_ffn_in + t_dot(spread, returned_grads)
    grad_gain_ffn = jnp.sum(grad_ffn_in * normed_ffn, 0)
    grad_hidden_state = grad_out + norm_back(grad_ffn_in * gain_ffn, normed_ffn, inverse_ffn)

    grad_attn_out = grad_hidden_state.astype(BF)
    late_attn_in, late_heads, grad_attn_out = together(attn_in, mixed_heads, grad_attn_out)
    grad_mixed = times_back(grad_attn_out, output_blocks).astype(BF)
    left_x, left_y = [group_left(late_attn_in, order[0]) for order in (first_x, first_y)]
    output_group = product_group(late_heads, grad_attn_out, first_y[0])
    grad_mixed, shared_sums = together(grad_mixed, shared_sums)
    shared_sums = [
        fold_step(pieces, order[2]) for pieces, order in zip(shared_sums, shared_orders)
    ]
    attention_grads = attend_back(
        grad_mixed,
        expand,
        keys,
        attention,
        queries,
        mixed_latent,
        query_nope,
        cosine,
        sine_table,
    )
    (grad_query_raw, grad_expand, grad_keys), shared_sums = together(attention_grads, shared_sums)
    shared_sums = [
        fold_step(pieces, order[3]) for pieces, order in zip(shared_sums, shared_orders)
    ]
    slot_half = SLOT // 2
    grad_own_keys = jnp.concatenate(
        [
            fold(
                [grad_keys[k * slot_half : (k + 1) * slot_half]],
                tuple(reversed(collect_bits[k])),
            )
            for k in range(2)
        ],
        0,
    )
    query_half = grad_query_raw.shape[1] // 2
    grad_query = jnp.concatenate(
        [
            product_sum(
                (left_x, group_right(grad_query_raw[:, :query_half], first_x[0])), first_x
            ),
            product_sum(
                (left_y, group_right(grad_query_raw[:, query_half:], first_y[0])), first_y
            ),
        ],
        -1,
    )
    expand_sums = fold_step(pair_partial(grad_expand, first_x), first_x[0])
    grad_own_keys, expand_sums = together(grad_own_keys, expand_sums)
    grad_expand = fold(expand_sums, first_x[1:])
    grad_output = product_sum(output_group, first_y)
    grad_latent_in = grad_own_keys[:, :RANK]
    grad_gain_latent = jnp.sum(grad_latent_in * normed_latent, 0)
    grad_latent = norm_back(grad_latent_in * gain_latent, normed_latent, inverse_latent)
    grad_latent_raw = jnp.concatenate(
        [grad_latent, rotate_back(grad_own_keys[:, RANK:], cosine, sine_table)], -1
    ).astype(BF)
    grad_latent_late, shared_sums = together(grad_latent_raw, shared_sums)
    grad_shared_out, *grad_shared_in = [fold_end(pieces) for pieces in shared_sums]
    grad_shared_in = jnp.concatenate(grad_shared_in, -1)
    grad_latent_weight = product_sum(
        (left_y, group_right(grad_latent_late, first_y[0])), first_y
    )
    grad_attn_in = times_back(grad_latent_raw, latent_blocks) + times_back(
        grad_query_raw, query_blocks
    )
    grad_gain_attn = jnp.sum(grad_attn_in * normed_attn, 0)
    tokens_grad = grad_hidden_state + norm_back(grad_attn_in * gain_attn, normed_attn, inverse_attn)
    devices = owners * shards
    rows = model_width // devices
    small = jnp.concatenate(
        [
            vector.reshape(devices, -1)
            for vector in (grad_router.T, grad_gain_attn, grad_gain_ffn, grad_gain_latent)
        ],
        1,
    )
    small, returned = together(small, returned)
    small = lax.all_to_all(small, ("expert", "shard"), split_axis=0, concat_axis=0, tiled=True)
    small = jnp.sum(small, 0)
    routed = t_dot(spread, returned)
    block_result = hidden_state + shared_result + routed
    cuts = [rows * experts_all, rows * (experts_all + 1), rows * (experts_all + 2)]
    return (
        block_result.astype(BF)[None],
        tokens_grad.astype(BF)[None],
        small[cuts[0] : cuts[1]],
        grad_query,
        grad_latent_weight,
        small[cuts[2] :],
        grad_expand,
        grad_output,
        small[cuts[1] : cuts[2]],
        small[: cuts[0]].reshape(rows, experts_all),
        grad_shared_in,
        grad_shared_out,
        grad_expert_in,
        grad_expert_out,
    )


def solution(mesh):
    return jax.shard_map(
        per_device,
        mesh=mesh,
        in_specs=(
            P("shard", "expert", None),
            P("shard", None),
            P("shard", "expert", None),
            P("shard"),
            P("shard", None),
            P("shard", None),
            P("shard"),
            P("shard", None),
            P("shard", None),
            P("shard"),
            P("shard", None),
            P("shard", None),
            P("shard", None),
            P("expert", None, None, "shard"),
            P("expert", "shard", None),
            P("shard", "expert", None),
        ),
        out_specs=(
            P("shard", "expert", None),
            P("shard", "expert", None),
            P(("expert", "shard")),
            P(("expert", "shard"), None),
            P(("expert", "shard"), None),
            P(("expert", "shard")),
            P(("expert", "shard"), None),
            P(("expert", "shard"), None),
            P(("expert", "shard")),
            P(("expert", "shard"), None),
            P(("expert", "shard"), None),
            P(("expert", "shard"), None),
            P("expert", None, None, "shard"),
            P("expert", "shard", None),
        ),
        check_vma=False,
    )
```

```python
import functools

import jax
import jax.numpy as jnp
from jax import lax
from jax.experimental import pallas as pl
from jax.experimental.pallas import tpu as pltpu
from jax.sharding import PartitionSpec as P

HEADS = 16
HEAD = 128
ROPE = 64
VHEAD = 128
RANK = 512
FF_S = 2816
SLOT = 2048

EPS = 1e-06
MASK_FILL = -1e30
BF = jnp.bfloat16
F32 = jnp.float32


def layout(lengths_slot, slot_index):
    first_len = lengths_slot[0]
    second_end = first_len + lengths_slot[1]
    segment = (slot_index >= first_len).astype(jnp.int32) + (slot_index >= second_end).astype(
        jnp.int32
    )
    seq_start = jnp.where(segment == 0, 0, jnp.where(segment == 1, first_len, second_end))
    return (segment, slot_index - seq_start, slot_index < second_end)


def rope_tables(positions):
    half_width = ROPE // 2
    inverse = 10000.0 ** (-jnp.arange(half_width, dtype=F32) / half_width)
    angles = positions.astype(F32)[:, None] * inverse[None, :]
    return (jnp.cos(angles), jnp.sin(angles))


def rotate(values, cosine, sine_table):
    half_width = values.shape[-1] // 2
    first_half = values[..., :half_width]
    second_half = values[..., half_width:]
    return jnp.concatenate(
        [
            first_half * cosine - second_half * sine_table,
            second_half * cosine + first_half * sine_table,
        ],
        -1,
    )


def rotate_back(grads_in, cosine, sine_table):
    return rotate(grads_in, cosine, -sine_table)


def silu_parts(gate_in):
    sigma = jax.nn.sigmoid(gate_in)
    return (gate_in * sigma, sigma * (1.0 + gate_in * (1.0 - sigma)))


def rms_scale(values):
    return lax.rsqrt(jnp.mean(values * values, -1, keepdims=True) + EPS)


def norm_back(grad_in, normed, inverse):
    return inverse * (grad_in - normed * jnp.mean(grad_in * normed, -1, keepdims=True))


def dot(left, right):
    return jnp.dot(left, right, preferred_element_type=F32)


def dot_t(left, right):
    return lax.dot_general(left, right, (((1,), (1,)), ((), ())), preferred_element_type=F32)


def t_dot(left, right):
    return lax.dot_general(left, right, (((0,), (0,)), ((), ())), preferred_element_type=F32)


def cross(values, bit):
    count = lax.axis_size("expert")
    return lax.ppermute(values, "expert", [(i, i ^ bit) for i in range(count)])


def swap(values):
    return lax.ppermute(values, "shard", [(0, 1), (1, 0)])


def whole_rows(weight):
    if lax.axis_size("shard") != 2:
        return lax.all_gather(weight, "shard", axis=0, tiled=True)
    other = swap(weight)
    first = lax.axis_index("shard") == 0
    return jnp.where(
        first, jnp.concatenate([weight, other], 0), jnp.concatenate([other, weight], 0)
    )


def row_blocks(weight):
    count = lax.axis_size("shard")
    if count == 2:
        own = lax.axis_index("shard")
        return [(own, weight), (1 - own, swap(weight))]
    blocks = lax.all_gather(weight, "shard", axis=0)
    return [(j, blocks[j]) for j in range(count)]


def times(values, blocks):
    rows = blocks[0][1].shape[0]
    return sum(
        dot(lax.dynamic_slice_in_dim(values, place * rows, rows, 1), block)
        for place, block in blocks
    )


def times_back(grads, blocks):
    pieces = [dot_t(grads, block) for _, block in blocks]
    if len(pieces) != 2:
        return jnp.concatenate(pieces, 1)
    first = lax.axis_index("shard") == 0
    return jnp.where(first, jnp.concatenate(pieces, 1), jnp.concatenate(pieces[::-1], 1))


def together(*values):
    leaves, tree = jax.tree.flatten(values)
    return jax.tree.unflatten(tree, lax.optimization_barrier(leaves))


def fold_order(bits):
    places = [0]
    for bit in reversed(bits):
        places = places + [place ^ bit for place in places]
    return places


def differing(blocks, bits, here):
    count = len(bits)
    blocks = blocks.reshape((2,) * count + blocks.shape[1:])
    ranked = sorted(bits, reverse=True)
    for k, bit in enumerate(ranked):
        blocks = jnp.where(here // bit % 2 == 1, jnp.flip(blocks, k), blocks)
    axes = [ranked.index(bit) for bit in bits]
    blocks = blocks.transpose(axes + list(range(count, blocks.ndim)))
    return blocks.reshape((1 << count,) + blocks.shape[count:])


def group_messages(own, crossed):
    if lax.axis_size("shard") != 2:
        both = lax.all_gather(jnp.concatenate([own, crossed], 0), "shard", axis=0, tiled=True)
        return [both]
    return [own, crossed, swap(own), swap(crossed)]


def product_kernel(rows, sources, order_ref, *refs):
    lefts, rights = refs[:sources], refs[sources : 2 * sources]
    kept_ref, sent_ref, picked_ref, turned_ref = refs[2 * sources :]
    count = order_ref.shape[0]
    padded = picked_ref.shape[0] // count

    @pl.when(pl.program_id(0) == 0)
    def _():
        start = 0
        for left_ref in lefts:
            tokens = left_ref.shape[0]
            turned_ref[:, start : start + tokens] = left_ref[...].astype(F32).T
            start += tokens
        if padded > rows:
            picked_ref[...] = jnp.zeros_like(picked_ref)
        for j in range(count):
            start = pl.multiple_of(order_ref[j] * rows, rows)
            picked_ref[j * padded : j * padded + rows, :] = turned_ref[
                pl.ds(start, rows), :
            ].astype(picked_ref.dtype)

    half = kept_ref.shape[0]
    right = jnp.concatenate([right_ref[...] for right_ref in rights], 0)
    kept_ref[...] = dot(picked_ref[:half, :].astype(BF), right).astype(kept_ref.dtype)
    sent_ref[...] = dot(picked_ref[half:, :].astype(BF), right).astype(sent_ref.dtype)


def product_halves(lefts, left_part, rights, right_part, bits):
    (left_start, left_columns), (start, columns) = left_part, right_part
    shards = lax.axis_size("shard")
    rows = left_columns // (lax.axis_size("expert") * shards)
    padded = -(-rows // 16) * 16
    order = (
        lax.axis_index("expert") ^ jnp.array(fold_order(bits), jnp.int32)
    ) * shards + lax.axis_index("shard")
    count = 1 << len(bits)
    half = count * padded // 2
    tokens = sum(left.shape[0] for left in lefts)
    if rows % 8:
        left = jnp.concatenate(
            [left[:, left_start : left_start + left_columns] for left in lefts], 0
        )
        right = jnp.concatenate([right[:, start : start + columns] for right in rights], 0)
        blocks = left.T.reshape(-1, shards, rows, tokens)
        blocks = lax.dynamic_index_in_dim(blocks, lax.axis_index("shard"), 1, keepdims=False)
        others = [bit for bit in (1, 2, 4, 8) if bit not in bits]
        picked = differing(blocks, (*others, *bits), lax.axis_index("expert"))[:count]
        picked = jnp.pad(picked, ((0, 0), (0, padded - rows), (0, 0))).reshape(-1, tokens)
        product = dot(picked, right).astype(BF)
        return product[:half], product[half:], picked
    tile = next(t for t in (512, 384, 256, 128) if columns % t == 0 and start % t == 0)
    return pl.pallas_call(
        functools.partial(product_kernel, rows, len(lefts)),
        grid_spec=pltpu.PrefetchScalarGridSpec(
            num_scalar_prefetch=1,
            grid=(columns // tile,),
            in_specs=[
                pl.BlockSpec(
                    (left.shape[0], left_columns),
                    lambda i, order: (0, left_start // left_columns),
                )
                for left in lefts
            ]
            + [
                pl.BlockSpec((right.shape[0], tile), lambda i, order: (0, i + start // tile))
                for right in rights
            ],
            out_specs=[
                pl.BlockSpec((half, tile), lambda i, order: (0, i)),
                pl.BlockSpec((half, tile), lambda i, order: (0, i)),
                pl.BlockSpec((count * padded, tokens), lambda i, order: (0, 0)),
            ],
            scratch_shapes=[pltpu.VMEM((left_columns, tokens), F32)],
        ),
        out_shape=[
            jax.ShapeDtypeStruct((half, columns), BF),
            jax.ShapeDtypeStruct((half, columns), BF),
            jax.ShapeDtypeStruct((count * padded, tokens), F32 if rows % 16 else BF),
        ],
        compiler_params=pltpu.CompilerParams(vmem_limit_bytes=56 << 20),
        cost_estimate=pl.CostEstimate(
            flops=4 * half * tokens * columns,
            bytes_accessed=4 * half * columns + 2 * tokens * (left_columns + columns),
            transcendentals=0,
        ),
    )(order.astype(jnp.int32), *lefts, *rights)


def pair_partial(partial, bits):
    experts, shards = lax.axis_size("expert"), lax.axis_size("shard")
    rows = partial.shape[0] // (experts * shards)
    if shards != 2:
        blocks = partial.reshape(experts, shards, rows, -1)
        total = lax.psum_scatter(blocks, "shard", scatter_dimension=1, tiled=True)[:, 0]
    else:
        own = lax.axis_index("shard")
        blocks = partial.reshape(experts, 2, rows, -1)
        kept = lax.dynamic_index_in_dim(blocks, own, 1, keepdims=False)
        sent = lax.dynamic_index_in_dim(blocks, 1 - own, 1, keepdims=False)
        total = (kept.astype(F32) + swap(sent).astype(F32)).astype(partial.dtype)
    return [differing(total, bits, lax.axis_index("expert")).reshape(experts * rows, -1)]


def line_places():
    return range(4, lax.axis_size("expert"), 4)


def partner(place):
    here = lax.axis_index("expert")
    there = here
    bit = 1
    while bit <= place:
        if place & bit:
            there = there + bit * (1 - 2 * (here // bit % 2))
        bit *= 2
    return there, lax.axis_index("shard")


def greet(places):
    barrier = pltpu.get_barrier_semaphore()
    for place in places:
        pl.semaphore_signal(
            barrier, inc=1, device_id=partner(place), device_id_type=pl.DeviceIdType.MESH
        )
    pl.semaphore_wait(barrier, len(places))


def slot_parts(rows):
    plane, line = (1, 2, 3), tuple(line_places())
    cut = rows // 4
    return (pl.ds(cut, rows - cut), line, plane), (pl.ds(0, cut), plane, line)


def gather_kernel(own_ref, out_ref, send_sems, recv_sems):
    parts = slot_parts(own_ref.shape[0])

    def send(k, rows, block, place):
        copy = pltpu.make_async_remote_copy(
            src_ref=out_ref.at[block, rows],
            dst_ref=out_ref.at[block ^ place, rows],
            send_sem=send_sems.at[k, block ^ place],
            recv_sem=recv_sems.at[k, block ^ place],
            device_id=partner(place),
            device_id_type=pl.DeviceIdType.MESH,
        )
        copy.start()
        return copy

    greet((1, 2, 3, *line_places()))
    out_ref[0] = own_ref[...]
    copies = {}
    for k, (rows, first, _) in enumerate(parts):
        for place in first:
            copies[k, place] = send(k, rows, 0, place)
    for k, (rows, _, second) in enumerate(parts):
        for place in second:
            copies[k, place] = send(k, rows, 0, place)
    arrived = set()
    for k in (1, 0):
        rows, first, second = parts[k]
        for block in first:
            copies[k, block].wait_recv()
            arrived.add((k, block))
            for place in second:
                copies[k, block ^ place] = send(k, rows, block, place)
    for key, copy in copies.items():
        copy.wait_send()
        if key not in arrived:
            copy.wait_recv()


def gather_slot(own):
    count = lax.axis_size("expert")
    return pl.pallas_call(
        gather_kernel,
        in_specs=[pl.BlockSpec(memory_space=pltpu.VMEM)],
        out_specs=pl.BlockSpec(memory_space=pltpu.VMEM),
        out_shape=jax.ShapeDtypeStruct((count, *own.shape), own.dtype),
        scratch_shapes=[pltpu.SemaphoreType.DMA((2, count)), pltpu.SemaphoreType.DMA((2, count))],
        compiler_params=pltpu.CompilerParams(
            collective_id=0, has_side_effects=True, vmem_limit_bytes=16 << 20
        ),
        cost_estimate=pl.CostEstimate(
            flops=5 * 10**10, bytes_accessed=4 * count * own.size, transcendentals=0
        ),
    )(own)


def scatter_kernel(part_ref, out_ref, *refs):
    parts = slot_parts(out_ref.shape[0])
    buffers = [refs[7 * k : 7 * k + 7] for k in range(2)]
    greet((1, 2, 3, *line_places()))
    copies = []

    def send(source, target, sems, index, place):
        copy = pltpu.make_async_remote_copy(
            src_ref=source,
            dst_ref=target,
            send_sem=sems[0].at[index],
            recv_sem=sems[1].at[index],
            device_id=partner(place),
            device_id_type=pl.DeviceIdType.MESH,
        )
        copy.start()
        copies.append(copy)
        return copy

    firsts = []
    for (rows, second, first), (first_ref, _, _, *sems) in zip(parts, buffers):
        firsts.append(
            [
                [
                    send(
                        part_ref.at[block ^ place, rows],
                        first_ref.at[k, i],
                        sems[:2],
                        (k, i),
                        place,
                    )
                    for i, place in enumerate(first)
                ]
                for k, block in enumerate((*second, 0))
            ]
        )
    lasts = {}
    for p in (1, 0):
        rows, second, _ = parts[p]
        first_ref, sum_ref, last_ref, *sems = buffers[p]
        for k, block in enumerate((*second, 0)):
            total = part_ref[block, rows, :].astype(F32)
            for i, copy in enumerate(firsts[p][k]):
                copy.wait_recv()
                total = total + first_ref[k, i].astype(F32)
            if block:
                sum_ref[k] = total.astype(sum_ref.dtype)
                lasts[p, k] = send(sum_ref.at[k], last_ref.at[k], sems[2:], k, block)
            else:
                out_ref[rows, :] = total
    for (p, k), copy in lasts.items():
        copy.wait_recv()
        out_ref[parts[p][0], :] += buffers[p][2][k].astype(F32)
    for copy in copies:
        copy.wait_send()


def scatter_slot(part):
    count, rows, columns = part.shape
    lines = count // 4
    cut = rows // 4
    scratch = []
    for height, groups, firsts in ((rows - cut, lines, 3), (cut, 4, lines - 1)):
        scratch += [
            pltpu.VMEM((groups, firsts, height, columns), part.dtype),
            pltpu.VMEM((groups - 1, height, columns), part.dtype),
            pltpu.VMEM((groups - 1, height, columns), part.dtype),
            pltpu.SemaphoreType.DMA((groups, firsts)),
            pltpu.SemaphoreType.DMA((groups, firsts)),
            pltpu.SemaphoreType.DMA((groups - 1,)),
            pltpu.SemaphoreType.DMA((groups - 1,)),
        ]
    return pl.pallas_call(
        scatter_kernel,
        in_specs=[pl.BlockSpec(memory_space=pltpu.VMEM)],
        out_specs=pl.BlockSpec(memory_space=pltpu.VMEM),
        out_shape=jax.ShapeDtypeStruct((rows, columns), F32),
        scratch_shapes=scratch,
        compiler_params=pltpu.CompilerParams(
            collective_id=1, has_side_effects=True, vmem_limit_bytes=24 << 20
        ),
        cost_estimate=pl.CostEstimate(
            flops=5 * 10**10, bytes_accessed=4 * part.size, transcendentals=0
        ),
    )(part)


REDUCE_STEPS = (1, 5, 3, 0, 7, 7, 4, 4, 3, 6, 2, 6, 0, 5, 7, 2,
                5, 2, 6, 7, 0, 3, 0, 4, 1, 2, 5, 3, 7, 1, 2)


def reduce_kernel(plans, steps, *refs):
    refs = list(refs)
    take = lambda count: [refs.pop(0) for _ in range(count)]
    pieces = [take(count) for _, count, _ in plans]
    firsts = [take(1)[0] if split else None for _, _, split in plans]
    outs = take(len(plans))
    sends = [[None if split and t == 0 else take(1)[0] for t in range(len(bits))] for bits, _, split in plans]
    arrivals = [take(len(bits)) for bits, _, _ in plans]
    send_sems, recv_sems = refs
    greet(sorted({bit for bits, _, _ in plans for bit in bits}))
    copies = []

    def add(target, parts, start, count):
        @pl.loop(0, count // 16)
        def _(k):
            here = pl.multiple_of(k * 16, 16)
            total = sum(part[pl.ds(start + here, 16), :].astype(F32) for part in parts)
            target[pl.ds(here, 16), :] = total.astype(target.dtype)

    latest = [None] * len(plans)
    done = [0] * len(plans)
    for g in steps:
        bits, _, split = plans[g]
        t = done[g]
        done[g] += 1
        if t:
            latest[g].wait_recv()
            pieces[g].append(arrivals[g][t - 1])
        if t == len(bits):
            add(outs[g], pieces[g], 0, outs[g].shape[0])
            continue
        count = arrivals[g][t].shape[0]
        source = firsts[g]
        if t or not split:
            source = sends[g][t]
            add(source, pieces[g], count, count)
        copy = pltpu.make_async_remote_copy(
            src_ref=source,
            dst_ref=arrivals[g][t],
            send_sem=send_sems.at[g, t],
            recv_sem=recv_sems.at[g, t],
            device_id=partner(bits[t]),
            device_id_type=pl.DeviceIdType.MESH,
        )
        copy.start()
        copies.append(copy)
        latest[g] = copy
    for copy in copies:
        copy.wait_send()


def reduce_all(groups, steps):
    plans = tuple((bits, len(pieces), first is not None) for bits, pieces, first in groups)
    outs, sends, arrivals = [], [], []
    for bits, pieces, first in groups:
        count, columns = pieces[0].shape
        count = count * (1 if first is None else 2)
        for t in range(len(bits)):
            count = count // 2
            arrivals.append(pltpu.VMEM((count, columns), BF))
            if t or first is None:
                sends.append(pltpu.VMEM((count, columns), BF))
        outs.append(jax.ShapeDtypeStruct((count, columns), F32))
    operands = [piece for _, pieces, _ in groups for piece in pieces]
    operands += [first for _, _, first in groups if first is not None]
    most = max(len(bits) for bits, _, _ in groups)
    in_vmem = pl.BlockSpec(memory_space=pltpu.VMEM)
    return pl.pallas_call(
        functools.partial(reduce_kernel, plans, steps),
        in_specs=[in_vmem] * len(operands),
        out_specs=[in_vmem] * len(outs),
        out_shape=outs,
        scratch_shapes=[
            *sends,
            *arrivals,
            pltpu.SemaphoreType.DMA((len(groups), most)),
            pltpu.SemaphoreType.DMA((len(groups), most)),
        ],
        compiler_params=pltpu.CompilerParams(
            collective_id=2, has_side_effects=True, vmem_limit_bytes=58 << 20
        ),
        cost_estimate=pl.CostEstimate(
            flops=10**11,
            bytes_accessed=4 * sum(operand.size for operand in operands),
            transcendentals=0,
        ),
    )(*operands)


def attend_kernel(
    raw_ref, cosine_ref, sine_ref, expand_ref, keys_ref, bias_ref,
    nope_ref, queries_ref, weights_ref, mixed_ref, out_ref,
):
    rows = raw_ref.shape[0]
    width = HEAD + ROPE
    cosine, sine = cosine_ref[...], sine_ref[...]
    for h in range(2):
        raw = raw_ref[:, h * width : (h + 1) * width]
        nope = raw[:, :HEAD].astype(BF)
        first = raw[:, HEAD : HEAD + ROPE // 2]
        second = raw[:, HEAD + ROPE // 2 :]
        turned = jnp.concatenate(
            [first * cosine - second * sine, second * cosine + first * sine], -1
        )
        nope_ref[:, h * HEAD : (h + 1) * HEAD] = nope
        latent = dot_t(nope, expand_ref[:, 2 * h * HEAD : (2 * h + 1) * HEAD])
        queries_ref[h * rows : (h + 1) * rows, :RANK] = latent.astype(BF)
        queries_ref[h * rows : (h + 1) * rows, RANK:] = turned.astype(BF)
    bias = bias_ref[...]
    for h in range(2):
        part = slice(h * rows, (h + 1) * rows)
        scores = dot_t(queries_ref[part, :], keys_ref[...]) * (HEAD + ROPE) ** -0.5 + bias
        shifted = jnp.exp(scores - jnp.max(scores, -1, keepdims=True))
        total = jnp.sum(shifted, -1, keepdims=True)
        weights_ref[part, :] = (shifted * (1.0 / total)).astype(BF)
    mixed_ref[...] = dot(weights_ref[...], keys_ref[:, :RANK]).astype(BF)
    for h in range(2):
        out_ref[:, h * VHEAD : (h + 1) * VHEAD] = dot(
            mixed_ref[h * rows : (h + 1) * rows, :],
            expand_ref[:, (2 * h + 1) * HEAD : (2 * h + 2) * HEAD],
        ).astype(BF)


def attend(query_raw, cosine, sine, expand, keys, bias):
    rows, slot = bias.shape
    steps = HEADS // 2
    whole = lambda *shape: pl.BlockSpec(shape, lambda i: (0,) * len(shape))
    return pl.pallas_call(
        attend_kernel,
        grid=(steps,),
        in_specs=[
            pl.BlockSpec((rows, 2 * (HEAD + ROPE)), lambda i: (0, i)),
            whole(rows, ROPE // 2),
            whole(rows, ROPE // 2),
            pl.BlockSpec((RANK, 4 * HEAD), lambda i: (0, i)),
            whole(slot, RANK + ROPE),
            whole(rows, slot),
        ],
        out_specs=[
            pl.BlockSpec((rows, 2 * HEAD), lambda i: (0, i)),
            pl.BlockSpec((2 * rows, RANK + ROPE), lambda i: (i, 0)),
            pl.BlockSpec((2 * rows, slot), lambda i: (i, 0)),
            pl.BlockSpec((2 * rows, RANK), lambda i: (i, 0)),
            pl.BlockSpec((rows, 2 * VHEAD), lambda i: (0, i)),
        ],
        out_shape=[
            jax.ShapeDtypeStruct((rows, HEADS * HEAD), BF),
            jax.ShapeDtypeStruct((HEADS * rows, RANK + ROPE), BF),
            jax.ShapeDtypeStruct((HEADS * rows, slot), BF),
            jax.ShapeDtypeStruct((HEADS * rows, RANK), BF),
            jax.ShapeDtypeStruct((rows, HEADS * VHEAD), BF),
        ],
        compiler_params=pltpu.CompilerParams(vmem_limit_bytes=40 << 20),
        cost_estimate=pl.CostEstimate(
            flops=2 * HEADS * rows * slot * (2 * RANK + ROPE),
            bytes_accessed=2 * HEADS * rows * slot,
            transcendentals=HEADS * rows * slot,
        ),
    )(query_raw, cosine, sine, expand, keys, bias)


def attend_back_kernel(
    order_ref, grad_ref, expand_ref, keys_ref, weights_ref, queries_ref, mixed_ref, nope_ref, cosine_ref,
    sine_ref, query_grad_ref, expand_grad_ref, key_out_ref, key_grad_ref, latent_ref, scores_ref,
):
    rows = grad_ref.shape[0]
    width = HEAD + ROPE
    scale = (HEAD + ROPE) ** -0.5

    @pl.when(pl.program_id(0) == 0)
    def _():
        key_grad_ref[...] = jnp.zeros_like(key_grad_ref)

    for h in range(2):
        part = slice(h * rows, (h + 1) * rows)
        grad = grad_ref[:, h * VHEAD : (h + 1) * VHEAD]
        latent_ref[part, :] = dot_t(
            grad, expand_ref[:, (2 * h + 1) * HEAD : (2 * h + 2) * HEAD]
        ).astype(BF)
        arrived = dot_t(latent_ref[part, :], keys_ref[:, :RANK])
        weights = weights_ref[part, :].astype(F32)
        mean = jnp.sum(weights * arrived, -1, keepdims=True)
        scores_ref[part, :] = (weights * (arrived - mean) * scale).astype(BF)
    key_grad_ref[...] += t_dot(queries_ref[...], scores_ref[...])
    key_grad_ref[:RANK, :] += t_dot(latent_ref[...], weights_ref[...])
    cosine, sine = cosine_ref[...], sine_ref[...]
    for h in range(2):
        part = slice(h * rows, (h + 1) * rows)
        query_grad = dot(scores_ref[part, :], keys_ref[...])
        latent = query_grad[:, :RANK].astype(BF)
        key_part = slice(2 * h * HEAD, (2 * h + 1) * HEAD)
        value_part = slice((2 * h + 1) * HEAD, (2 * h + 2) * HEAD)
        nope = dot(latent, expand_ref[:, key_part])
        first = query_grad[:, RANK : RANK + ROPE // 2]
        second = query_grad[:, RANK + ROPE // 2 :]
        query_grad_ref[:, h * width : (h + 1) * width] = jnp.concatenate(
            [nope, first * cosine + second * sine, second * cosine - first * sine], -1
        ).astype(BF)
        key_grad = t_dot(latent, nope_ref[:, h * HEAD : (h + 1) * HEAD]).astype(BF)
        value_grad = t_dot(
            mixed_ref[part, :], grad_ref[:, h * VHEAD : (h + 1) * VHEAD]
        ).astype(BF)
        count = order_ref.shape[0]
        height = RANK // count
        for j in range(count):
            target = pl.ds(pl.multiple_of(order_ref[j] * height, height), height)
            source = slice(j * height, (j + 1) * height)
            expand_grad_ref[target, key_part] = key_grad[source, :]
            expand_grad_ref[target, value_part] = value_grad[source, :]

    @pl.when(pl.program_id(0) == pl.num_programs(0) - 1)
    def _():
        key_out_ref[...] = key_grad_ref[...].T.astype(BF)


def attend_back(grad_out, expand, keys, weights, queries, mixed, nope, cosine, sine, order):
    rows = grad_out.shape[0]
    slot = keys.shape[0]
    whole = lambda *shape: pl.BlockSpec(shape, lambda i, order: (0,) * len(shape))
    return pl.pallas_call(
        attend_back_kernel,
        grid_spec=pltpu.PrefetchScalarGridSpec(
            num_scalar_prefetch=1,
            grid=(HEADS // 2,),
            in_specs=[
            pl.BlockSpec((rows, 2 * VHEAD), lambda i, order: (0, i)),
            pl.BlockSpec((RANK, 4 * HEAD), lambda i, order: (0, i)),
            whole(slot, RANK + ROPE),
            pl.BlockSpec((2 * rows, slot), lambda i, order: (i, 0)),
            pl.BlockSpec((2 * rows, RANK + ROPE), lambda i, order: (i, 0)),
            pl.BlockSpec((2 * rows, RANK), lambda i, order: (i, 0)),
            pl.BlockSpec((rows, 2 * HEAD), lambda i, order: (0, i)),
            whole(rows, ROPE // 2),
            whole(rows, ROPE // 2),
        ],
        out_specs=[
            pl.BlockSpec((rows, 2 * (HEAD + ROPE)), lambda i, order: (0, i)),
            pl.BlockSpec((RANK, 4 * HEAD), lambda i, order: (0, i)),
            whole(slot, RANK + ROPE),
        ],
        scratch_shapes=[
            pltpu.VMEM((RANK + ROPE, slot), F32),
            pltpu.VMEM((2 * rows, RANK), BF),
            pltpu.VMEM((2 * rows, slot), BF),
        ],
        ),
        out_shape=[
            jax.ShapeDtypeStruct((rows, HEADS * (HEAD + ROPE)), BF),
            jax.ShapeDtypeStruct((RANK, 2 * HEADS * HEAD), BF),
            jax.ShapeDtypeStruct((slot, RANK + ROPE), BF),
        ],
        compiler_params=pltpu.CompilerParams(vmem_limit_bytes=48 << 20),
        cost_estimate=pl.CostEstimate(
            flops=2 * HEADS * rows * slot * (3 * RANK + 2 * (RANK + ROPE)),
            bytes_accessed=2 * HEADS * rows * slot,
            transcendentals=0,
        ),
    )(order, grad_out, expand, keys, weights, queries, mixed, nope, cosine, sine)


def expert_kernel(sources, here_ref, rows_ref, grads_ref, router_ref, *refs):
    weights = refs[: 2 * sources]
    (
        row_grad_ref, units_ref, back_ref, gate_ref, logit_grad_ref, total_ref, probs_ref, share_ref,
    ) = refs[2 * sources :]
    step = pl.program_id(0)
    chunks = pl.num_programs(0) // sources

    @pl.when(step == 0)
    def _():
        logits = dot_t(router_ref[...], rows_ref[...])
        powers = jnp.exp(logits - jnp.max(logits, 0, keepdims=True))
        probs = powers / jnp.sum(powers, 0, keepdims=True)
        own = lax.broadcasted_iota(jnp.int32, probs.shape, 0) == here_ref[0]
        probs_ref[...] = probs
        gate_ref[...] = jnp.sum(jnp.where(own, probs, 0.0), 0, keepdims=True)
        share_ref[...] = jnp.zeros_like(share_ref)
        total_ref[...] = jnp.zeros_like(total_ref)

    def work(in_ref, out_ref):
        gate = dot_t(in_ref[0], rows_ref[...])
        up = dot_t(in_ref[1], rows_ref[...])
        back = dot_t(out_ref[...], grads_ref[...])
        sigma = 1.0 / (1.0 + jnp.exp(-gate))
        act = gate * sigma
        units = (act * up).astype(BF)
        units_ref[...] = units
        share_ref[...] += jnp.sum(back * units.astype(F32), 0, keepdims=True)
        back = back * gate_ref[...]
        back_ref[0] = (back * up * (sigma * (1.0 + gate * (1.0 - sigma)))).astype(BF)
        back_ref[1] = (back * act).astype(BF)
        total_ref[...] += t_dot(back_ref[0], in_ref[0])
        total_ref[...] += t_dot(back_ref[1], in_ref[1])

    for k in range(sources):

        @pl.when(step // chunks == k)
        def _(k=k):
            work(weights[2 * k], weights[2 * k + 1])

    @pl.when(step == pl.num_programs(0) - 1)
    def _():
        probs = probs_ref[...]
        own = lax.broadcasted_iota(jnp.int32, probs.shape, 0) == here_ref[0]
        grad = probs * (own.astype(F32) - gate_ref[...]) * share_ref[...]
        logit_grad_ref[...] = grad.astype(BF)
        row_grad_ref[...] = (
            total_ref[...] + t_dot(logit_grad_ref[...], router_ref[...])
        ).astype(BF)


def expert_pass(here, rows, grads, router, weights):
    count, width = rows.shape
    experts = router.shape[0]
    sources = len(weights)
    units = weights[0][1].shape[0]
    tile = next(t for t in (352, 176, 88, 64, 32, 16, units) if units % t == 0)
    chunks = units // tile
    once = pl.Buffered(1)
    in_specs = [
        pl.BlockSpec((count, width), lambda i, h: (0, 0), pipeline_mode=once),
        pl.BlockSpec((count, width), lambda i, h: (0, 0), pipeline_mode=once),
        pl.BlockSpec((experts, width), lambda i, h: (0, 0)),
    ]
    for k in range(sources):
        at = lambda i, k=k: jnp.clip(i - k * chunks, 0, chunks - 1)
        in_specs.append(pl.BlockSpec((2, tile, width), lambda i, h, at=at: (0, at(i), 0)))
        in_specs.append(pl.BlockSpec((tile, width), lambda i, h, at=at: (at(i), 0)))
    return pl.pallas_call(
        functools.partial(expert_kernel, sources),
        grid_spec=pltpu.PrefetchScalarGridSpec(
            num_scalar_prefetch=1,
            grid=(sources * chunks,),
            in_specs=in_specs,
            out_specs=[
                pl.BlockSpec((count, width), lambda i, h: (0, 0), pipeline_mode=once),
                pl.BlockSpec((tile, count), lambda i, h: (i, 0)),
                pl.BlockSpec(
                    (None, 2, tile, count), lambda i, h: (i // chunks, 0, i % chunks, 0)
                ),
                pl.BlockSpec((1, count), lambda i, h: (0, 0)),
                pl.BlockSpec((experts, count), lambda i, h: (0, 0)),
            ],
            scratch_shapes=[
                pltpu.VMEM((count, width), F32),
                pltpu.VMEM((experts, count), F32),
                pltpu.VMEM((1, count), F32),
            ],
        ),
        out_shape=[
            jax.ShapeDtypeStruct((count, width), BF),
            jax.ShapeDtypeStruct((sources * units, count), BF),
            jax.ShapeDtypeStruct((sources, 2, units, count), BF),
            jax.ShapeDtypeStruct((1, count), F32),
            jax.ShapeDtypeStruct((experts, count), BF),
        ],
        compiler_params=pltpu.CompilerParams(vmem_limit_bytes=58 << 20),
        cost_estimate=pl.CostEstimate(
            flops=10 * count * width * sources * units,
            bytes_accessed=6 * (count + sources * units) * width,
            transcendentals=count * sources * units,
        ),
    )(here, rows, grads, router, *[piece for pair in weights for piece in pair])


def per_device(
    tokens,
    lengths,
    routes,
    attn_gain,
    query_weight,
    latent_weight,
    latent_gain,
    expand_weight,
    output_weight,
    ffn_gain,
    router_weight,
    shared_in,
    shared_out,
    expert_in,
    expert_out,
    cotangent,
):
    local_rows = tokens.shape[1]
    model_width = tokens.shape[2]
    owners, shards = lax.axis_size("expert"), lax.axis_size("shard")
    experts_all = router_weight.shape[1]
    assert experts_all == owners
    topk_count = routes.shape[2]
    capacity = max(2, 9 * local_rows * topk_count // (8 * experts_all))
    capacity = -(-capacity // 8) * 8
    here = lax.axis_index("expert")

    query_blocks = row_blocks(query_weight)
    latent_blocks = row_blocks(latent_weight)
    gains = jnp.concatenate([attn_gain, ffn_gain, latent_gain])[None]
    gains = (
        jnp.where(
            lax.axis_index("shard") == 0,
            jnp.concatenate([gains, swap(gains)], 0),
            jnp.concatenate([swap(gains), gains], 0),
        )
        if shards == 2
        else lax.all_gather(gains, "shard", axis=0, tiled=True)
    ).astype(F32)
    cut = attn_gain.shape[0]
    gain_attn = gains[:, :cut].reshape(-1)
    gain_ffn = gains[:, cut : 2 * cut].reshape(-1)
    gain_latent = gains[:, 2 * cut :].reshape(-1)
    expand = whole_rows(expand_weight)
    here_index = here * local_rows + jnp.arange(local_rows, dtype=jnp.int32)
    query_segment, query_position, query_valid = layout(lengths[0], here_index)
    cosine, sine_table = rope_tables(query_position)
    live_rows = query_valid.astype(F32)[:, None]
    grad_out = cotangent[0].astype(F32) * live_rows
    grad_out_low = grad_out.astype(BF)

    expert_ids = jnp.arange(experts_all, dtype=jnp.int32)
    member = jnp.any(routes[0].T[None] == expert_ids[:, None, None], 1)
    token_ids = jnp.arange(local_rows, dtype=jnp.int32)
    earlier = (token_ids[:, None] < token_ids[None, :]).astype(BF)
    rank = dot(member.astype(BF), earlier).astype(jnp.int32)
    place_ids = jnp.arange(capacity, dtype=jnp.int32)
    spread = (
        (member[:, None, :] & (rank[:, None, :] == place_ids[None, :, None]))
        .reshape(experts_all * capacity, local_rows)
        .astype(BF)
    )

    def exchange(rows):
        return lax.all_to_all(
            rows.reshape(owners, capacity, model_width),
            "expert",
            split_axis=0,
            concat_axis=0,
            tiled=True,
        ).reshape(owners * capacity, model_width)


    inputs = tokens[0].astype(F32)
    inverse_attn = rms_scale(inputs)
    normed_attn = inputs * inverse_attn
    attn_in = (normed_attn * gain_attn).astype(BF)
    latent_raw = times(attn_in, latent_blocks)
    latent = latent_raw[:, :RANK]
    inverse_latent = rms_scale(latent)
    normed_latent = latent * inverse_latent
    latent_in = (normed_latent * gain_latent).astype(BF)
    key_rope = rotate(latent_raw[:, RANK:], cosine, sine_table).astype(BF)
    own_keys = jnp.concatenate([latent_in, key_rope], -1)
    expert_in_rows, expert_out_rows = expert_in[0].transpose(1, 2, 0), expert_out[0]
    (
        own_keys, output_weight, router_weight, shared_in, shared_out, expert_in_rows, expert_out_rows,
    ) = together(
        own_keys, output_weight, router_weight, shared_in, shared_out, expert_in_rows, expert_out_rows,
    )
    output_blocks = row_blocks(output_weight)
    router = whole_rows(router_weight)
    shared_out_blocks = row_blocks(shared_out)
    shared_in_blocks = row_blocks(shared_in)
    if shards == 2:
        expert_weights = [
            (expert_in_rows, expert_out_rows),
            (swap(expert_in_rows), swap(expert_out_rows)),
        ]
    else:
        expert_weights = [
            (
                lax.all_gather(expert_in_rows, "shard", axis=1, tiled=True),
                lax.all_gather(expert_out_rows, "shard", axis=0, tiled=True),
            )
        ]

    sent_grads = dot(spread, grad_out_low).astype(BF)
    keys, sent_grads = together(gather_slot(own_keys), sent_grads)
    received_grads = exchange(sent_grads)
    keys = keys.reshape(-1, RANK + ROPE)
    key_index = (
        (here ^ jnp.arange(owners, dtype=jnp.int32))[:, None] * local_rows
        + jnp.arange(local_rows, dtype=jnp.int32)[None, :]
    ).reshape(-1)

    query_raw = times(attn_in, query_blocks)
    key_segment = layout(lengths[0], key_index)[0]
    allowed = (query_segment[:, None] == key_segment[None, :]) & (
        key_index[None, :] <= here_index[:, None]
    )
    bias = jnp.where(allowed, 0.0, MASK_FILL).astype(F32)
    query_nope, queries, attention, mixed_latent, mixed_heads = attend(
        query_raw, cosine, sine_table, expand, keys, bias
    )
    (
        mixed_heads, received_grads, output_blocks, router, shared_in_blocks, shared_out_blocks,
        expert_weights,
    ) = together(
        mixed_heads, received_grads, output_blocks, router, shared_in_blocks, shared_out_blocks,
        expert_weights,
    )
    hidden_state = inputs + times(mixed_heads, output_blocks)
    inverse_ffn = rms_scale(hidden_state)
    normed_ffn = hidden_state * inverse_ffn
    ffn_in = (normed_ffn * gain_ffn).astype(BF)

    received = exchange(dot(spread, ffn_in).astype(BF))
    shared_both = times(ffn_in, shared_in_blocks)
    shared_act, shared_slope = silu_parts(shared_both[:, :FF_S])
    shared_up = shared_both[:, FF_S:]
    shared_hidden = (shared_act * shared_up).astype(BF)
    shared_result = times(shared_hidden, shared_out_blocks)
    grad_shared_hidden = times_back(grad_out_low, shared_out_blocks)
    grad_shared_gate = (grad_shared_hidden * shared_up * shared_slope).astype(BF)
    grad_shared_up = (grad_shared_hidden * shared_act).astype(BF)
    grad_ffn_in = times_back(
        jnp.concatenate([grad_shared_gate, grad_shared_up], -1), shared_in_blocks
    )
    out_message = jnp.concatenate([shared_hidden, grad_out_low], 1)
    in_message = jnp.concatenate([ffn_in, grad_shared_gate, grad_shared_up], 1)
    received, shared_result, grad_ffn_in, out_message, in_message = together(
        received, shared_result, grad_ffn_in, out_message, in_message
    )

    early_message = jnp.concatenate([attn_in, mixed_heads], 1)
    received, early_message = together(received, early_message)
    arrived = cross(out_message, 1), cross(in_message, 4), cross(early_message, 2)
    expert_results = expert_pass(
        here[None], received, received_grads, router.T, expert_weights
    )
    row_grads, hidden, hidden_grads, row_gate, row_grad_logits = expert_results

    returned_grads = exchange(row_grads)
    units = expert_weights[0][1].shape[0]
    row_gate = row_gate.reshape(-1, 1)
    weighted_grads = (row_gate * received_grads.astype(F32)).astype(BF)

    def expert_grads(j):
        return (
            dot(hidden_grads[j].reshape(2 * units, -1), received).reshape(2, units, -1),
            dot(hidden[j * units : (j + 1) * units], weighted_grads),
        )

    other_parts = [part.astype(BF) for part in expert_grads(len(expert_weights) - 1)]
    other_parts, arrived = together(other_parts, arrived)
    out_messages = group_messages(out_message, arrived[0])
    in_messages = group_messages(in_message, arrived[1])
    early_messages = group_messages(early_message, arrived[2])
    cut = 4096
    shared_halves = [
        product_halves(messages, left_part, messages, right_part, order)[:2]
        for messages, left_part, right_part, order in (
            (out_messages, (0, FF_S), (FF_S, model_width), (2, 8, 4)),
            (in_messages, (0, model_width), (model_width, cut), (1, 2, 8)),
            (in_messages, (0, model_width), (model_width + cut, 2 * FF_S - cut), (2, 1, 8)),
        )
    ]
    hidden, hidden_grads, shared_halves, early_messages = together(
        hidden, hidden_grads, shared_halves, early_messages
    )
    shared_sums = [
        [kept, cross(sent, bit)] for (kept, sent), bit in zip(shared_halves, (2, 1, 2))
    ]
    row_out = 0.0
    for j, (_, weight) in enumerate(expert_weights):
        row_out = row_out + t_dot(hidden[j * units : (j + 1) * units], weight)
    row_out = (row_gate * row_out).astype(BF)
    if shards == 2:
        hidden, hidden_grads, other_parts = together(
            hidden, hidden_grads, [swap(part) for part in other_parts]
        )
        grad_expert_in, grad_expert_out = [
            own + other.astype(F32) for own, other in zip(expert_grads(0), other_parts)
        ]
    else:
        grad_expert_in, grad_expert_out = [
            lax.psum_scatter(part, "shard", scatter_dimension=part.ndim - 2, tiled=True).astype(F32)
            for part in other_parts
        ]
    grad_router = dot(row_grad_logits, received)
    returned_grads, row_out, grad_expert_in, grad_expert_out, grad_router = together(
        returned_grads, row_out, grad_expert_in, grad_expert_out, grad_router
    )
    grad_expert_in = grad_expert_in.transpose(2, 0, 1)[None]
    grad_expert_out = grad_expert_out[None]
    returned = exchange(row_out)
    grad_ffn_in = grad_ffn_in + t_dot(spread, returned_grads)
    grad_gain_ffn = jnp.sum(grad_ffn_in * normed_ffn, 0)
    grad_hidden_state = grad_out + norm_back(grad_ffn_in * gain_ffn, normed_ffn, inverse_ffn)

    grad_attn_out = grad_hidden_state.astype(BF)
    grad_mixed = times_back(grad_attn_out, output_blocks).astype(BF)
    grad_mixed, grad_attn_out = together(grad_mixed, grad_attn_out)
    out_arrived = cross(grad_attn_out, 2)
    expand_order = (2, 1, 4, 8)
    if shards == 2:
        differs = here ^ jnp.arange(owners, dtype=jnp.int32)
        place = sum((differs // bit % 2) << (3 - k) for k, bit in enumerate(expand_order))
        other = lax.axis_index("shard") ^ jnp.arange(2, dtype=jnp.int32)
        block_order = (other[None, :] * owners + place[:, None]).reshape(-1).astype(jnp.int32)
    else:
        block_order = jnp.zeros((1,), jnp.int32)
    attention_grads = attend_back(
        grad_mixed,
        expand,
        keys,
        attention,
        queries,
        mixed_latent,
        query_nope,
        cosine,
        sine_table,
        block_order,
    )
    attention_grads, shared_sums, out_arrived = together(
        attention_grads, shared_sums, out_arrived
    )
    grad_query_raw, grad_expand, grad_keys = attention_grads

    query_arrived = cross(grad_query_raw, 2)
    own_query = grad_query_raw
    if shards == 2:
        half_rank = RANK // 2
        expand_pair = [grad_expand[:half_rank], swap(grad_expand[half_rank:])]
    else:
        expand_pair = pair_partial(grad_expand, expand_order)
    grad_own_keys, returned, query_arrived, grad_query_raw, expand_pair = together(
        scatter_slot(grad_keys.reshape(owners, local_rows, -1)),
        returned,
        query_arrived,
        grad_query_raw,
        expand_pair,
    )
    grad_latent_in = grad_own_keys[:, :RANK]
    grad_gain_latent = jnp.sum(grad_latent_in * normed_latent, 0)
    grad_latent = norm_back(grad_latent_in * gain_latent, normed_latent, inverse_latent)
    grad_latent_raw = jnp.concatenate(
        [grad_latent, rotate_back(grad_own_keys[:, RANK:], cosine, sine_table)], -1
    ).astype(BF)
    latent_message = jnp.pad(grad_latent_raw, ((0, 0), (0, -grad_latent_raw.shape[1] % 128)))
    latent_messages = group_messages(latent_message, cross(latent_message, 2))
    query_messages = group_messages(own_query, query_arrived)
    out_messages = group_messages(grad_attn_out, out_arrived)
    in_part, heads_part = (0, model_width), (model_width, HEADS * VHEAD)
    whole_part = lambda array: (0, array.shape[1])
    *query_halves, picked = product_halves(
        early_messages, in_part, query_messages, whole_part(grad_query_raw), (1, 4, 8)
    )
    output_halves = product_halves(
        early_messages, heads_part, out_messages, whole_part(grad_attn_out), (4, 1, 8)
    )[:2]
    latent_product = dot(picked, jnp.concatenate(latent_messages, 0)).astype(BF)
    latent_halves = jnp.split(latent_product, 2, 0)
    grad_attn_in = times_back(grad_latent_raw, latent_blocks) + times_back(
        grad_query_raw, query_blocks
    )
    grad_gain_attn = jnp.sum(grad_attn_in * normed_attn, 0)
    tokens_grad = grad_hidden_state + norm_back(grad_attn_in * gain_attn, normed_attn, inverse_attn)
    devices = owners * shards
    rows = model_width // devices
    small = jnp.concatenate(
        [
            vector.reshape(devices, -1)
            for vector in (grad_router.T, grad_gain_attn, grad_gain_ffn, grad_gain_latent)
        ],
        1,
    )
    cuts = [rows * experts_all, rows * (experts_all + 1), rows * (experts_all + 2)]
    small = jnp.pad(small, ((0, 0), (0, -small.shape[1] % 2048))).reshape(devices * 16, -1)
    small_pair = pair_partial(small.astype(BF), expand_order)
    sums = reduce_all(
        [
            ((1, 4, 8), [latent_halves[0]], latent_halves[1]),
            ((8, 4), shared_sums[0], None),
            (expand_order, expand_pair, None),
            ((1, 4, 8), [query_halves[0]], query_halves[1]),
            ((2, 8), shared_sums[1], None),
            ((4, 1, 8), [output_halves[0]], output_halves[1]),
            ((1, 8), shared_sums[2], None),
            (expand_order, small_pair, None),
        ],
        REDUCE_STEPS,
    )
    grad_latent_weight = sums[0][:, : RANK + ROPE]
    grad_shared_out = sums[1][: FF_S // devices]
    grad_expand, grad_query = sums[2:4]
    grad_shared_in = jnp.concatenate([sums[4], sums[6]], 1)
    grad_output = sums[5]
    small = sums[7].reshape(-1)
    routed = t_dot(spread, returned)
    block_result = hidden_state + shared_result + routed
    return (
        block_result.astype(BF)[None],
        tokens_grad.astype(BF)[None],
        small[cuts[0] : cuts[1]],
        grad_query,
        grad_latent_weight,
        small[cuts[2] : cuts[2] + RANK // devices],
        grad_expand,
        grad_output,
        small[cuts[1] : cuts[2]],
        small[: cuts[0]].reshape(rows, experts_all),
        grad_shared_in,
        grad_shared_out,
        grad_expert_in,
        grad_expert_out,
    )


def solution(mesh):
    return jax.shard_map(
        per_device,
        mesh=mesh,
        in_specs=(
            P("shard", "expert", None),
            P("shard", None),
            P("shard", "expert", None),
            P("shard"),
            P("shard", None),
            P("shard", None),
            P("shard"),
            P("shard", None),
            P("shard", None),
            P("shard"),
            P("shard", None),
            P("shard", None),
            P("shard", None),
            P("expert", None, None, "shard"),
            P("expert", "shard", None),
            P("shard", "expert", None),
        ),
        out_specs=(
            P("shard", "expert", None),
            P("shard", "expert", None),
            P(("expert", "shard")),
            P(("expert", "shard"), None),
            P(("expert", "shard"), None),
            P(("expert", "shard")),
            P(("expert", "shard"), None),
            P(("expert", "shard"), None),
            P(("expert", "shard")),
            P(("expert", "shard"), None),
            P(("expert", "shard"), None),
            P(("expert", "shard"), None),
            P("expert", None, None, "shard"),
            P("expert", "shard", None),
        ),
        check_vma=False,
    )
```

```python
import functools

import jax
import jax.numpy as jnp
from jax import lax
from jax.experimental import pallas as pl
from jax.experimental.pallas import tpu as pltpu
from jax.sharding import PartitionSpec as P

HEADS = 16
HEAD = 128
ROPE = 64
VHEAD = 128
RANK = 512
FF_S = 2816
SLOT = 2048

EPS = 1e-06
MASK_FILL = -1e30
BF = jnp.bfloat16
F32 = jnp.float32


def layout(lengths_slot, slot_index):
    first_len = lengths_slot[0]
    second_end = first_len + lengths_slot[1]
    segment = (slot_index >= first_len).astype(jnp.int32) + (slot_index >= second_end).astype(
        jnp.int32
    )
    seq_start = jnp.where(segment == 0, 0, jnp.where(segment == 1, first_len, second_end))
    return (segment, slot_index - seq_start, slot_index < second_end)


def rope_tables(positions):
    half_width = ROPE // 2
    inverse = 10000.0 ** (-jnp.arange(half_width, dtype=F32) / half_width)
    angles = positions.astype(F32)[:, None] * inverse[None, :]
    return (jnp.cos(angles), jnp.sin(angles))


def rotate(values, cosine, sine_table):
    half_width = values.shape[-1] // 2
    first_half = values[..., :half_width]
    second_half = values[..., half_width:]
    return jnp.concatenate(
        [
            first_half * cosine - second_half * sine_table,
            second_half * cosine + first_half * sine_table,
        ],
        -1,
    )


def rotate_back(grads_in, cosine, sine_table):
    return rotate(grads_in, cosine, -sine_table)


def silu_parts(gate_in):
    sigma = jax.nn.sigmoid(gate_in)
    return (gate_in * sigma, sigma * (1.0 + gate_in * (1.0 - sigma)))


def rms_scale(values):
    return lax.rsqrt(jnp.mean(values * values, -1, keepdims=True) + EPS)


def norm_back(grad_in, normed, inverse):
    return inverse * (grad_in - normed * jnp.mean(grad_in * normed, -1, keepdims=True))


def dot(left, right):
    return jnp.dot(left, right, preferred_element_type=F32)


def dot_t(left, right):
    return lax.dot_general(left, right, (((1,), (1,)), ((), ())), preferred_element_type=F32)


def t_dot(left, right):
    return lax.dot_general(left, right, (((0,), (0,)), ((), ())), preferred_element_type=F32)


def cross(values, bit):
    count = lax.axis_size("expert")
    return lax.ppermute(values, "expert", [(i, i ^ bit) for i in range(count)])


def swap(values):
    return lax.ppermute(values, "shard", [(0, 1), (1, 0)])


def whole_rows(weight):
    if lax.axis_size("shard") != 2:
        return lax.all_gather(weight, "shard", axis=0, tiled=True)
    other = swap(weight)
    first = lax.axis_index("shard") == 0
    return jnp.where(
        first, jnp.concatenate([weight, other], 0), jnp.concatenate([other, weight], 0)
    )


def row_blocks(weight):
    count = lax.axis_size("shard")
    if count == 2:
        own = lax.axis_index("shard")
        return [(own, weight), (1 - own, swap(weight))]
    blocks = lax.all_gather(weight, "shard", axis=0)
    return [(j, blocks[j]) for j in range(count)]


def times(values, blocks):
    rows = blocks[0][1].shape[0]
    return sum(
        dot(lax.dynamic_slice_in_dim(values, place * rows, rows, 1), block)
        for place, block in blocks
    )


def times_back(grads, blocks):
    pieces = [dot_t(grads, block) for _, block in blocks]
    if len(pieces) != 2:
        return jnp.concatenate(pieces, 1)
    first = lax.axis_index("shard") == 0
    return jnp.where(first, jnp.concatenate(pieces, 1), jnp.concatenate(pieces[::-1], 1))


def together(*values):
    leaves, tree = jax.tree.flatten(values)
    return jax.tree.unflatten(tree, lax.optimization_barrier(leaves))


def fold_order(bits):
    places = [0]
    for bit in reversed(bits):
        places = places + [place ^ bit for place in places]
    return places


def differing(blocks, bits, here):
    count = len(bits)
    blocks = blocks.reshape((2,) * count + blocks.shape[1:])
    ranked = sorted(bits, reverse=True)
    for k, bit in enumerate(ranked):
        blocks = jnp.where(here // bit % 2 == 1, jnp.flip(blocks, k), blocks)
    axes = [ranked.index(bit) for bit in bits]
    blocks = blocks.transpose(axes + list(range(count, blocks.ndim)))
    return blocks.reshape((1 << count,) + blocks.shape[count:])


def group_messages(own, crossed):
    if lax.axis_size("shard") != 2:
        both = lax.all_gather(jnp.concatenate([own, crossed], 0), "shard", axis=0, tiled=True)
        return [both]
    return [own, crossed, swap(own), swap(crossed)]


def product_kernel(rows, sources, order_ref, *refs):
    lefts, rights = refs[:sources], refs[sources : 2 * sources]
    kept_ref, sent_ref, picked_ref, turned_ref = refs[2 * sources :]
    count = order_ref.shape[0]
    padded = picked_ref.shape[0] // count

    @pl.when(pl.program_id(0) == 0)
    def _():
        start = 0
        for left_ref in lefts:
            tokens = left_ref.shape[0]
            turned_ref[:, start : start + tokens] = left_ref[...].astype(F32).T
            start += tokens
        if padded > rows:
            picked_ref[...] = jnp.zeros_like(picked_ref)
        for j in range(count):
            start = pl.multiple_of(order_ref[j] * rows, rows)
            picked_ref[j * padded : j * padded + rows, :] = turned_ref[
                pl.ds(start, rows), :
            ].astype(picked_ref.dtype)

    half = kept_ref.shape[0]
    right = jnp.concatenate([right_ref[...] for right_ref in rights], 0)
    kept_ref[...] = dot(picked_ref[:half, :].astype(BF), right).astype(kept_ref.dtype)
    sent_ref[...] = dot(picked_ref[half:, :].astype(BF), right).astype(sent_ref.dtype)


def product_halves(lefts, left_part, rights, right_part, bits):
    (left_start, left_columns), (start, columns) = left_part, right_part
    shards = lax.axis_size("shard")
    rows = left_columns // (lax.axis_size("expert") * shards)
    padded = -(-rows // 16) * 16
    order = (
        lax.axis_index("expert") ^ jnp.array(fold_order(bits), jnp.int32)
    ) * shards + lax.axis_index("shard")
    count = 1 << len(bits)
    half = count * padded // 2
    tokens = sum(left.shape[0] for left in lefts)
    if rows % 8:
        left = jnp.concatenate(
            [left[:, left_start : left_start + left_columns] for left in lefts], 0
        )
        right = jnp.concatenate([right[:, start : start + columns] for right in rights], 0)
        blocks = left.T.reshape(-1, shards, rows, tokens)
        blocks = lax.dynamic_index_in_dim(blocks, lax.axis_index("shard"), 1, keepdims=False)
        others = [bit for bit in (1, 2, 4, 8) if bit not in bits]
        picked = differing(blocks, (*others, *bits), lax.axis_index("expert"))[:count]
        picked = jnp.pad(picked, ((0, 0), (0, padded - rows), (0, 0))).reshape(-1, tokens)
        product = dot(picked, right).astype(BF)
        return product[:half], product[half:], picked
    tile = next(t for t in (512, 384, 256, 128) if columns % t == 0 and start % t == 0)
    return pl.pallas_call(
        functools.partial(product_kernel, rows, len(lefts)),
        grid_spec=pltpu.PrefetchScalarGridSpec(
            num_scalar_prefetch=1,
            grid=(columns // tile,),
            in_specs=[
                pl.BlockSpec(
                    (left.shape[0], left_columns),
                    lambda i, order: (0, left_start // left_columns),
                )
                for left in lefts
            ]
            + [
                pl.BlockSpec((right.shape[0], tile), lambda i, order: (0, i + start // tile))
                for right in rights
            ],
            out_specs=[
                pl.BlockSpec((half, tile), lambda i, order: (0, i)),
                pl.BlockSpec((half, tile), lambda i, order: (0, i)),
                pl.BlockSpec((count * padded, tokens), lambda i, order: (0, 0)),
            ],
            scratch_shapes=[pltpu.VMEM((left_columns, tokens), F32)],
        ),
        out_shape=[
            jax.ShapeDtypeStruct((half, columns), BF),
            jax.ShapeDtypeStruct((half, columns), BF),
            jax.ShapeDtypeStruct((count * padded, tokens), F32 if rows % 16 else BF),
        ],
        compiler_params=pltpu.CompilerParams(vmem_limit_bytes=56 << 20),
        cost_estimate=pl.CostEstimate(
            flops=4 * half * tokens * columns,
            bytes_accessed=4 * half * columns + 2 * tokens * (left_columns + columns),
            transcendentals=0,
        ),
    )(order.astype(jnp.int32), *lefts, *rights)


def pair_partial(partial, bits):
    experts, shards = lax.axis_size("expert"), lax.axis_size("shard")
    rows = partial.shape[0] // (experts * shards)
    if shards != 2:
        blocks = partial.reshape(experts, shards, rows, -1)
        total = lax.psum_scatter(blocks, "shard", scatter_dimension=1, tiled=True)[:, 0]
    else:
        own = lax.axis_index("shard")
        blocks = partial.reshape(experts, 2, rows, -1)
        kept = lax.dynamic_index_in_dim(blocks, own, 1, keepdims=False)
        sent = lax.dynamic_index_in_dim(blocks, 1 - own, 1, keepdims=False)
        total = (kept.astype(F32) + swap(sent).astype(F32)).astype(partial.dtype)
    return [differing(total, bits, lax.axis_index("expert")).reshape(experts * rows, -1)]


def line_places():
    return range(4, lax.axis_size("expert"), 4)


def partner(place):
    here = lax.axis_index("expert")
    there = here
    bit = 1
    while bit <= place:
        if place & bit:
            there = there + bit * (1 - 2 * (here // bit % 2))
        bit *= 2
    return there, lax.axis_index("shard")


def greet(places):
    barrier = pltpu.get_barrier_semaphore()
    for place in places:
        pl.semaphore_signal(
            barrier, inc=1, device_id=partner(place), device_id_type=pl.DeviceIdType.MESH
        )
    pl.semaphore_wait(barrier, len(places))


def slot_parts(rows):
    plane, line = (1, 2, 3), tuple(line_places())
    cut = rows // 4
    return (pl.ds(cut, rows - cut), line, plane), (pl.ds(0, cut), plane, line)


def gather_kernel(own_ref, out_ref, send_sems, recv_sems):
    parts = slot_parts(own_ref.shape[0])

    def send(k, rows, block, place):
        copy = pltpu.make_async_remote_copy(
            src_ref=out_ref.at[block, rows],
            dst_ref=out_ref.at[block ^ place, rows],
            send_sem=send_sems.at[k, block ^ place],
            recv_sem=recv_sems.at[k, block ^ place],
            device_id=partner(place),
            device_id_type=pl.DeviceIdType.MESH,
        )
        copy.start()
        return copy

    greet((1, 2, 3, *line_places()))
    out_ref[0] = own_ref[...]
    copies = {}
    for k, (rows, first, _) in enumerate(parts):
        for place in first:
            copies[k, place] = send(k, rows, 0, place)
    for k, (rows, _, second) in enumerate(parts):
        for place in second:
            copies[k, place] = send(k, rows, 0, place)
    arrived = set()
    for k in (1, 0):
        rows, first, second = parts[k]
        for block in first:
            copies[k, block].wait_recv()
            arrived.add((k, block))
            for place in second:
                copies[k, block ^ place] = send(k, rows, block, place)
    for key, copy in copies.items():
        copy.wait_send()
        if key not in arrived:
            copy.wait_recv()


def gather_slot(own):
    count = lax.axis_size("expert")
    return pl.pallas_call(
        gather_kernel,
        in_specs=[pl.BlockSpec(memory_space=pltpu.VMEM)],
        out_specs=pl.BlockSpec(memory_space=pltpu.VMEM),
        out_shape=jax.ShapeDtypeStruct((count, *own.shape), own.dtype),
        scratch_shapes=[pltpu.SemaphoreType.DMA((2, count)), pltpu.SemaphoreType.DMA((2, count))],
        compiler_params=pltpu.CompilerParams(
            collective_id=0, has_side_effects=True, vmem_limit_bytes=16 << 20
        ),
        cost_estimate=pl.CostEstimate(
            flops=5 * 10**10, bytes_accessed=4 * count * own.size, transcendentals=0
        ),
    )(own)


def scatter_kernel(part_ref, out_ref, *refs):
    parts = slot_parts(out_ref.shape[0])
    buffers = [refs[7 * k : 7 * k + 7] for k in range(2)]
    greet((1, 2, 3, *line_places()))
    copies = []

    def send(source, target, sems, index, place):
        copy = pltpu.make_async_remote_copy(
            src_ref=source,
            dst_ref=target,
            send_sem=sems[0].at[index],
            recv_sem=sems[1].at[index],
            device_id=partner(place),
            device_id_type=pl.DeviceIdType.MESH,
        )
        copy.start()
        copies.append(copy)
        return copy

    firsts = []
    for (rows, second, first), (first_ref, _, _, *sems) in zip(parts, buffers):
        firsts.append(
            [
                [
                    send(
                        part_ref.at[block ^ place, rows],
                        first_ref.at[k, i],
                        sems[:2],
                        (k, i),
                        place,
                    )
                    for i, place in enumerate(first)
                ]
                for k, block in enumerate((*second, 0))
            ]
        )
    lasts = {}
    for p in (1, 0):
        rows, second, _ = parts[p]
        first_ref, sum_ref, last_ref, *sems = buffers[p]
        for k, block in enumerate((*second, 0)):
            total = part_ref[block, rows, :].astype(F32)
            for i, copy in enumerate(firsts[p][k]):
                copy.wait_recv()
                total = total + first_ref[k, i].astype(F32)
            if block:
                sum_ref[k] = total.astype(sum_ref.dtype)
                lasts[p, k] = send(sum_ref.at[k], last_ref.at[k], sems[2:], k, block)
            else:
                out_ref[rows, :] = total
    for (p, k), copy in lasts.items():
        copy.wait_recv()
        out_ref[parts[p][0], :] += buffers[p][2][k].astype(F32)
    for copy in copies:
        copy.wait_send()


def scatter_slot(part):
    count, rows, columns = part.shape
    lines = count // 4
    cut = rows // 4
    scratch = []
    for height, groups, firsts in ((rows - cut, lines, 3), (cut, 4, lines - 1)):
        scratch += [
            pltpu.VMEM((groups, firsts, height, columns), part.dtype),
            pltpu.VMEM((groups - 1, height, columns), part.dtype),
            pltpu.VMEM((groups - 1, height, columns), part.dtype),
            pltpu.SemaphoreType.DMA((groups, firsts)),
            pltpu.SemaphoreType.DMA((groups, firsts)),
            pltpu.SemaphoreType.DMA((groups - 1,)),
            pltpu.SemaphoreType.DMA((groups - 1,)),
        ]
    return pl.pallas_call(
        scatter_kernel,
        in_specs=[pl.BlockSpec(memory_space=pltpu.VMEM)],
        out_specs=pl.BlockSpec(memory_space=pltpu.VMEM),
        out_shape=jax.ShapeDtypeStruct((rows, columns), F32),
        scratch_shapes=scratch,
        compiler_params=pltpu.CompilerParams(
            collective_id=1, has_side_effects=True, vmem_limit_bytes=24 << 20
        ),
        cost_estimate=pl.CostEstimate(
            flops=5 * 10**10, bytes_accessed=4 * part.size, transcendentals=0
        ),
    )(part)


REDUCE_STEPS = (1, 5, 3, 0, 7, 7, 4, 4, 3, 6, 2, 6, 0, 5, 7, 2,
                5, 2, 6, 7, 0, 3, 0, 4, 1, 2, 5, 3, 7, 1, 2)


def reduce_kernel(plans, steps, *refs):
    refs = list(refs)
    take = lambda count: [refs.pop(0) for _ in range(count)]
    pieces = [take(count) for _, count, _ in plans]
    firsts = [take(1)[0] if split else None for _, _, split in plans]
    outs = take(len(plans))
    sends = [[None if split and t == 0 else take(1)[0] for t in range(len(bits))] for bits, _, split in plans]
    arrivals = [take(len(bits)) for bits, _, _ in plans]
    send_sems, recv_sems = refs
    greet(sorted({bit for bits, _, _ in plans for bit in bits}))
    copies = []

    def add(target, parts, start, count):
        @pl.loop(0, count // 16)
        def _(k):
            here = pl.multiple_of(k * 16, 16)
            total = sum(part[pl.ds(start + here, 16), :].astype(F32) for part in parts)
            target[pl.ds(here, 16), :] = total.astype(target.dtype)

    latest = [None] * len(plans)
    done = [0] * len(plans)
    for g in steps:
        bits, _, split = plans[g]
        t = done[g]
        done[g] += 1
        if t:
            latest[g].wait_recv()
            pieces[g].append(arrivals[g][t - 1])
        if t == len(bits):
            add(outs[g], pieces[g], 0, outs[g].shape[0])
            continue
        count = arrivals[g][t].shape[0]
        source = firsts[g]
        if t or not split:
            source = sends[g][t]
            add(source, pieces[g], count, count)
        copy = pltpu.make_async_remote_copy(
            src_ref=source,
            dst_ref=arrivals[g][t],
            send_sem=send_sems.at[g, t],
            recv_sem=recv_sems.at[g, t],
            device_id=partner(bits[t]),
            device_id_type=pl.DeviceIdType.MESH,
        )
        copy.start()
        copies.append(copy)
        latest[g] = copy
    for copy in copies:
        copy.wait_send()


def reduce_all(groups, steps):
    plans = tuple((bits, len(pieces), first is not None) for bits, pieces, first in groups)
    outs, sends, arrivals = [], [], []
    for bits, pieces, first in groups:
        count, columns = pieces[0].shape
        count = count * (1 if first is None else 2)
        for t in range(len(bits)):
            count = count // 2
            arrivals.append(pltpu.VMEM((count, columns), BF))
            if t or first is None:
                sends.append(pltpu.VMEM((count, columns), BF))
        outs.append(jax.ShapeDtypeStruct((count, columns), F32))
    operands = [piece for _, pieces, _ in groups for piece in pieces]
    operands += [first for _, _, first in groups if first is not None]
    most = max(len(bits) for bits, _, _ in groups)
    in_vmem = pl.BlockSpec(memory_space=pltpu.VMEM)
    return pl.pallas_call(
        functools.partial(reduce_kernel, plans, steps),
        in_specs=[in_vmem] * len(operands),
        out_specs=[in_vmem] * len(outs),
        out_shape=outs,
        scratch_shapes=[
            *sends,
            *arrivals,
            pltpu.SemaphoreType.DMA((len(groups), most)),
            pltpu.SemaphoreType.DMA((len(groups), most)),
        ],
        compiler_params=pltpu.CompilerParams(
            collective_id=2, has_side_effects=True, vmem_limit_bytes=58 << 20
        ),
        cost_estimate=pl.CostEstimate(
            flops=10**11,
            bytes_accessed=4 * sum(operand.size for operand in operands),
            transcendentals=0,
        ),
    )(*operands)


def attend_kernel(
    raw_ref, cosine_ref, sine_ref, expand_ref, keys_ref, bias_ref,
    nope_ref, queries_ref, weights_ref, mixed_ref, out_ref,
):
    rows = raw_ref.shape[0]
    width = HEAD + ROPE
    cosine, sine = cosine_ref[...], sine_ref[...]
    for h in range(2):
        raw = raw_ref[:, h * width : (h + 1) * width]
        nope = raw[:, :HEAD].astype(BF)
        first = raw[:, HEAD : HEAD + ROPE // 2]
        second = raw[:, HEAD + ROPE // 2 :]
        turned = jnp.concatenate(
            [first * cosine - second * sine, second * cosine + first * sine], -1
        )
        nope_ref[:, h * HEAD : (h + 1) * HEAD] = nope
        latent = dot_t(nope, expand_ref[:, 2 * h * HEAD : (2 * h + 1) * HEAD])
        queries_ref[h * rows : (h + 1) * rows, :RANK] = latent.astype(BF)
        queries_ref[h * rows : (h + 1) * rows, RANK:] = turned.astype(BF)
    bias = bias_ref[...]
    for h in range(2):
        part = slice(h * rows, (h + 1) * rows)
        scores = dot_t(queries_ref[part, :], keys_ref[...]) * (HEAD + ROPE) ** -0.5 + bias
        shifted = jnp.exp(scores - jnp.max(scores, -1, keepdims=True))
        total = jnp.sum(shifted, -1, keepdims=True)
        weights_ref[part, :] = (shifted * (1.0 / total)).astype(BF)
    mixed_ref[...] = dot(weights_ref[...], keys_ref[:, :RANK]).astype(BF)
    for h in range(2):
        out_ref[:, h * VHEAD : (h + 1) * VHEAD] = dot(
            mixed_ref[h * rows : (h + 1) * rows, :],
            expand_ref[:, (2 * h + 1) * HEAD : (2 * h + 2) * HEAD],
        ).astype(BF)


def attend(query_raw, cosine, sine, expand, keys, bias):
    rows, slot = bias.shape
    steps = HEADS // 2
    whole = lambda *shape: pl.BlockSpec(shape, lambda i: (0,) * len(shape))
    return pl.pallas_call(
        attend_kernel,
        grid=(steps,),
        in_specs=[
            pl.BlockSpec((rows, 2 * (HEAD + ROPE)), lambda i: (0, i)),
            whole(rows, ROPE // 2),
            whole(rows, ROPE // 2),
            pl.BlockSpec((RANK, 4 * HEAD), lambda i: (0, i)),
            whole(slot, RANK + ROPE),
            whole(rows, slot),
        ],
        out_specs=[
            pl.BlockSpec((rows, 2 * HEAD), lambda i: (0, i)),
            pl.BlockSpec((2 * rows, RANK + ROPE), lambda i: (i, 0)),
            pl.BlockSpec((2 * rows, slot), lambda i: (i, 0)),
            pl.BlockSpec((2 * rows, RANK), lambda i: (i, 0)),
            pl.BlockSpec((rows, 2 * VHEAD), lambda i: (0, i)),
        ],
        out_shape=[
            jax.ShapeDtypeStruct((rows, HEADS * HEAD), BF),
            jax.ShapeDtypeStruct((HEADS * rows, RANK + ROPE), BF),
            jax.ShapeDtypeStruct((HEADS * rows, slot), BF),
            jax.ShapeDtypeStruct((HEADS * rows, RANK), BF),
            jax.ShapeDtypeStruct((rows, HEADS * VHEAD), BF),
        ],
        compiler_params=pltpu.CompilerParams(vmem_limit_bytes=40 << 20),
        cost_estimate=pl.CostEstimate(
            flops=2 * HEADS * rows * slot * (2 * RANK + ROPE),
            bytes_accessed=2 * HEADS * rows * slot,
            transcendentals=HEADS * rows * slot,
        ),
    )(query_raw, cosine, sine, expand, keys, bias)


def attend_back_kernel(
    order_ref, grad_ref, expand_ref, keys_ref, weights_ref, queries_ref, mixed_ref, nope_ref, cosine_ref,
    sine_ref, query_grad_ref, expand_grad_ref, key_out_ref, key_grad_ref, latent_ref, scores_ref,
):
    rows = grad_ref.shape[0]
    width = HEAD + ROPE
    scale = (HEAD + ROPE) ** -0.5

    @pl.when(pl.program_id(0) == 0)
    def _():
        key_grad_ref[...] = jnp.zeros_like(key_grad_ref)

    for h in range(2):
        part = slice(h * rows, (h + 1) * rows)
        grad = grad_ref[:, h * VHEAD : (h + 1) * VHEAD]
        latent_ref[part, :] = dot_t(
            grad, expand_ref[:, (2 * h + 1) * HEAD : (2 * h + 2) * HEAD]
        ).astype(BF)
        arrived = dot_t(latent_ref[part, :], keys_ref[:, :RANK])
        weights = weights_ref[part, :].astype(F32)
        mean = jnp.sum(weights * arrived, -1, keepdims=True)
        scores_ref[part, :] = (weights * (arrived - mean) * scale).astype(BF)
    key_grad_ref[...] += t_dot(queries_ref[...], scores_ref[...])
    key_grad_ref[:RANK, :] += t_dot(latent_ref[...], weights_ref[...])
    cosine, sine = cosine_ref[...], sine_ref[...]
    for h in range(2):
        part = slice(h * rows, (h + 1) * rows)
        query_grad = dot(scores_ref[part, :], keys_ref[...])
        latent = query_grad[:, :RANK].astype(BF)
        key_part = slice(2 * h * HEAD, (2 * h + 1) * HEAD)
        value_part = slice((2 * h + 1) * HEAD, (2 * h + 2) * HEAD)
        nope = dot(latent, expand_ref[:, key_part])
        first = query_grad[:, RANK : RANK + ROPE // 2]
        second = query_grad[:, RANK + ROPE // 2 :]
        query_grad_ref[:, h * width : (h + 1) * width] = jnp.concatenate(
            [nope, first * cosine + second * sine, second * cosine - first * sine], -1
        ).astype(BF)
        key_grad = t_dot(latent, nope_ref[:, h * HEAD : (h + 1) * HEAD]).astype(BF)
        value_grad = t_dot(
            mixed_ref[part, :], grad_ref[:, h * VHEAD : (h + 1) * VHEAD]
        ).astype(BF)
        count = order_ref.shape[0]
        height = RANK // count
        for j in range(count):
            target = pl.ds(pl.multiple_of(order_ref[j] * height, height), height)
            source = slice(j * height, (j + 1) * height)
            expand_grad_ref[target, key_part] = key_grad[source, :]
            expand_grad_ref[target, value_part] = value_grad[source, :]

    @pl.when(pl.program_id(0) == pl.num_programs(0) - 1)
    def _():
        key_out_ref[...] = key_grad_ref[...].T.astype(BF)


def attend_back(grad_out, expand, keys, weights, queries, mixed, nope, cosine, sine, order):
    rows = grad_out.shape[0]
    slot = keys.shape[0]
    whole = lambda *shape: pl.BlockSpec(shape, lambda i, order: (0,) * len(shape))
    return pl.pallas_call(
        attend_back_kernel,
        grid_spec=pltpu.PrefetchScalarGridSpec(
            num_scalar_prefetch=1,
            grid=(HEADS // 2,),
            in_specs=[
            pl.BlockSpec((rows, 2 * VHEAD), lambda i, order: (0, i)),
            pl.BlockSpec((RANK, 4 * HEAD), lambda i, order: (0, i)),
            whole(slot, RANK + ROPE),
            pl.BlockSpec((2 * rows, slot), lambda i, order: (i, 0)),
            pl.BlockSpec((2 * rows, RANK + ROPE), lambda i, order: (i, 0)),
            pl.BlockSpec((2 * rows, RANK), lambda i, order: (i, 0)),
            pl.BlockSpec((rows, 2 * HEAD), lambda i, order: (0, i)),
            whole(rows, ROPE // 2),
            whole(rows, ROPE // 2),
        ],
        out_specs=[
            pl.BlockSpec((rows, 2 * (HEAD + ROPE)), lambda i, order: (0, i)),
            pl.BlockSpec((RANK, 4 * HEAD), lambda i, order: (0, i)),
            whole(slot, RANK + ROPE),
        ],
        scratch_shapes=[
            pltpu.VMEM((RANK + ROPE, slot), F32),
            pltpu.VMEM((2 * rows, RANK), BF),
            pltpu.VMEM((2 * rows, slot), BF),
        ],
        ),
        out_shape=[
            jax.ShapeDtypeStruct((rows, HEADS * (HEAD + ROPE)), BF),
            jax.ShapeDtypeStruct((RANK, 2 * HEADS * HEAD), BF),
            jax.ShapeDtypeStruct((slot, RANK + ROPE), BF),
        ],
        compiler_params=pltpu.CompilerParams(vmem_limit_bytes=48 << 20),
        cost_estimate=pl.CostEstimate(
            flops=2 * HEADS * rows * slot * (3 * RANK + 2 * (RANK + ROPE)),
            bytes_accessed=2 * HEADS * rows * slot,
            transcendentals=0,
        ),
    )(order, grad_out, expand, keys, weights, queries, mixed, nope, cosine, sine)


def expert_kernel(sources, here_ref, rows_ref, router_ref, *refs):
    weights = refs[: 2 * sources]
    (
        row_grad_ref, units_ref, back_ref, gate_ref, logit_grad_ref, total_ref, probs_ref, share_ref,
    ) = refs[2 * sources :]
    step = pl.program_id(0)
    chunks = pl.num_programs(0) // sources

    @pl.when(step == 0)
    def _():
        logits = dot_t(router_ref[...], rows_ref[...])
        powers = jnp.exp(logits - jnp.max(logits, 0, keepdims=True))
        probs = powers / jnp.sum(powers, 0, keepdims=True)
        own = lax.broadcasted_iota(jnp.int32, probs.shape, 0) == here_ref[0]
        probs_ref[...] = probs
        gate_ref[...] = jnp.sum(jnp.where(own, probs, 0.0), 0, keepdims=True)
        share_ref[...] = jnp.zeros_like(share_ref)
        total_ref[...] = jnp.zeros_like(total_ref)

    def work(in_ref, slopes_ref):
        gate = dot_t(in_ref[0], rows_ref[...])
        up = dot_t(in_ref[1], rows_ref[...])
        back = slopes_ref[...]
        sigma = 1.0 / (1.0 + jnp.exp(-gate))
        act = gate * sigma
        units = (act * up).astype(BF)
        units_ref[...] = units
        share_ref[...] += jnp.sum(back * units.astype(F32), 0, keepdims=True)
        back = back * gate_ref[...]
        back_ref[0] = (back * up * (sigma * (1.0 + gate * (1.0 - sigma)))).astype(BF)
        back_ref[1] = (back * act).astype(BF)
        total_ref[...] += t_dot(back_ref[0], in_ref[0])
        total_ref[...] += t_dot(back_ref[1], in_ref[1])

    for k in range(sources):

        @pl.when(step // chunks == k)
        def _(k=k):
            work(weights[2 * k], weights[2 * k + 1])

    @pl.when(step == pl.num_programs(0) - 1)
    def _():
        probs = probs_ref[...]
        own = lax.broadcasted_iota(jnp.int32, probs.shape, 0) == here_ref[0]
        grad = probs * (own.astype(F32) - gate_ref[...]) * share_ref[...]
        logit_grad_ref[...] = grad.astype(BF)
        row_grad_ref[...] = (
            total_ref[...] + t_dot(logit_grad_ref[...], router_ref[...])
        ).astype(BF)


def expert_pass(here, rows, router, weights):
    count, width = rows.shape
    experts = router.shape[0]
    sources = len(weights)
    units = weights[0][1].shape[0]
    tile = next(t for t in (352, 176, 88, 64, 32, 16, units) if units % t == 0)
    chunks = units // tile
    once = pl.Buffered(1)
    in_specs = [
        pl.BlockSpec((count, width), lambda i, h: (0, 0), pipeline_mode=once),
        pl.BlockSpec((experts, width), lambda i, h: (0, 0)),
    ]
    for k in range(sources):
        at = lambda i, k=k: jnp.clip(i - k * chunks, 0, chunks - 1)
        in_specs.append(pl.BlockSpec((2, tile, width), lambda i, h, at=at: (0, at(i), 0)))
        in_specs.append(pl.BlockSpec((tile, count), lambda i, h, at=at: (at(i), 0)))
    return pl.pallas_call(
        functools.partial(expert_kernel, sources),
        grid_spec=pltpu.PrefetchScalarGridSpec(
            num_scalar_prefetch=1,
            grid=(sources * chunks,),
            in_specs=in_specs,
            out_specs=[
                pl.BlockSpec((count, width), lambda i, h: (0, 0), pipeline_mode=once),
                pl.BlockSpec((tile, count), lambda i, h: (i, 0)),
                pl.BlockSpec(
                    (None, 2, tile, count), lambda i, h: (i // chunks, 0, i % chunks, 0)
                ),
                pl.BlockSpec((1, count), lambda i, h: (0, 0)),
                pl.BlockSpec((experts, count), lambda i, h: (0, 0)),
            ],
            scratch_shapes=[
                pltpu.VMEM((count, width), F32),
                pltpu.VMEM((experts, count), F32),
                pltpu.VMEM((1, count), F32),
            ],
        ),
        out_shape=[
            jax.ShapeDtypeStruct((count, width), BF),
            jax.ShapeDtypeStruct((sources * units, count), BF),
            jax.ShapeDtypeStruct((sources, 2, units, count), BF),
            jax.ShapeDtypeStruct((1, count), F32),
            jax.ShapeDtypeStruct((experts, count), BF),
        ],
        compiler_params=pltpu.CompilerParams(vmem_limit_bytes=58 << 20),
        cost_estimate=pl.CostEstimate(
            flops=8 * count * width * sources * units,
            bytes_accessed=4 * (count + sources * units) * width,
            transcendentals=count * sources * units,
        ),
    )(here, rows, router, *[piece for pair in weights for piece in pair])


def per_device(
    tokens,
    lengths,
    routes,
    attn_gain,
    query_weight,
    latent_weight,
    latent_gain,
    expand_weight,
    output_weight,
    ffn_gain,
    router_weight,
    shared_in,
    shared_out,
    expert_in,
    expert_out,
    cotangent,
):
    local_rows = tokens.shape[1]
    model_width = tokens.shape[2]
    owners, shards = lax.axis_size("expert"), lax.axis_size("shard")
    experts_all = router_weight.shape[1]
    assert experts_all == owners
    topk_count = routes.shape[2]
    capacity = max(2, 9 * local_rows * topk_count // (8 * experts_all))
    capacity = -(-capacity // 8) * 8
    here = lax.axis_index("expert")

    query_blocks = row_blocks(query_weight)
    latent_blocks = row_blocks(latent_weight)
    gains = jnp.concatenate([attn_gain, ffn_gain, latent_gain])[None]
    gains = (
        jnp.where(
            lax.axis_index("shard") == 0,
            jnp.concatenate([gains, swap(gains)], 0),
            jnp.concatenate([swap(gains), gains], 0),
        )
        if shards == 2
        else lax.all_gather(gains, "shard", axis=0, tiled=True)
    ).astype(F32)
    cut = attn_gain.shape[0]
    gain_attn = gains[:, :cut].reshape(-1)
    gain_ffn = gains[:, cut : 2 * cut].reshape(-1)
    gain_latent = gains[:, 2 * cut :].reshape(-1)
    expand = whole_rows(expand_weight)
    here_index = here * local_rows + jnp.arange(local_rows, dtype=jnp.int32)
    query_segment, query_position, query_valid = layout(lengths[0], here_index)
    cosine, sine_table = rope_tables(query_position)
    live_rows = query_valid.astype(F32)[:, None]
    grad_out = cotangent[0].astype(F32) * live_rows
    grad_out_low = grad_out.astype(BF)

    expert_ids = jnp.arange(experts_all, dtype=jnp.int32)
    member = jnp.any(routes[0].T[None] == expert_ids[:, None, None], 1)
    token_ids = jnp.arange(local_rows, dtype=jnp.int32)
    earlier = (token_ids[:, None] < token_ids[None, :]).astype(BF)
    rank = dot(member.astype(BF), earlier).astype(jnp.int32)
    place_ids = jnp.arange(capacity, dtype=jnp.int32)
    spread = (
        (member[:, None, :] & (rank[:, None, :] == place_ids[None, :, None]))
        .reshape(experts_all * capacity, local_rows)
        .astype(BF)
    )

    def exchange(rows):
        return lax.all_to_all(
            rows.reshape(owners, capacity, model_width),
            "expert",
            split_axis=0,
            concat_axis=0,
            tiled=True,
        ).reshape(owners * capacity, model_width)


    inputs = tokens[0].astype(F32)
    inverse_attn = rms_scale(inputs)
    normed_attn = inputs * inverse_attn
    attn_in = (normed_attn * gain_attn).astype(BF)
    latent_raw = times(attn_in, latent_blocks)
    latent = latent_raw[:, :RANK]
    inverse_latent = rms_scale(latent)
    normed_latent = latent * inverse_latent
    latent_in = (normed_latent * gain_latent).astype(BF)
    key_rope = rotate(latent_raw[:, RANK:], cosine, sine_table).astype(BF)
    own_keys = jnp.concatenate([latent_in, key_rope], -1)
    expert_in_rows, expert_out_rows = expert_in[0].transpose(1, 2, 0), expert_out[0]
    (
        own_keys, output_weight, router_weight, shared_in, shared_out, expert_in_rows, expert_out_rows,
    ) = together(
        own_keys, output_weight, router_weight, shared_in, shared_out, expert_in_rows, expert_out_rows,
    )
    output_blocks = row_blocks(output_weight)
    router = whole_rows(router_weight)
    shared_out_blocks = row_blocks(shared_out)
    shared_in_blocks = row_blocks(shared_in)
    if shards == 2:
        expert_weights = [
            (expert_in_rows, expert_out_rows),
            (swap(expert_in_rows), swap(expert_out_rows)),
        ]
    else:
        expert_weights = [
            (
                lax.all_gather(expert_in_rows, "shard", axis=1, tiled=True),
                lax.all_gather(expert_out_rows, "shard", axis=0, tiled=True),
            )
        ]

    sent_grads = dot(spread, grad_out_low).astype(BF)
    keys, sent_grads = together(gather_slot(own_keys), sent_grads)
    received_grads = exchange(sent_grads)
    keys = keys.reshape(-1, RANK + ROPE)
    key_index = (
        (here ^ jnp.arange(owners, dtype=jnp.int32))[:, None] * local_rows
        + jnp.arange(local_rows, dtype=jnp.int32)[None, :]
    ).reshape(-1)

    query_raw = times(attn_in, query_blocks)
    key_segment = layout(lengths[0], key_index)[0]
    allowed = (query_segment[:, None] == key_segment[None, :]) & (
        key_index[None, :] <= here_index[:, None]
    )
    bias = jnp.where(allowed, 0.0, MASK_FILL).astype(F32)
    query_nope, queries, attention, mixed_latent, mixed_heads = attend(
        query_raw, cosine, sine_table, expand, keys, bias
    )
    (
        mixed_heads, received_grads, output_blocks, router, shared_in_blocks, shared_out_blocks,
        expert_weights,
    ) = together(
        mixed_heads, received_grads, output_blocks, router, shared_in_blocks, shared_out_blocks,
        expert_weights,
    )
    hidden_state = inputs + times(mixed_heads, output_blocks)
    inverse_ffn = rms_scale(hidden_state)
    normed_ffn = hidden_state * inverse_ffn
    ffn_in = (normed_ffn * gain_ffn).astype(BF)

    received = exchange(dot(spread, ffn_in).astype(BF))
    shared_both = times(ffn_in, shared_in_blocks)
    shared_act, shared_slope = silu_parts(shared_both[:, :FF_S])
    shared_up = shared_both[:, FF_S:]
    shared_hidden = (shared_act * shared_up).astype(BF)
    shared_result = times(shared_hidden, shared_out_blocks)
    grad_shared_hidden = times_back(grad_out_low, shared_out_blocks)
    grad_shared_gate = (grad_shared_hidden * shared_up * shared_slope).astype(BF)
    grad_shared_up = (grad_shared_hidden * shared_act).astype(BF)
    grad_ffn_in = times_back(
        jnp.concatenate([grad_shared_gate, grad_shared_up], -1), shared_in_blocks
    )
    out_slopes = [dot_t(weight_out, received_grads) for _, weight_out in expert_weights]
    out_message = jnp.concatenate([shared_hidden, grad_out_low], 1)
    in_message = jnp.concatenate([ffn_in, grad_shared_gate, grad_shared_up], 1)
    received, shared_result, grad_ffn_in, out_slopes, out_message, in_message = together(
        received, shared_result, grad_ffn_in, out_slopes, out_message, in_message
    )

    early_message = jnp.concatenate([attn_in, mixed_heads], 1)
    received, early_message = together(received, early_message)
    arrived = cross(out_message, 1), cross(in_message, 4), cross(early_message, 2)
    expert_results = expert_pass(
        here[None],
        received,
        router.T,
        [(weight_in, slopes) for (weight_in, _), slopes in zip(expert_weights, out_slopes)],
    )
    row_grads, hidden, hidden_grads, row_gate, row_grad_logits = expert_results

    returned_grads = exchange(row_grads)
    units = expert_weights[0][1].shape[0]
    row_gate = row_gate.reshape(-1, 1)
    weighted_grads = (row_gate * received_grads.astype(F32)).astype(BF)

    def expert_grads(j):
        return (
            dot(hidden_grads[j].reshape(2 * units, -1), received).reshape(2, units, -1),
            dot(hidden[j * units : (j + 1) * units], weighted_grads),
        )

    other_parts = [part.astype(BF) for part in expert_grads(len(expert_weights) - 1)]
    other_parts, arrived = together(other_parts, arrived)
    out_messages = group_messages(out_message, arrived[0])
    in_messages = group_messages(in_message, arrived[1])
    early_messages = group_messages(early_message, arrived[2])
    cut = 4096
    shared_halves = [
        product_halves(messages, left_part, messages, right_part, order)[:2]
        for messages, left_part, right_part, order in (
            (out_messages, (0, FF_S), (FF_S, model_width), (2, 8, 4)),
            (in_messages, (0, model_width), (model_width, cut), (1, 2, 8)),
            (in_messages, (0, model_width), (model_width + cut, 2 * FF_S - cut), (2, 1, 8)),
        )
    ]
    hidden, hidden_grads, shared_halves, early_messages = together(
        hidden, hidden_grads, shared_halves, early_messages
    )
    shared_sums = [
        [kept, cross(sent, bit)] for (kept, sent), bit in zip(shared_halves, (2, 1, 2))
    ]
    row_out = 0.0
    for j, (_, weight) in enumerate(expert_weights):
        row_out = row_out + t_dot(hidden[j * units : (j + 1) * units], weight)
    row_out = (row_gate * row_out).astype(BF)
    if shards == 2:
        hidden, hidden_grads, other_parts = together(
            hidden, hidden_grads, [swap(part) for part in other_parts]
        )
        grad_expert_in, grad_expert_out = [
            own + other.astype(F32) for own, other in zip(expert_grads(0), other_parts)
        ]
    else:
        grad_expert_in, grad_expert_out = [
            lax.psum_scatter(part, "shard", scatter_dimension=part.ndim - 2, tiled=True).astype(F32)
            for part in other_parts
        ]
    grad_router = dot(row_grad_logits, received)
    returned_grads, row_out, grad_expert_in, grad_expert_out, grad_router = together(
        returned_grads, row_out, grad_expert_in, grad_expert_out, grad_router
    )
    grad_expert_in = grad_expert_in.transpose(2, 0, 1)[None]
    grad_expert_out = grad_expert_out[None]
    returned = exchange(row_out)
    grad_ffn_in = grad_ffn_in + t_dot(spread, returned_grads)
    grad_gain_ffn = jnp.sum(grad_ffn_in * normed_ffn, 0)
    grad_hidden_state = grad_out + norm_back(grad_ffn_in * gain_ffn, normed_ffn, inverse_ffn)

    grad_attn_out = grad_hidden_state.astype(BF)
    grad_mixed = times_back(grad_attn_out, output_blocks).astype(BF)
    grad_mixed, grad_attn_out = together(grad_mixed, grad_attn_out)
    out_arrived = cross(grad_attn_out, 2)
    expand_order = (2, 1, 4, 8)
    if shards == 2:
        differs = here ^ jnp.arange(owners, dtype=jnp.int32)
        place = sum((differs // bit % 2) << (3 - k) for k, bit in enumerate(expand_order))
        other = lax.axis_index("shard") ^ jnp.arange(2, dtype=jnp.int32)
        block_order = (other[None, :] * owners + place[:, None]).reshape(-1).astype(jnp.int32)
    else:
        block_order = jnp.zeros((1,), jnp.int32)
    attention_grads = attend_back(
        grad_mixed,
        expand,
        keys,
        attention,
        queries,
        mixed_latent,
        query_nope,
        cosine,
        sine_table,
        block_order,
    )
    attention_grads, shared_sums, out_arrived = together(
        attention_grads, shared_sums, out_arrived
    )
    grad_query_raw, grad_expand, grad_keys = attention_grads

    query_arrived = cross(grad_query_raw, 2)
    own_query = grad_query_raw
    if shards == 2:
        half_rank = RANK // 2
        expand_pair = [grad_expand[:half_rank], swap(grad_expand[half_rank:])]
    else:
        expand_pair = pair_partial(grad_expand, expand_order)
    grad_own_keys, returned, query_arrived, grad_query_raw, expand_pair = together(
        scatter_slot(grad_keys.reshape(owners, local_rows, -1)),
        returned,
        query_arrived,
        grad_query_raw,
        expand_pair,
    )
    grad_latent_in = grad_own_keys[:, :RANK]
    grad_gain_latent = jnp.sum(grad_latent_in * normed_latent, 0)
    grad_latent = norm_back(grad_latent_in * gain_latent, normed_latent, inverse_latent)
    grad_latent_raw = jnp.concatenate(
        [grad_latent, rotate_back(grad_own_keys[:, RANK:], cosine, sine_table)], -1
    ).astype(BF)
    latent_message = jnp.pad(grad_latent_raw, ((0, 0), (0, -grad_latent_raw.shape[1] % 128)))
    latent_messages = group_messages(latent_message, cross(latent_message, 2))
    query_messages = group_messages(own_query, query_arrived)
    out_messages = group_messages(grad_attn_out, out_arrived)
    in_part, heads_part = (0, model_width), (model_width, HEADS * VHEAD)
    whole_part = lambda array: (0, array.shape[1])
    *query_halves, picked = product_halves(
        early_messages, in_part, query_messages, whole_part(grad_query_raw), (1, 4, 8)
    )
    output_halves = product_halves(
        early_messages, heads_part, out_messages, whole_part(grad_attn_out), (4, 1, 8)
    )[:2]
    latent_product = dot(picked, jnp.concatenate(latent_messages, 0)).astype(BF)
    latent_halves = jnp.split(latent_product, 2, 0)
    grad_attn_in = times_back(grad_latent_raw, latent_blocks) + times_back(
        grad_query_raw, query_blocks
    )
    grad_gain_attn = jnp.sum(grad_attn_in * normed_attn, 0)
    tokens_grad = grad_hidden_state + norm_back(grad_attn_in * gain_attn, normed_attn, inverse_attn)
    devices = owners * shards
    rows = model_width // devices
    small = jnp.concatenate(
        [
            vector.reshape(devices, -1)
            for vector in (grad_router.T, grad_gain_attn, grad_gain_ffn, grad_gain_latent)
        ],
        1,
    )
    cuts = [rows * experts_all, rows * (experts_all + 1), rows * (experts_all + 2)]
    small = jnp.pad(small, ((0, 0), (0, -small.shape[1] % 2048))).reshape(devices * 16, -1)
    small_pair = pair_partial(small.astype(BF), expand_order)
    sums = reduce_all(
        [
            ((1, 4, 8), [latent_halves[0]], latent_halves[1]),
            ((8, 4), shared_sums[0], None),
            (expand_order, expand_pair, None),
            ((1, 4, 8), [query_halves[0]], query_halves[1]),
            ((2, 8), shared_sums[1], None),
            ((4, 1, 8), [output_halves[0]], output_halves[1]),
            ((1, 8), shared_sums[2], None),
            (expand_order, small_pair, None),
        ],
        REDUCE_STEPS,
    )
    grad_latent_weight = sums[0][:, : RANK + ROPE]
    grad_shared_out = sums[1][: FF_S // devices]
    grad_expand, grad_query = sums[2:4]
    grad_shared_in = jnp.concatenate([sums[4], sums[6]], 1)
    grad_output = sums[5]
    small = sums[7].reshape(-1)
    routed = t_dot(spread, returned)
    block_result = hidden_state + shared_result + routed
    return (
        block_result.astype(BF)[None],
        tokens_grad.astype(BF)[None],
        small[cuts[0] : cuts[1]],
        grad_query,
        grad_latent_weight,
        small[cuts[2] : cuts[2] + RANK // devices],
        grad_expand,
        grad_output,
        small[cuts[1] : cuts[2]],
        small[: cuts[0]].reshape(rows, experts_all),
        grad_shared_in,
        grad_shared_out,
        grad_expert_in,
        grad_expert_out,
    )


def solution(mesh):
    return jax.shard_map(
        per_device,
        mesh=mesh,
        in_specs=(
            P("shard", "expert", None),
            P("shard", None),
            P("shard", "expert", None),
            P("shard"),
            P("shard", None),
            P("shard", None),
            P("shard"),
            P("shard", None),
            P("shard", None),
            P("shard"),
            P("shard", None),
            P("shard", None),
            P("shard", None),
            P("expert", None, None, "shard"),
            P("expert", "shard", None),
            P("shard", "expert", None),
        ),
        out_specs=(
            P("shard", "expert", None),
            P("shard", "expert", None),
            P(("expert", "shard")),
            P(("expert", "shard"), None),
            P(("expert", "shard"), None),
            P(("expert", "shard")),
            P(("expert", "shard"), None),
            P(("expert", "shard"), None),
            P(("expert", "shard")),
            P(("expert", "shard"), None),
            P(("expert", "shard"), None),
            P(("expert", "shard"), None),
            P("expert", None, None, "shard"),
            P("expert", "shard", None),
        ),
        check_vma=False,
    )
```

```python
import functools

import jax
import jax.numpy as jnp
from jax import lax
from jax.experimental import pallas as pl
from jax.experimental.pallas import tpu as pltpu
from jax.sharding import PartitionSpec as P

HEADS = 16
HEAD = 128
ROPE = 64
VHEAD = 128
RANK = 512
FF_S = 2816
SLOT = 2048

EPS = 1e-06
MASK_FILL = -1e30
BF = jnp.bfloat16
F32 = jnp.float32


def layout(lengths_slot, slot_index):
    first_len = lengths_slot[0]
    second_end = first_len + lengths_slot[1]
    segment = (slot_index >= first_len).astype(jnp.int32) + (slot_index >= second_end).astype(
        jnp.int32
    )
    seq_start = jnp.where(segment == 0, 0, jnp.where(segment == 1, first_len, second_end))
    return (segment, slot_index - seq_start, slot_index < second_end)


def rope_tables(positions):
    half_width = ROPE // 2
    inverse = 10000.0 ** (-jnp.arange(half_width, dtype=F32) / half_width)
    angles = positions.astype(F32)[:, None] * inverse[None, :]
    return (jnp.cos(angles), jnp.sin(angles))


def rotate(values, cosine, sine_table):
    half_width = values.shape[-1] // 2
    first_half = values[..., :half_width]
    second_half = values[..., half_width:]
    return jnp.concatenate(
        [
            first_half * cosine - second_half * sine_table,
            second_half * cosine + first_half * sine_table,
        ],
        -1,
    )


def rotate_back(grads_in, cosine, sine_table):
    return rotate(grads_in, cosine, -sine_table)


def silu_parts(gate_in):
    sigma = jax.nn.sigmoid(gate_in)
    return (gate_in * sigma, sigma * (1.0 + gate_in * (1.0 - sigma)))


def rms_scale(values):
    return lax.rsqrt(jnp.mean(values * values, -1, keepdims=True) + EPS)


def norm_back(grad_in, normed, inverse):
    return inverse * (grad_in - normed * jnp.mean(grad_in * normed, -1, keepdims=True))


def dot(left, right):
    return jnp.dot(left, right, preferred_element_type=F32)


def dot_t(left, right):
    return lax.dot_general(left, right, (((1,), (1,)), ((), ())), preferred_element_type=F32)


def t_dot(left, right):
    return lax.dot_general(left, right, (((0,), (0,)), ((), ())), preferred_element_type=F32)


def cross(values, bit):
    count = lax.axis_size("expert")
    return lax.ppermute(values, "expert", [(i, i ^ bit) for i in range(count)])


def swap(values):
    return lax.ppermute(values, "shard", [(0, 1), (1, 0)])


def whole_rows(weight):
    if lax.axis_size("shard") != 2:
        return lax.all_gather(weight, "shard", axis=0, tiled=True)
    other = swap(weight)
    first = lax.axis_index("shard") == 0
    return jnp.where(
        first, jnp.concatenate([weight, other], 0), jnp.concatenate([other, weight], 0)
    )


def row_blocks(weight):
    count = lax.axis_size("shard")
    if count == 2:
        own = lax.axis_index("shard")
        return [(own, weight), (1 - own, swap(weight))]
    blocks = lax.all_gather(weight, "shard", axis=0)
    return [(j, blocks[j]) for j in range(count)]


def times(values, blocks):
    rows = blocks[0][1].shape[0]
    return sum(
        dot(lax.dynamic_slice_in_dim(values, place * rows, rows, 1), block)
        for place, block in blocks
    )


def times_back(grads, blocks):
    pieces = [dot_t(grads, block) for _, block in blocks]
    if len(pieces) != 2:
        return jnp.concatenate(pieces, 1)
    first = lax.axis_index("shard") == 0
    return jnp.where(first, jnp.concatenate(pieces, 1), jnp.concatenate(pieces[::-1], 1))


def together(*values):
    leaves, tree = jax.tree.flatten(values)
    return jax.tree.unflatten(tree, lax.optimization_barrier(leaves))


def fold_order(bits):
    places = [0]
    for bit in reversed(bits):
        places = places + [place ^ bit for place in places]
    return places


def differing(blocks, bits, here):
    count = len(bits)
    blocks = blocks.reshape((2,) * count + blocks.shape[1:])
    ranked = sorted(bits, reverse=True)
    for k, bit in enumerate(ranked):
        blocks = jnp.where(here // bit % 2 == 1, jnp.flip(blocks, k), blocks)
    axes = [ranked.index(bit) for bit in bits]
    blocks = blocks.transpose(axes + list(range(count, blocks.ndim)))
    return blocks.reshape((1 << count,) + blocks.shape[count:])


def group_messages(own, crossed):
    if lax.axis_size("shard") != 2:
        both = lax.all_gather(jnp.concatenate([own, crossed], 0), "shard", axis=0, tiled=True)
        return [both]
    return [own, crossed, swap(own), swap(crossed)]


def product_kernel(rows, group, sources, order_ref, *refs):
    lefts, rights = refs[:sources], refs[sources : 2 * sources]
    kept_ref, sent_ref, picked_ref, turned_ref = refs[2 * sources :]
    count = order_ref.shape[0]
    padded = picked_ref.shape[0] // count
    left_columns = lefts[0].shape[1]

    def turn(block, place):
        start = 0
        columns = pl.ds(pl.multiple_of(block * group, group), group) if group < left_columns else slice(None)
        for left_ref in lefts:
            tokens = left_ref.shape[0]
            turned_ref[place * group : (place + 1) * group, start : start + tokens] = (
                left_ref[:, columns].astype(F32).T
            )
            start += tokens

    @pl.when(pl.program_id(0) == 0)
    def _():
        if padded > rows:
            picked_ref[...] = jnp.zeros_like(picked_ref)
        if group == left_columns:
            turn(0, 0)
        for j in range(count):
            if group < left_columns:
                turn(order_ref[j] * rows // group, j)
                start = pl.multiple_of(j * group + order_ref[j] * rows % group, rows)
            else:
                start = pl.multiple_of(order_ref[j] * rows, rows)
            picked_ref[j * padded : j * padded + rows, :] = turned_ref[
                pl.ds(start, rows), :
            ].astype(picked_ref.dtype)

    half = kept_ref.shape[0]
    right = jnp.concatenate([right_ref[...] for right_ref in rights], 0)
    kept_ref[...] = dot(picked_ref[:half, :].astype(BF), right).astype(kept_ref.dtype)
    sent_ref[...] = dot(picked_ref[half:, :].astype(BF), right).astype(sent_ref.dtype)


def product_halves(lefts, left_part, rights, right_part, bits):
    (left_start, left_columns), (start, columns) = left_part, right_part
    shards = lax.axis_size("shard")
    rows = left_columns // (lax.axis_size("expert") * shards)
    padded = -(-rows // 16) * 16
    order = (
        lax.axis_index("expert") ^ jnp.array(fold_order(bits), jnp.int32)
    ) * shards + lax.axis_index("shard")
    count = 1 << len(bits)
    half = count * padded // 2
    tokens = sum(left.shape[0] for left in lefts)
    if rows % 8:
        left = jnp.concatenate(
            [left[:, left_start : left_start + left_columns] for left in lefts], 0
        )
        right = jnp.concatenate([right[:, start : start + columns] for right in rights], 0)
        blocks = left.T.reshape(-1, shards, rows, tokens)
        blocks = lax.dynamic_index_in_dim(blocks, lax.axis_index("shard"), 1, keepdims=False)
        others = [bit for bit in (1, 2, 4, 8) if bit not in bits]
        picked = differing(blocks, (*others, *bits), lax.axis_index("expert"))[:count]
        picked = jnp.pad(picked, ((0, 0), (0, padded - rows), (0, 0))).reshape(-1, tokens)
        product = dot(picked, right).astype(BF)
        return product[:half], product[half:], picked
    tile = next(t for t in (2048, 1536, 1024, 512, 384, 256, 128) if columns % t == 0 and start % t == 0)
    group = rows * shards if rows * shards % 128 == 0 else left_columns
    turned = left_columns if group == left_columns else count * group
    return pl.pallas_call(
        functools.partial(product_kernel, rows, group, len(lefts)),
        grid_spec=pltpu.PrefetchScalarGridSpec(
            num_scalar_prefetch=1,
            grid=(columns // tile,),
            in_specs=[
                pl.BlockSpec(
                    (left.shape[0], left_columns),
                    lambda i, order: (0, left_start // left_columns),
                )
                for left in lefts
            ]
            + [
                pl.BlockSpec((right.shape[0], tile), lambda i, order: (0, i + start // tile))
                for right in rights
            ],
            out_specs=[
                pl.BlockSpec((half, tile), lambda i, order: (0, i)),
                pl.BlockSpec((half, tile), lambda i, order: (0, i)),
                pl.BlockSpec((count * padded, tokens), lambda i, order: (0, 0)),
            ],
            scratch_shapes=[pltpu.VMEM((turned, tokens), F32)],
        ),
        out_shape=[
            jax.ShapeDtypeStruct((half, columns), BF),
            jax.ShapeDtypeStruct((half, columns), BF),
            jax.ShapeDtypeStruct((count * padded, tokens), F32 if rows % 16 else BF),
        ],
        compiler_params=pltpu.CompilerParams(vmem_limit_bytes=56 << 20),
        cost_estimate=pl.CostEstimate(
            flops=4 * half * tokens * columns,
            bytes_accessed=4 * half * columns + 2 * tokens * (left_columns + columns),
            transcendentals=0,
        ),
    )(order.astype(jnp.int32), *lefts, *rights)


def pair_partial(partial, bits):
    experts, shards = lax.axis_size("expert"), lax.axis_size("shard")
    rows = partial.shape[0] // (experts * shards)
    if shards != 2:
        blocks = partial.reshape(experts, shards, rows, -1)
        total = lax.psum_scatter(blocks, "shard", scatter_dimension=1, tiled=True)[:, 0]
    else:
        own = lax.axis_index("shard")
        blocks = partial.reshape(experts, 2, rows, -1)
        kept = lax.dynamic_index_in_dim(blocks, own, 1, keepdims=False)
        sent = lax.dynamic_index_in_dim(blocks, 1 - own, 1, keepdims=False)
        total = (kept.astype(F32) + swap(sent).astype(F32)).astype(partial.dtype)
    return [differing(total, bits, lax.axis_index("expert")).reshape(experts * rows, -1)]


def line_places():
    return range(4, lax.axis_size("expert"), 4)


def partner(place):
    here = lax.axis_index("expert")
    there = here
    bit = 1
    while bit <= place:
        if place & bit:
            there = there + bit * (1 - 2 * (here // bit % 2))
        bit *= 2
    return there, lax.axis_index("shard")


def greet(places):
    barrier = pltpu.get_barrier_semaphore()
    for place in places:
        pl.semaphore_signal(
            barrier, inc=1, device_id=partner(place), device_id_type=pl.DeviceIdType.MESH
        )
    pl.semaphore_wait(barrier, len(places))


def slot_parts(rows):
    plane, line = (1, 2, 3), tuple(line_places())
    cut = rows // 4
    return (pl.ds(cut, rows - cut), line, plane), (pl.ds(0, cut), plane, line)


def gather_kernel(own_ref, out_ref, send_sems, recv_sems):
    parts = slot_parts(own_ref.shape[0])

    def send(k, rows, block, place):
        copy = pltpu.make_async_remote_copy(
            src_ref=out_ref.at[block, rows],
            dst_ref=out_ref.at[block ^ place, rows],
            send_sem=send_sems.at[k, block ^ place],
            recv_sem=recv_sems.at[k, block ^ place],
            device_id=partner(place),
            device_id_type=pl.DeviceIdType.MESH,
        )
        copy.start()
        return copy

    greet((1, 2, 3, *line_places()))
    out_ref[0] = own_ref[...]
    copies = {}
    for k, (rows, first, _) in enumerate(parts):
        for place in first:
            copies[k, place] = send(k, rows, 0, place)
    for k, (rows, _, second) in enumerate(parts):
        for place in second:
            copies[k, place] = send(k, rows, 0, place)
    arrived = set()
    for k in (1, 0):
        rows, first, second = parts[k]
        for block in first:
            copies[k, block].wait_recv()
            arrived.add((k, block))
            for place in second:
                copies[k, block ^ place] = send(k, rows, block, place)
    for key, copy in copies.items():
        copy.wait_send()
        if key not in arrived:
            copy.wait_recv()


def gather_slot(own):
    count = lax.axis_size("expert")
    return pl.pallas_call(
        gather_kernel,
        in_specs=[pl.BlockSpec(memory_space=pltpu.VMEM)],
        out_specs=pl.BlockSpec(memory_space=pltpu.VMEM),
        out_shape=jax.ShapeDtypeStruct((count, *own.shape), own.dtype),
        scratch_shapes=[pltpu.SemaphoreType.DMA((2, count)), pltpu.SemaphoreType.DMA((2, count))],
        compiler_params=pltpu.CompilerParams(
            collective_id=0, has_side_effects=True, vmem_limit_bytes=16 << 20
        ),
        cost_estimate=pl.CostEstimate(
            flops=5 * 10**10, bytes_accessed=4 * count * own.size, transcendentals=0
        ),
    )(own)


def scatter_kernel(part_ref, out_ref, *refs):
    parts = slot_parts(out_ref.shape[0])
    buffers = [refs[7 * k : 7 * k + 7] for k in range(2)]
    greet((1, 2, 3, *line_places()))
    copies = []

    def send(source, target, sems, index, place):
        copy = pltpu.make_async_remote_copy(
            src_ref=source,
            dst_ref=target,
            send_sem=sems[0].at[index],
            recv_sem=sems[1].at[index],
            device_id=partner(place),
            device_id_type=pl.DeviceIdType.MESH,
        )
        copy.start()
        copies.append(copy)
        return copy

    firsts = []
    for (rows, second, first), (first_ref, _, _, *sems) in zip(parts, buffers):
        firsts.append(
            [
                [
                    send(
                        part_ref.at[block ^ place, rows],
                        first_ref.at[k, i],
                        sems[:2],
                        (k, i),
                        place,
                    )
                    for i, place in enumerate(first)
                ]
                for k, block in enumerate((*second, 0))
            ]
        )
    lasts = {}
    for p in (1, 0):
        rows, second, _ = parts[p]
        first_ref, sum_ref, last_ref, *sems = buffers[p]
        for k, block in enumerate((*second, 0)):
            total = part_ref[block, rows, :].astype(F32)
            for i, copy in enumerate(firsts[p][k]):
                copy.wait_recv()
                total = total + first_ref[k, i].astype(F32)
            if block:
                sum_ref[k] = total.astype(sum_ref.dtype)
                lasts[p, k] = send(sum_ref.at[k], last_ref.at[k], sems[2:], k, block)
            else:
                out_ref[rows, :] = total
    for (p, k), copy in lasts.items():
        copy.wait_recv()
        out_ref[parts[p][0], :] += buffers[p][2][k].astype(F32)
    for copy in copies:
        copy.wait_send()


def scatter_slot(part):
    count, rows, columns = part.shape
    lines = count // 4
    cut = rows // 4
    scratch = []
    for height, groups, firsts in ((rows - cut, lines, 3), (cut, 4, lines - 1)):
        scratch += [
            pltpu.VMEM((groups, firsts, height, columns), part.dtype),
            pltpu.VMEM((groups - 1, height, columns), part.dtype),
            pltpu.VMEM((groups - 1, height, columns), part.dtype),
            pltpu.SemaphoreType.DMA((groups, firsts)),
            pltpu.SemaphoreType.DMA((groups, firsts)),
            pltpu.SemaphoreType.DMA((groups - 1,)),
            pltpu.SemaphoreType.DMA((groups - 1,)),
        ]
    return pl.pallas_call(
        scatter_kernel,
        in_specs=[pl.BlockSpec(memory_space=pltpu.VMEM)],
        out_specs=pl.BlockSpec(memory_space=pltpu.VMEM),
        out_shape=jax.ShapeDtypeStruct((rows, columns), F32),
        scratch_shapes=scratch,
        compiler_params=pltpu.CompilerParams(
            collective_id=1, has_side_effects=True, vmem_limit_bytes=24 << 20
        ),
        cost_estimate=pl.CostEstimate(
            flops=5 * 10**10, bytes_accessed=4 * part.size, transcendentals=0
        ),
    )(part)


REDUCE_STEPS = (1, 5, 3, 0, 7, 7, 4, 4, 3, 6, 2, 6, 0, 5, 7, 2,
                5, 2, 6, 7, 0, 3, 0, 4, 1, 2, 5, 3, 7, 1, 2)


def reduce_kernel(plans, steps, *refs):
    refs = list(refs)
    take = lambda count: [refs.pop(0) for _ in range(count)]
    pieces = [take(count) for _, count, _ in plans]
    firsts = [take(1)[0] if split else None for _, _, split in plans]
    outs = take(len(plans))
    sends = [[None if split and t == 0 else take(1)[0] for t in range(len(bits))] for bits, _, split in plans]
    arrivals = [take(len(bits)) for bits, _, _ in plans]
    send_sems, recv_sems = refs
    greet(sorted({bit for bits, _, _ in plans for bit in bits}))
    copies = []

    def add(target, parts, start, count):
        @pl.loop(0, count // 16)
        def _(k):
            here = pl.multiple_of(k * 16, 16)
            total = sum(part[pl.ds(start + here, 16), :].astype(F32) for part in parts)
            target[pl.ds(here, 16), :] = total.astype(target.dtype)

    latest = [None] * len(plans)
    done = [0] * len(plans)
    for g in steps:
        bits, _, split = plans[g]
        t = done[g]
        done[g] += 1
        if t:
            latest[g].wait_recv()
            pieces[g].append(arrivals[g][t - 1])
        if t == len(bits):
            add(outs[g], pieces[g], 0, outs[g].shape[0])
            continue
        count = arrivals[g][t].shape[0]
        source = firsts[g]
        if t or not split:
            source = sends[g][t]
            add(source, pieces[g], count, count)
        copy = pltpu.make_async_remote_copy(
            src_ref=source,
            dst_ref=arrivals[g][t],
            send_sem=send_sems.at[g, t],
            recv_sem=recv_sems.at[g, t],
            device_id=partner(bits[t]),
            device_id_type=pl.DeviceIdType.MESH,
        )
        copy.start()
        copies.append(copy)
        latest[g] = copy
    for copy in copies:
        copy.wait_send()


def reduce_all(groups, steps):
    plans = tuple((bits, len(pieces), first is not None) for bits, pieces, first in groups)
    outs, sends, arrivals = [], [], []
    for bits, pieces, first in groups:
        count, columns = pieces[0].shape
        count = count * (1 if first is None else 2)
        for t in range(len(bits)):
            count = count // 2
            arrivals.append(pltpu.VMEM((count, columns), BF))
            if t or first is None:
                sends.append(pltpu.VMEM((count, columns), BF))
        outs.append(jax.ShapeDtypeStruct((count, columns), F32))
    operands = [piece for _, pieces, _ in groups for piece in pieces]
    operands += [first for _, _, first in groups if first is not None]
    most = max(len(bits) for bits, _, _ in groups)
    in_vmem = pl.BlockSpec(memory_space=pltpu.VMEM)
    return pl.pallas_call(
        functools.partial(reduce_kernel, plans, steps),
        in_specs=[in_vmem] * len(operands),
        out_specs=[in_vmem] * len(outs),
        out_shape=outs,
        scratch_shapes=[
            *sends,
            *arrivals,
            pltpu.SemaphoreType.DMA((len(groups), most)),
            pltpu.SemaphoreType.DMA((len(groups), most)),
        ],
        compiler_params=pltpu.CompilerParams(
            collective_id=2, has_side_effects=True, vmem_limit_bytes=58 << 20
        ),
        cost_estimate=pl.CostEstimate(
            flops=10**11,
            bytes_accessed=4 * sum(operand.size for operand in operands),
            transcendentals=0,
        ),
    )(*operands)


def attend_kernel(
    raw_ref, cosine_ref, sine_ref, expand_ref, keys_ref, bias_ref,
    nope_ref, queries_ref, weights_ref, mixed_ref, out_ref,
):
    rows = raw_ref.shape[0]
    width = HEAD + ROPE
    cosine, sine = cosine_ref[...], sine_ref[...]
    for h in range(2):
        raw = raw_ref[:, h * width : (h + 1) * width]
        nope = raw[:, :HEAD].astype(BF)
        first = raw[:, HEAD : HEAD + ROPE // 2]
        second = raw[:, HEAD + ROPE // 2 :]
        turned = jnp.concatenate(
            [first * cosine - second * sine, second * cosine + first * sine], -1
        )
        nope_ref[:, h * HEAD : (h + 1) * HEAD] = nope
        latent = dot_t(nope, expand_ref[:, 2 * h * HEAD : (2 * h + 1) * HEAD])
        queries_ref[h * rows : (h + 1) * rows, :RANK] = latent.astype(BF)
        queries_ref[h * rows : (h + 1) * rows, RANK:] = turned.astype(BF)
    bias = bias_ref[...]
    for h in range(2):
        part = slice(h * rows, (h + 1) * rows)
        scores = dot_t(queries_ref[part, :], keys_ref[...]) * (HEAD + ROPE) ** -0.5 + bias
        shifted = jnp.exp(scores - jnp.max(scores, -1, keepdims=True))
        total = jnp.sum(shifted, -1, keepdims=True)
        weights_ref[part, :] = (shifted * (1.0 / total)).astype(BF)
    mixed_ref[...] = dot(weights_ref[...], keys_ref[:, :RANK]).astype(BF)
    for h in range(2):
        out_ref[:, h * VHEAD : (h + 1) * VHEAD] = dot(
            mixed_ref[h * rows : (h + 1) * rows, :],
            expand_ref[:, (2 * h + 1) * HEAD : (2 * h + 2) * HEAD],
        ).astype(BF)


def attend(query_raw, cosine, sine, expand, keys, bias):
    rows, slot = bias.shape
    steps = HEADS // 2
    whole = lambda *shape: pl.BlockSpec(shape, lambda i: (0,) * len(shape))
    return pl.pallas_call(
        attend_kernel,
        grid=(steps,),
        in_specs=[
            pl.BlockSpec((rows, 2 * (HEAD + ROPE)), lambda i: (0, i)),
            whole(rows, ROPE // 2),
            whole(rows, ROPE // 2),
            pl.BlockSpec((RANK, 4 * HEAD), lambda i: (0, i)),
            whole(slot, RANK + ROPE),
            whole(rows, slot),
        ],
        out_specs=[
            pl.BlockSpec((rows, 2 * HEAD), lambda i: (0, i)),
            pl.BlockSpec((2 * rows, RANK + ROPE), lambda i: (i, 0)),
            pl.BlockSpec((2 * rows, slot), lambda i: (i, 0)),
            pl.BlockSpec((2 * rows, RANK), lambda i: (i, 0)),
            pl.BlockSpec((rows, 2 * VHEAD), lambda i: (0, i)),
        ],
        out_shape=[
            jax.ShapeDtypeStruct((rows, HEADS * HEAD), BF),
            jax.ShapeDtypeStruct((HEADS * rows, RANK + ROPE), BF),
            jax.ShapeDtypeStruct((HEADS * rows, slot), BF),
            jax.ShapeDtypeStruct((HEADS * rows, RANK), BF),
            jax.ShapeDtypeStruct((rows, HEADS * VHEAD), BF),
        ],
        compiler_params=pltpu.CompilerParams(vmem_limit_bytes=40 << 20),
        cost_estimate=pl.CostEstimate(
            flops=2 * HEADS * rows * slot * (2 * RANK + ROPE),
            bytes_accessed=2 * HEADS * rows * slot,
            transcendentals=HEADS * rows * slot,
        ),
    )(query_raw, cosine, sine, expand, keys, bias)


def attend_back_kernel(
    order_ref, grad_ref, expand_ref, keys_ref, weights_ref, queries_ref, mixed_ref, nope_ref, cosine_ref,
    sine_ref, query_grad_ref, expand_grad_ref, key_out_ref, key_grad_ref, latent_ref, scores_ref,
):
    rows = grad_ref.shape[0]
    width = HEAD + ROPE
    scale = (HEAD + ROPE) ** -0.5

    @pl.when(pl.program_id(0) == 0)
    def _():
        key_grad_ref[...] = jnp.zeros_like(key_grad_ref)

    for h in range(2):
        part = slice(h * rows, (h + 1) * rows)
        grad = grad_ref[:, h * VHEAD : (h + 1) * VHEAD]
        latent_ref[part, :] = dot_t(
            grad, expand_ref[:, (2 * h + 1) * HEAD : (2 * h + 2) * HEAD]
        ).astype(BF)
        arrived = dot_t(latent_ref[part, :], keys_ref[:, :RANK])
        weights = weights_ref[part, :].astype(F32)
        mean = jnp.sum(weights * arrived, -1, keepdims=True)
        scores_ref[part, :] = (weights * (arrived - mean) * scale).astype(BF)
    key_grad_ref[...] += t_dot(queries_ref[...], scores_ref[...])
    key_grad_ref[:RANK, :] += t_dot(latent_ref[...], weights_ref[...])
    cosine, sine = cosine_ref[...], sine_ref[...]
    for h in range(2):
        part = slice(h * rows, (h + 1) * rows)
        query_grad = dot(scores_ref[part, :], keys_ref[...])
        latent = query_grad[:, :RANK].astype(BF)
        key_part = slice(2 * h * HEAD, (2 * h + 1) * HEAD)
        value_part = slice((2 * h + 1) * HEAD, (2 * h + 2) * HEAD)
        nope = dot(latent, expand_ref[:, key_part])
        first = query_grad[:, RANK : RANK + ROPE // 2]
        second = query_grad[:, RANK + ROPE // 2 :]
        query_grad_ref[:, h * width : (h + 1) * width] = jnp.concatenate(
            [nope, first * cosine + second * sine, second * cosine - first * sine], -1
        ).astype(BF)
        key_grad = t_dot(latent, nope_ref[:, h * HEAD : (h + 1) * HEAD]).astype(BF)
        value_grad = t_dot(
            mixed_ref[part, :], grad_ref[:, h * VHEAD : (h + 1) * VHEAD]
        ).astype(BF)
        count = order_ref.shape[0]
        height = RANK // count
        for j in range(count):
            target = pl.ds(pl.multiple_of(order_ref[j] * height, height), height)
            source = slice(j * height, (j + 1) * height)
            expand_grad_ref[target, key_part] = key_grad[source, :]
            expand_grad_ref[target, value_part] = value_grad[source, :]

    @pl.when(pl.program_id(0) == pl.num_programs(0) - 1)
    def _():
        key_out_ref[...] = key_grad_ref[...].T.astype(BF)


def attend_back(grad_out, expand, keys, weights, queries, mixed, nope, cosine, sine, order):
    rows = grad_out.shape[0]
    slot = keys.shape[0]
    whole = lambda *shape: pl.BlockSpec(shape, lambda i, order: (0,) * len(shape))
    return pl.pallas_call(
        attend_back_kernel,
        grid_spec=pltpu.PrefetchScalarGridSpec(
            num_scalar_prefetch=1,
            grid=(HEADS // 2,),
            in_specs=[
            pl.BlockSpec((rows, 2 * VHEAD), lambda i, order: (0, i)),
            pl.BlockSpec((RANK, 4 * HEAD), lambda i, order: (0, i)),
            whole(slot, RANK + ROPE),
            pl.BlockSpec((2 * rows, slot), lambda i, order: (i, 0)),
            pl.BlockSpec((2 * rows, RANK + ROPE), lambda i, order: (i, 0)),
            pl.BlockSpec((2 * rows, RANK), lambda i, order: (i, 0)),
            pl.BlockSpec((rows, 2 * HEAD), lambda i, order: (0, i)),
            whole(rows, ROPE // 2),
            whole(rows, ROPE // 2),
        ],
        out_specs=[
            pl.BlockSpec((rows, 2 * (HEAD + ROPE)), lambda i, order: (0, i)),
            pl.BlockSpec((RANK, 4 * HEAD), lambda i, order: (0, i)),
            whole(slot, RANK + ROPE),
        ],
        scratch_shapes=[
            pltpu.VMEM((RANK + ROPE, slot), F32),
            pltpu.VMEM((2 * rows, RANK), BF),
            pltpu.VMEM((2 * rows, slot), BF),
        ],
        ),
        out_shape=[
            jax.ShapeDtypeStruct((rows, HEADS * (HEAD + ROPE)), BF),
            jax.ShapeDtypeStruct((RANK, 2 * HEADS * HEAD), BF),
            jax.ShapeDtypeStruct((slot, RANK + ROPE), BF),
        ],
        compiler_params=pltpu.CompilerParams(vmem_limit_bytes=48 << 20),
        cost_estimate=pl.CostEstimate(
            flops=2 * HEADS * rows * slot * (3 * RANK + 2 * (RANK + ROPE)),
            bytes_accessed=2 * HEADS * rows * slot,
            transcendentals=0,
        ),
    )(order, grad_out, expand, keys, weights, queries, mixed, nope, cosine, sine)


def expert_kernel(sources, here_ref, rows_ref, router_ref, *refs):
    weights = refs[: 2 * sources]
    (
        row_grad_ref, units_ref, back_ref, gate_ref, logit_grad_ref, total_ref, probs_ref, share_ref,
    ) = refs[2 * sources :]
    step = pl.program_id(0)
    chunks = pl.num_programs(0) // sources

    @pl.when(step == 0)
    def _():
        logits = dot_t(router_ref[...], rows_ref[...])
        powers = jnp.exp(logits - jnp.max(logits, 0, keepdims=True))
        probs = powers / jnp.sum(powers, 0, keepdims=True)
        own = lax.broadcasted_iota(jnp.int32, probs.shape, 0) == here_ref[0]
        probs_ref[...] = probs
        gate_ref[...] = jnp.sum(jnp.where(own, probs, 0.0), 0, keepdims=True)
        share_ref[...] = jnp.zeros_like(share_ref)
        total_ref[...] = jnp.zeros_like(total_ref)

    def work(in_ref, slopes_ref):
        gate = dot_t(in_ref[0], rows_ref[...])
        up = dot_t(in_ref[1], rows_ref[...])
        back = slopes_ref[...]
        sigma = 1.0 / (1.0 + jnp.exp(-gate))
        act = gate * sigma
        units = (act * up).astype(BF)
        units_ref[...] = units
        share_ref[...] += jnp.sum(back * units.astype(F32), 0, keepdims=True)
        back = back * gate_ref[...]
        back_ref[0] = (back * up * (sigma * (1.0 + gate * (1.0 - sigma)))).astype(BF)
        back_ref[1] = (back * act).astype(BF)
        total_ref[...] += t_dot(back_ref[0], in_ref[0])
        total_ref[...] += t_dot(back_ref[1], in_ref[1])

    for k in range(sources):

        @pl.when(step // chunks == k)
        def _(k=k):
            work(weights[2 * k], weights[2 * k + 1])

    @pl.when(step == pl.num_programs(0) - 1)
    def _():
        probs = probs_ref[...]
        own = lax.broadcasted_iota(jnp.int32, probs.shape, 0) == here_ref[0]
        grad = probs * (own.astype(F32) - gate_ref[...]) * share_ref[...]
        logit_grad_ref[...] = grad.astype(BF)
        row_grad_ref[...] = (
            total_ref[...] + t_dot(logit_grad_ref[...], router_ref[...])
        ).astype(BF)


def expert_pass(here, rows, router, weights):
    count, width = rows.shape
    experts = router.shape[0]
    sources = len(weights)
    units = weights[0][1].shape[0]
    tile = next(t for t in (352, 176, 88, 64, 32, 16, units) if units % t == 0)
    chunks = units // tile
    once = pl.Buffered(1)
    in_specs = [
        pl.BlockSpec((count, width), lambda i, h: (0, 0), pipeline_mode=once),
        pl.BlockSpec((experts, width), lambda i, h: (0, 0)),
    ]
    for k in range(sources):
        at = lambda i, k=k: jnp.clip(i - k * chunks, 0, chunks - 1)
        in_specs.append(pl.BlockSpec((2, tile, width), lambda i, h, at=at: (0, at(i), 0)))
        in_specs.append(pl.BlockSpec((tile, count), lambda i, h, at=at: (at(i), 0)))
    return pl.pallas_call(
        functools.partial(expert_kernel, sources),
        grid_spec=pltpu.PrefetchScalarGridSpec(
            num_scalar_prefetch=1,
            grid=(sources * chunks,),
            in_specs=in_specs,
            out_specs=[
                pl.BlockSpec((count, width), lambda i, h: (0, 0), pipeline_mode=once),
                pl.BlockSpec((tile, count), lambda i, h: (i, 0)),
                pl.BlockSpec(
                    (None, 2, tile, count), lambda i, h: (i // chunks, 0, i % chunks, 0)
                ),
                pl.BlockSpec((1, count), lambda i, h: (0, 0)),
                pl.BlockSpec((experts, count), lambda i, h: (0, 0)),
            ],
            scratch_shapes=[
                pltpu.VMEM((count, width), F32),
                pltpu.VMEM((experts, count), F32),
                pltpu.VMEM((1, count), F32),
            ],
        ),
        out_shape=[
            jax.ShapeDtypeStruct((count, width), BF),
            jax.ShapeDtypeStruct((sources * units, count), BF),
            jax.ShapeDtypeStruct((sources, 2, units, count), BF),
            jax.ShapeDtypeStruct((1, count), F32),
            jax.ShapeDtypeStruct((experts, count), BF),
        ],
        compiler_params=pltpu.CompilerParams(vmem_limit_bytes=58 << 20),
        cost_estimate=pl.CostEstimate(
            flops=8 * count * width * sources * units,
            bytes_accessed=4 * (count + sources * units) * width,
            transcendentals=count * sources * units,
        ),
    )(here, rows, router, *[piece for pair in weights for piece in pair])


def per_device(
    tokens,
    lengths,
    routes,
    attn_gain,
    query_weight,
    latent_weight,
    latent_gain,
    expand_weight,
    output_weight,
    ffn_gain,
    router_weight,
    shared_in,
    shared_out,
    expert_in,
    expert_out,
    cotangent,
):
    local_rows = tokens.shape[1]
    model_width = tokens.shape[2]
    owners, shards = lax.axis_size("expert"), lax.axis_size("shard")
    experts_all = router_weight.shape[1]
    assert experts_all == owners
    topk_count = routes.shape[2]
    capacity = max(2, 9 * local_rows * topk_count // (8 * experts_all))
    capacity = -(-capacity // 8) * 8
    here = lax.axis_index("expert")

    query_blocks = row_blocks(query_weight)
    latent_blocks = row_blocks(latent_weight)
    gains = jnp.concatenate([attn_gain, ffn_gain, latent_gain])[None]
    gains = (
        jnp.where(
            lax.axis_index("shard") == 0,
            jnp.concatenate([gains, swap(gains)], 0),
            jnp.concatenate([swap(gains), gains], 0),
        )
        if shards == 2
        else lax.all_gather(gains, "shard", axis=0, tiled=True)
    ).astype(F32)
    cut = attn_gain.shape[0]
    gain_attn = gains[:, :cut].reshape(-1)
    gain_ffn = gains[:, cut : 2 * cut].reshape(-1)
    gain_latent = gains[:, 2 * cut :].reshape(-1)
    expand = whole_rows(expand_weight)
    here_index = here * local_rows + jnp.arange(local_rows, dtype=jnp.int32)
    query_segment, query_position, query_valid = layout(lengths[0], here_index)
    cosine, sine_table = rope_tables(query_position)
    live_rows = query_valid.astype(F32)[:, None]
    grad_out = cotangent[0].astype(F32) * live_rows
    grad_out_low = grad_out.astype(BF)

    expert_ids = jnp.arange(experts_all, dtype=jnp.int32)
    member = jnp.any(routes[0].T[None] == expert_ids[:, None, None], 1)
    token_ids = jnp.arange(local_rows, dtype=jnp.int32)
    earlier = (token_ids[:, None] < token_ids[None, :]).astype(BF)
    rank = dot(member.astype(BF), earlier).astype(jnp.int32)
    place_ids = jnp.arange(capacity, dtype=jnp.int32)
    spread = (
        (member[:, None, :] & (rank[:, None, :] == place_ids[None, :, None]))
        .reshape(experts_all * capacity, local_rows)
        .astype(BF)
    )

    def exchange(rows):
        return lax.all_to_all(
            rows.reshape(owners, capacity, model_width),
            "expert",
            split_axis=0,
            concat_axis=0,
            tiled=True,
        ).reshape(owners * capacity, model_width)


    inputs = tokens[0].astype(F32)
    inverse_attn = rms_scale(inputs)
    normed_attn = inputs * inverse_attn
    attn_in = (normed_attn * gain_attn).astype(BF)
    latent_raw = times(attn_in, latent_blocks)
    latent = latent_raw[:, :RANK]
    inverse_latent = rms_scale(latent)
    normed_latent = latent * inverse_latent
    latent_in = (normed_latent * gain_latent).astype(BF)
    key_rope = rotate(latent_raw[:, RANK:], cosine, sine_table).astype(BF)
    own_keys = jnp.concatenate([latent_in, key_rope], -1)
    expert_in_rows, expert_out_rows = expert_in[0].transpose(1, 2, 0), expert_out[0]
    (
        own_keys, output_weight, router_weight, shared_in, shared_out, expert_in_rows, expert_out_rows,
    ) = together(
        own_keys, output_weight, router_weight, shared_in, shared_out, expert_in_rows, expert_out_rows,
    )
    output_blocks = row_blocks(output_weight)
    router = whole_rows(router_weight)
    shared_out_blocks = row_blocks(shared_out)
    shared_in_blocks = row_blocks(shared_in)
    if shards == 2:
        expert_weights = [
            (expert_in_rows, expert_out_rows),
            (swap(expert_in_rows), swap(expert_out_rows)),
        ]
    else:
        expert_weights = [
            (
                lax.all_gather(expert_in_rows, "shard", axis=1, tiled=True),
                lax.all_gather(expert_out_rows, "shard", axis=0, tiled=True),
            )
        ]

    sent_grads = dot(spread, grad_out_low).astype(BF)
    keys, sent_grads = together(gather_slot(own_keys), sent_grads)
    received_grads = exchange(sent_grads)
    keys = keys.reshape(-1, RANK + ROPE)
    key_index = (
        (here ^ jnp.arange(owners, dtype=jnp.int32))[:, None] * local_rows
        + jnp.arange(local_rows, dtype=jnp.int32)[None, :]
    ).reshape(-1)

    query_raw = times(attn_in, query_blocks)
    key_segment = layout(lengths[0], key_index)[0]
    allowed = (query_segment[:, None] == key_segment[None, :]) & (
        key_index[None, :] <= here_index[:, None]
    )
    bias = jnp.where(allowed, 0.0, MASK_FILL).astype(F32)
    query_nope, queries, attention, mixed_latent, mixed_heads = attend(
        query_raw, cosine, sine_table, expand, keys, bias
    )
    (
        mixed_heads, received_grads, output_blocks, router, shared_in_blocks, shared_out_blocks,
        expert_weights,
    ) = together(
        mixed_heads, received_grads, output_blocks, router, shared_in_blocks, shared_out_blocks,
        expert_weights,
    )
    hidden_state = inputs + times(mixed_heads, output_blocks)
    inverse_ffn = rms_scale(hidden_state)
    normed_ffn = hidden_state * inverse_ffn
    ffn_in = (normed_ffn * gain_ffn).astype(BF)

    received = exchange(dot(spread, ffn_in).astype(BF))
    shared_both = times(ffn_in, shared_in_blocks)
    shared_act, shared_slope = silu_parts(shared_both[:, :FF_S])
    shared_up = shared_both[:, FF_S:]
    shared_hidden = (shared_act * shared_up).astype(BF)
    shared_result = times(shared_hidden, shared_out_blocks)
    grad_shared_hidden = times_back(grad_out_low, shared_out_blocks)
    grad_shared_gate = (grad_shared_hidden * shared_up * shared_slope).astype(BF)
    grad_shared_up = (grad_shared_hidden * shared_act).astype(BF)
    grad_ffn_in = times_back(
        jnp.concatenate([grad_shared_gate, grad_shared_up], -1), shared_in_blocks
    )
    out_slopes = [dot_t(weight_out, received_grads) for _, weight_out in expert_weights]
    out_message = jnp.concatenate([shared_hidden, grad_out_low], 1)
    in_message = jnp.concatenate([ffn_in, grad_shared_gate, grad_shared_up], 1)
    received, shared_result, grad_ffn_in, out_slopes, out_message, in_message = together(
        received, shared_result, grad_ffn_in, out_slopes, out_message, in_message
    )

    early_message = jnp.concatenate([attn_in, mixed_heads], 1)
    received, early_message = together(received, early_message)
    arrived = cross(out_message, 1), cross(in_message, 4), cross(early_message, 2)
    expert_results = expert_pass(
        here[None],
        received,
        router.T,
        [(weight_in, slopes) for (weight_in, _), slopes in zip(expert_weights, out_slopes)],
    )
    row_grads, hidden, hidden_grads, row_gate, row_grad_logits = expert_results

    returned_grads = exchange(row_grads)
    units = expert_weights[0][1].shape[0]
    row_gate = row_gate.reshape(-1, 1)
    weighted_grads = (row_gate * received_grads.astype(F32)).astype(BF)

    def expert_grads(j):
        return (
            dot(hidden_grads[j].reshape(2 * units, -1), received).reshape(2, units, -1),
            dot(hidden[j * units : (j + 1) * units], weighted_grads),
        )

    other_parts = [part.astype(BF) for part in expert_grads(len(expert_weights) - 1)]
    other_parts, arrived = together(other_parts, arrived)
    out_messages = group_messages(out_message, arrived[0])
    in_messages = group_messages(in_message, arrived[1])
    early_messages = group_messages(early_message, arrived[2])
    cut = 4096
    shared_halves = [
        product_halves(messages, left_part, messages, right_part, order)[:2]
        for messages, left_part, right_part, order in (
            (out_messages, (0, FF_S), (FF_S, model_width), (2, 8, 4)),
            (in_messages, (0, model_width), (model_width, cut), (1, 2, 8)),
            (in_messages, (0, model_width), (model_width + cut, 2 * FF_S - cut), (2, 1, 8)),
        )
    ]
    hidden, hidden_grads, shared_halves, early_messages = together(
        hidden, hidden_grads, shared_halves, early_messages
    )
    shared_sums = [
        [kept, cross(sent, bit)] for (kept, sent), bit in zip(shared_halves, (2, 1, 2))
    ]
    row_out = 0.0
    for j, (_, weight) in enumerate(expert_weights):
        row_out = row_out + t_dot(hidden[j * units : (j + 1) * units], weight)
    row_out = (row_gate * row_out).astype(BF)
    if shards == 2:
        hidden, hidden_grads, other_parts = together(
            hidden, hidden_grads, [swap(part) for part in other_parts]
        )
        grad_expert_in, grad_expert_out = [
            own + other.astype(F32) for own, other in zip(expert_grads(0), other_parts)
        ]
    else:
        grad_expert_in, grad_expert_out = [
            lax.psum_scatter(part, "shard", scatter_dimension=part.ndim - 2, tiled=True).astype(F32)
            for part in other_parts
        ]
    grad_router = dot(row_grad_logits, received)
    returned_grads, row_out, grad_expert_in, grad_expert_out, grad_router = together(
        returned_grads, row_out, grad_expert_in, grad_expert_out, grad_router
    )
    grad_expert_in = grad_expert_in.transpose(2, 0, 1)[None]
    grad_expert_out = grad_expert_out[None]
    returned = exchange(row_out)
    grad_ffn_in = grad_ffn_in + t_dot(spread, returned_grads)
    grad_gain_ffn = jnp.sum(grad_ffn_in * normed_ffn, 0)
    grad_hidden_state = grad_out + norm_back(grad_ffn_in * gain_ffn, normed_ffn, inverse_ffn)

    grad_attn_out = grad_hidden_state.astype(BF)
    grad_mixed = times_back(grad_attn_out, output_blocks).astype(BF)
    grad_mixed, grad_attn_out = together(grad_mixed, grad_attn_out)
    out_arrived = cross(grad_attn_out, 2)
    expand_order = (2, 1, 4, 8)
    if shards == 2:
        differs = here ^ jnp.arange(owners, dtype=jnp.int32)
        place = sum((differs // bit % 2) << (3 - k) for k, bit in enumerate(expand_order))
        other = lax.axis_index("shard") ^ jnp.arange(2, dtype=jnp.int32)
        block_order = (other[None, :] * owners + place[:, None]).reshape(-1).astype(jnp.int32)
    else:
        block_order = jnp.zeros((1,), jnp.int32)
    attention_grads = attend_back(
        grad_mixed,
        expand,
        keys,
        attention,
        queries,
        mixed_latent,
        query_nope,
        cosine,
        sine_table,
        block_order,
    )
    attention_grads, shared_sums, out_arrived = together(
        attention_grads, shared_sums, out_arrived
    )
    grad_query_raw, grad_expand, grad_keys = attention_grads

    query_arrived = cross(grad_query_raw, 2)
    own_query = grad_query_raw
    if shards == 2:
        half_rank = RANK // 2
        expand_pair = [grad_expand[:half_rank], swap(grad_expand[half_rank:])]
    else:
        expand_pair = pair_partial(grad_expand, expand_order)
    grad_own_keys, returned, query_arrived, grad_query_raw, expand_pair = together(
        scatter_slot(grad_keys.reshape(owners, local_rows, -1)),
        returned,
        query_arrived,
        grad_query_raw,
        expand_pair,
    )
    grad_latent_in = grad_own_keys[:, :RANK]
    grad_gain_latent = jnp.sum(grad_latent_in * normed_latent, 0)
    grad_latent = norm_back(grad_latent_in * gain_latent, normed_latent, inverse_latent)
    grad_latent_raw = jnp.concatenate(
        [grad_latent, rotate_back(grad_own_keys[:, RANK:], cosine, sine_table)], -1
    ).astype(BF)
    latent_message = jnp.pad(grad_latent_raw, ((0, 0), (0, -grad_latent_raw.shape[1] % 128)))
    latent_messages = group_messages(latent_message, cross(latent_message, 2))
    query_messages = group_messages(own_query, query_arrived)
    out_messages = group_messages(grad_attn_out, out_arrived)
    in_part, heads_part = (0, model_width), (model_width, HEADS * VHEAD)
    whole_part = lambda array: (0, array.shape[1])
    *query_halves, picked = product_halves(
        early_messages, in_part, query_messages, whole_part(grad_query_raw), (1, 4, 8)
    )
    output_halves = product_halves(
        early_messages, heads_part, out_messages, whole_part(grad_attn_out), (4, 1, 8)
    )[:2]
    latent_product = dot(picked, jnp.concatenate(latent_messages, 0)).astype(BF)
    latent_halves = jnp.split(latent_product, 2, 0)
    grad_attn_in = times_back(grad_latent_raw, latent_blocks) + times_back(
        grad_query_raw, query_blocks
    )
    grad_gain_attn = jnp.sum(grad_attn_in * normed_attn, 0)
    tokens_grad = grad_hidden_state + norm_back(grad_attn_in * gain_attn, normed_attn, inverse_attn)
    devices = owners * shards
    rows = model_width // devices
    small = jnp.concatenate(
        [
            vector.reshape(devices, -1)
            for vector in (grad_router.T, grad_gain_attn, grad_gain_ffn, grad_gain_latent)
        ],
        1,
    )
    cuts = [rows * experts_all, rows * (experts_all + 1), rows * (experts_all + 2)]
    small = jnp.pad(small, ((0, 0), (0, -small.shape[1] % 2048))).reshape(devices * 16, -1)
    small_pair = pair_partial(small.astype(BF), expand_order)
    sums = reduce_all(
        [
            ((1, 4, 8), [latent_halves[0]], latent_halves[1]),
            ((8, 4), shared_sums[0], None),
            (expand_order, expand_pair, None),
            ((1, 4, 8), [query_halves[0]], query_halves[1]),
            ((2, 8), shared_sums[1], None),
            ((4, 1, 8), [output_halves[0]], output_halves[1]),
            ((1, 8), shared_sums[2], None),
            (expand_order, small_pair, None),
        ],
        REDUCE_STEPS,
    )
    grad_latent_weight = sums[0][:, : RANK + ROPE]
    grad_shared_out = sums[1][: FF_S // devices]
    grad_expand, grad_query = sums[2:4]
    grad_shared_in = jnp.concatenate([sums[4], sums[6]], 1)
    grad_output = sums[5]
    small = sums[7].reshape(-1)
    routed = t_dot(spread, returned)
    block_result = hidden_state + shared_result + routed
    return (
        block_result.astype(BF)[None],
        tokens_grad.astype(BF)[None],
        small[cuts[0] : cuts[1]],
        grad_query,
        grad_latent_weight,
        small[cuts[2] : cuts[2] + RANK // devices],
        grad_expand,
        grad_output,
        small[cuts[1] : cuts[2]],
        small[: cuts[0]].reshape(rows, experts_all),
        grad_shared_in,
        grad_shared_out,
        grad_expert_in,
        grad_expert_out,
    )


def solution(mesh):
    return jax.shard_map(
        per_device,
        mesh=mesh,
        in_specs=(
            P("shard", "expert", None),
            P("shard", None),
            P("shard", "expert", None),
            P("shard"),
            P("shard", None),
            P("shard", None),
            P("shard"),
            P("shard", None),
            P("shard", None),
            P("shard"),
            P("shard", None),
            P("shard", None),
            P("shard", None),
            P("expert", None, None, "shard"),
            P("expert", "shard", None),
            P("shard", "expert", None),
        ),
        out_specs=(
            P("shard", "expert", None),
            P("shard", "expert", None),
            P(("expert", "shard")),
            P(("expert", "shard"), None),
            P(("expert", "shard"), None),
            P(("expert", "shard")),
            P(("expert", "shard"), None),
            P(("expert", "shard"), None),
            P(("expert", "shard")),
            P(("expert", "shard"), None),
            P(("expert", "shard"), None),
            P(("expert", "shard"), None),
            P("expert", None, None, "shard"),
            P("expert", "shard", None),
        ),
        check_vma=False,
    )
```

```python
import functools

import jax
import jax.numpy as jnp
from jax import lax
from jax.experimental import pallas as pl
from jax.experimental.pallas import tpu as pltpu
from jax.sharding import PartitionSpec as P

HEADS = 16
HEAD = 128
ROPE = 64
VHEAD = 128
RANK = 512
FF_S = 2816
SLOT = 2048

EPS = 1e-06
MASK_FILL = -1e30
BF = jnp.bfloat16
F32 = jnp.float32


def layout(lengths_slot, slot_index):
    first_len = lengths_slot[0]
    second_end = first_len + lengths_slot[1]
    segment = (slot_index >= first_len).astype(jnp.int32) + (slot_index >= second_end).astype(
        jnp.int32
    )
    seq_start = jnp.where(segment == 0, 0, jnp.where(segment == 1, first_len, second_end))
    return (segment, slot_index - seq_start, slot_index < second_end)


def rope_tables(positions):
    half_width = ROPE // 2
    inverse = 10000.0 ** (-jnp.arange(half_width, dtype=F32) / half_width)
    angles = positions.astype(F32)[:, None] * inverse[None, :]
    return (jnp.cos(angles), jnp.sin(angles))


def rotate(values, cosine, sine_table):
    half_width = values.shape[-1] // 2
    first_half = values[..., :half_width]
    second_half = values[..., half_width:]
    return jnp.concatenate(
        [
            first_half * cosine - second_half * sine_table,
            second_half * cosine + first_half * sine_table,
        ],
        -1,
    )


def rotate_back(grads_in, cosine, sine_table):
    return rotate(grads_in, cosine, -sine_table)


def silu_parts(gate_in):
    sigma = jax.nn.sigmoid(gate_in)
    return (gate_in * sigma, sigma * (1.0 + gate_in * (1.0 - sigma)))


def rms_scale(values):
    return lax.rsqrt(jnp.mean(values * values, -1, keepdims=True) + EPS)


def norm_back(grad_in, normed, inverse):
    return inverse * (grad_in - normed * jnp.mean(grad_in * normed, -1, keepdims=True))


def dot(left, right):
    return jnp.dot(left, right, preferred_element_type=F32)


def dot_t(left, right):
    return lax.dot_general(left, right, (((1,), (1,)), ((), ())), preferred_element_type=F32)


def t_dot(left, right):
    return lax.dot_general(left, right, (((0,), (0,)), ((), ())), preferred_element_type=F32)


def cross(values, bit):
    count = lax.axis_size("expert")
    return lax.ppermute(values, "expert", [(i, i ^ bit) for i in range(count)])


def swap(values):
    return lax.ppermute(values, "shard", [(0, 1), (1, 0)])


def whole_rows(weight):
    if lax.axis_size("shard") != 2:
        return lax.all_gather(weight, "shard", axis=0, tiled=True)
    other = swap(weight)
    first = lax.axis_index("shard") == 0
    return jnp.where(
        first, jnp.concatenate([weight, other], 0), jnp.concatenate([other, weight], 0)
    )


def row_blocks(weight):
    count = lax.axis_size("shard")
    if count == 2:
        own = lax.axis_index("shard")
        return [(own, weight), (1 - own, swap(weight))]
    blocks = lax.all_gather(weight, "shard", axis=0)
    return [(j, blocks[j]) for j in range(count)]


def times(values, blocks):
    rows = blocks[0][1].shape[0]
    return sum(
        dot(lax.dynamic_slice_in_dim(values, place * rows, rows, 1), block)
        for place, block in blocks
    )


def times_back(grads, blocks):
    pieces = [dot_t(grads, block) for _, block in blocks]
    if len(pieces) != 2:
        return jnp.concatenate(pieces, 1)
    first = lax.axis_index("shard") == 0
    return jnp.where(first, jnp.concatenate(pieces, 1), jnp.concatenate(pieces[::-1], 1))


def together(*values):
    leaves, tree = jax.tree.flatten(values)
    return jax.tree.unflatten(tree, lax.optimization_barrier(leaves))


def fold_order(bits):
    places = [0]
    for bit in reversed(bits):
        places = places + [place ^ bit for place in places]
    return places


def differing(blocks, bits, here):
    count = len(bits)
    blocks = blocks.reshape((2,) * count + blocks.shape[1:])
    ranked = sorted(bits, reverse=True)
    for k, bit in enumerate(ranked):
        blocks = jnp.where(here // bit % 2 == 1, jnp.flip(blocks, k), blocks)
    axes = [ranked.index(bit) for bit in bits]
    blocks = blocks.transpose(axes + list(range(count, blocks.ndim)))
    return blocks.reshape((1 << count,) + blocks.shape[count:])


def group_messages(own, crossed):
    if lax.axis_size("shard") != 2:
        both = lax.all_gather(jnp.concatenate([own, crossed], 0), "shard", axis=0, tiled=True)
        return [both]
    return [own, crossed, swap(own), swap(crossed)]


def product_kernel(rows, group, sources, order_ref, *refs):
    lefts, rights = refs[:sources], refs[sources : 2 * sources]
    kept_ref, sent_ref, picked_ref, turned_ref = refs[2 * sources :]
    count = order_ref.shape[0]
    padded = picked_ref.shape[0] // count
    left_columns = lefts[0].shape[1]

    def turn(block, place):
        start = 0
        columns = pl.ds(pl.multiple_of(block * group, group), group) if group < left_columns else slice(None)
        for left_ref in lefts:
            tokens = left_ref.shape[0]
            turned_ref[place * group : (place + 1) * group, start : start + tokens] = (
                left_ref[:, columns].astype(F32).T
            )
            start += tokens

    @pl.when(pl.program_id(0) == 0)
    def _():
        if padded > rows:
            picked_ref[...] = jnp.zeros_like(picked_ref)
        if group == left_columns:
            turn(0, 0)
        for j in range(count):
            if group < left_columns:
                turn(order_ref[j] * rows // group, j)
                start = pl.multiple_of(j * group + order_ref[j] * rows % group, rows)
            else:
                start = pl.multiple_of(order_ref[j] * rows, rows)
            picked_ref[j * padded : j * padded + rows, :] = turned_ref[
                pl.ds(start, rows), :
            ].astype(picked_ref.dtype)

    half = kept_ref.shape[0]
    right = jnp.concatenate([right_ref[...] for right_ref in rights], 0)
    kept_ref[...] = dot(picked_ref[:half, :].astype(BF), right).astype(kept_ref.dtype)
    sent_ref[...] = dot(picked_ref[half:, :].astype(BF), right).astype(sent_ref.dtype)


def product_halves(lefts, left_part, rights, right_part, bits):
    (left_start, left_columns), (start, columns) = left_part, right_part
    shards = lax.axis_size("shard")
    rows = left_columns // (lax.axis_size("expert") * shards)
    padded = -(-rows // 16) * 16
    order = (
        lax.axis_index("expert") ^ jnp.array(fold_order(bits), jnp.int32)
    ) * shards + lax.axis_index("shard")
    count = 1 << len(bits)
    half = count * padded // 2
    tokens = sum(left.shape[0] for left in lefts)
    if rows % 8:
        left = jnp.concatenate(
            [left[:, left_start : left_start + left_columns] for left in lefts], 0
        )
        right = jnp.concatenate([right[:, start : start + columns] for right in rights], 0)
        blocks = left.T.reshape(-1, shards, rows, tokens)
        blocks = lax.dynamic_index_in_dim(blocks, lax.axis_index("shard"), 1, keepdims=False)
        others = [bit for bit in (1, 2, 4, 8) if bit not in bits]
        picked = differing(blocks, (*others, *bits), lax.axis_index("expert"))[:count]
        picked = jnp.pad(picked, ((0, 0), (0, padded - rows), (0, 0))).reshape(-1, tokens)
        product = dot(picked, right).astype(BF)
        return product[:half], product[half:], picked
    tile = next(t for t in (2048, 1536, 1024, 512, 384, 256, 128) if columns % t == 0 and start % t == 0)
    group = rows * shards if rows * shards % 128 == 0 else left_columns
    turned = left_columns if group == left_columns else count * group
    return pl.pallas_call(
        functools.partial(product_kernel, rows, group, len(lefts)),
        grid_spec=pltpu.PrefetchScalarGridSpec(
            num_scalar_prefetch=1,
            grid=(columns // tile,),
            in_specs=[
                pl.BlockSpec(
                    (left.shape[0], left_columns),
                    lambda i, order: (0, left_start // left_columns),
                )
                for left in lefts
            ]
            + [
                pl.BlockSpec((right.shape[0], tile), lambda i, order: (0, i + start // tile))
                for right in rights
            ],
            out_specs=[
                pl.BlockSpec((half, tile), lambda i, order: (0, i)),
                pl.BlockSpec((half, tile), lambda i, order: (0, i)),
                pl.BlockSpec((count * padded, tokens), lambda i, order: (0, 0)),
            ],
            scratch_shapes=[pltpu.VMEM((turned, tokens), F32)],
        ),
        out_shape=[
            jax.ShapeDtypeStruct((half, columns), BF),
            jax.ShapeDtypeStruct((half, columns), BF),
            jax.ShapeDtypeStruct((count * padded, tokens), F32 if rows % 16 else BF),
        ],
        compiler_params=pltpu.CompilerParams(vmem_limit_bytes=56 << 20),
        cost_estimate=pl.CostEstimate(
            flops=4 * half * tokens * columns,
            bytes_accessed=4 * half * columns + 2 * tokens * (left_columns + columns),
            transcendentals=0,
        ),
    )(order.astype(jnp.int32), *lefts, *rights)


def pair_partial(partial, bits):
    experts, shards = lax.axis_size("expert"), lax.axis_size("shard")
    rows = partial.shape[0] // (experts * shards)
    if shards != 2:
        blocks = partial.reshape(experts, shards, rows, -1)
        total = lax.psum_scatter(blocks, "shard", scatter_dimension=1, tiled=True)[:, 0]
    else:
        own = lax.axis_index("shard")
        blocks = partial.reshape(experts, 2, rows, -1)
        kept = lax.dynamic_index_in_dim(blocks, own, 1, keepdims=False)
        sent = lax.dynamic_index_in_dim(blocks, 1 - own, 1, keepdims=False)
        total = (kept.astype(F32) + swap(sent).astype(F32)).astype(partial.dtype)
    return [differing(total, bits, lax.axis_index("expert")).reshape(experts * rows, -1)]


def line_places():
    return range(4, lax.axis_size("expert"), 4)


def partner(place):
    here = lax.axis_index("expert")
    there = here
    bit = 1
    while bit <= place:
        if place & bit:
            there = there + bit * (1 - 2 * (here // bit % 2))
        bit *= 2
    return there, lax.axis_index("shard")


def greet(places):
    barrier = pltpu.get_barrier_semaphore()
    for place in places:
        pl.semaphore_signal(
            barrier, inc=1, device_id=partner(place), device_id_type=pl.DeviceIdType.MESH
        )
    pl.semaphore_wait(barrier, len(places))


def slot_parts(rows):
    plane, line = (1, 2, 3), tuple(line_places())
    cut = rows // 4
    return (pl.ds(cut, rows - cut), line, plane), (pl.ds(0, cut), plane, line)


def gather_kernel(own_ref, out_ref, send_sems, recv_sems):
    parts = slot_parts(own_ref.shape[0])

    def send(k, rows, block, place):
        copy = pltpu.make_async_remote_copy(
            src_ref=out_ref.at[block, rows],
            dst_ref=out_ref.at[block ^ place, rows],
            send_sem=send_sems.at[k, block ^ place],
            recv_sem=recv_sems.at[k, block ^ place],
            device_id=partner(place),
            device_id_type=pl.DeviceIdType.MESH,
        )
        copy.start()
        return copy

    greet((1, 2, 3, *line_places()))
    out_ref[0] = own_ref[...]
    copies = {}
    for k, (rows, first, _) in enumerate(parts):
        for place in first:
            copies[k, place] = send(k, rows, 0, place)
    for k, (rows, _, second) in enumerate(parts):
        for place in second:
            copies[k, place] = send(k, rows, 0, place)
    arrived = set()
    for k in (1, 0):
        rows, first, second = parts[k]
        for block in first:
            copies[k, block].wait_recv()
            arrived.add((k, block))
            for place in second:
                copies[k, block ^ place] = send(k, rows, block, place)
    for key, copy in copies.items():
        copy.wait_send()
        if key not in arrived:
            copy.wait_recv()


def gather_slot(own):
    count = lax.axis_size("expert")
    return pl.pallas_call(
        gather_kernel,
        in_specs=[pl.BlockSpec(memory_space=pltpu.VMEM)],
        out_specs=pl.BlockSpec(memory_space=pltpu.VMEM),
        out_shape=jax.ShapeDtypeStruct((count, *own.shape), own.dtype),
        scratch_shapes=[pltpu.SemaphoreType.DMA((2, count)), pltpu.SemaphoreType.DMA((2, count))],
        compiler_params=pltpu.CompilerParams(
            collective_id=0, has_side_effects=True, vmem_limit_bytes=16 << 20
        ),
        cost_estimate=pl.CostEstimate(
            flops=5 * 10**10, bytes_accessed=4 * count * own.size, transcendentals=0
        ),
    )(own)


def scatter_kernel(part_ref, out_ref, *refs):
    parts = slot_parts(out_ref.shape[0])
    buffers = [refs[7 * k : 7 * k + 7] for k in range(2)]
    greet((1, 2, 3, *line_places()))
    copies = []

    def send(source, target, sems, index, place):
        copy = pltpu.make_async_remote_copy(
            src_ref=source,
            dst_ref=target,
            send_sem=sems[0].at[index],
            recv_sem=sems[1].at[index],
            device_id=partner(place),
            device_id_type=pl.DeviceIdType.MESH,
        )
        copy.start()
        copies.append(copy)
        return copy

    firsts = []
    for (rows, second, first), (first_ref, _, _, *sems) in zip(parts, buffers):
        firsts.append(
            [
                [
                    send(
                        part_ref.at[block ^ place, rows],
                        first_ref.at[k, i],
                        sems[:2],
                        (k, i),
                        place,
                    )
                    for i, place in enumerate(first)
                ]
                for k, block in enumerate((*second, 0))
            ]
        )
    lasts = {}
    for p in (1, 0):
        rows, second, _ = parts[p]
        first_ref, sum_ref, last_ref, *sems = buffers[p]
        for k, block in enumerate((*second, 0)):
            total = part_ref[block, rows, :].astype(F32)
            for i, copy in enumerate(firsts[p][k]):
                copy.wait_recv()
                total = total + first_ref[k, i].astype(F32)
            if block:
                sum_ref[k] = total.astype(sum_ref.dtype)
                lasts[p, k] = send(sum_ref.at[k], last_ref.at[k], sems[2:], k, block)
            else:
                out_ref[rows, :] = total
    for (p, k), copy in lasts.items():
        copy.wait_recv()
        out_ref[parts[p][0], :] += buffers[p][2][k].astype(F32)
    for copy in copies:
        copy.wait_send()


def scatter_slot(part):
    count, rows, columns = part.shape
    lines = count // 4
    cut = rows // 4
    scratch = []
    for height, groups, firsts in ((rows - cut, lines, 3), (cut, 4, lines - 1)):
        scratch += [
            pltpu.VMEM((groups, firsts, height, columns), part.dtype),
            pltpu.VMEM((groups - 1, height, columns), part.dtype),
            pltpu.VMEM((groups - 1, height, columns), part.dtype),
            pltpu.SemaphoreType.DMA((groups, firsts)),
            pltpu.SemaphoreType.DMA((groups, firsts)),
            pltpu.SemaphoreType.DMA((groups - 1,)),
            pltpu.SemaphoreType.DMA((groups - 1,)),
        ]
    return pl.pallas_call(
        scatter_kernel,
        in_specs=[pl.BlockSpec(memory_space=pltpu.VMEM)],
        out_specs=pl.BlockSpec(memory_space=pltpu.VMEM),
        out_shape=jax.ShapeDtypeStruct((rows, columns), F32),
        scratch_shapes=scratch,
        compiler_params=pltpu.CompilerParams(
            collective_id=1, has_side_effects=True, vmem_limit_bytes=24 << 20
        ),
        cost_estimate=pl.CostEstimate(
            flops=5 * 10**10, bytes_accessed=4 * part.size, transcendentals=0
        ),
    )(part)


REDUCE_STEPS = (1, 5, 3, 0, 7, 7, 4, 4, 3, 6, 2, 6, 0, 5, 7, 2,
                5, 2, 6, 7, 0, 3, 0, 4, 1, 2, 5, 3, 7, 1, 2)


def reduce_kernel(plans, steps, *refs):
    refs = list(refs)
    take = lambda count: [refs.pop(0) for _ in range(count)]
    pieces = [take(count) for _, count, _ in plans]
    firsts = [take(1)[0] if split else None for _, _, split in plans]
    outs = take(len(plans))
    sends = [[None if split and t == 0 else take(1)[0] for t in range(len(bits))] for bits, _, split in plans]
    arrivals = [take(len(bits)) for bits, _, _ in plans]
    send_sems, recv_sems = refs
    greet(sorted({bit for bits, _, _ in plans for bit in bits}))
    copies = []

    def add(target, parts, start, count):
        @pl.loop(0, count // 16)
        def _(k):
            here = pl.multiple_of(k * 16, 16)
            total = sum(part[pl.ds(start + here, 16), :].astype(F32) for part in parts)
            target[pl.ds(here, 16), :] = total.astype(target.dtype)

    latest = [None] * len(plans)
    done = [0] * len(plans)
    for g in steps:
        bits, _, split = plans[g]
        t = done[g]
        done[g] += 1
        if t:
            latest[g].wait_recv()
            pieces[g].append(arrivals[g][t - 1])
        if t == len(bits):
            add(outs[g], pieces[g], 0, outs[g].shape[0])
            continue
        count = arrivals[g][t].shape[0]
        source = firsts[g]
        if t or not split:
            source = sends[g][t]
            add(source, pieces[g], count, count)
        copy = pltpu.make_async_remote_copy(
            src_ref=source,
            dst_ref=arrivals[g][t],
            send_sem=send_sems.at[g, t],
            recv_sem=recv_sems.at[g, t],
            device_id=partner(bits[t]),
            device_id_type=pl.DeviceIdType.MESH,
        )
        copy.start()
        copies.append(copy)
        latest[g] = copy
    for copy in copies:
        copy.wait_send()


def reduce_all(groups, steps):
    plans = tuple((bits, len(pieces), first is not None) for bits, pieces, first in groups)
    outs, sends, arrivals = [], [], []
    for bits, pieces, first in groups:
        count, columns = pieces[0].shape
        count = count * (1 if first is None else 2)
        for t in range(len(bits)):
            count = count // 2
            arrivals.append(pltpu.VMEM((count, columns), BF))
            if t or first is None:
                sends.append(pltpu.VMEM((count, columns), BF))
        outs.append(jax.ShapeDtypeStruct((count, columns), F32))
    operands = [piece for _, pieces, _ in groups for piece in pieces]
    operands += [first for _, _, first in groups if first is not None]
    most = max(len(bits) for bits, _, _ in groups)
    in_vmem = pl.BlockSpec(memory_space=pltpu.VMEM)
    return pl.pallas_call(
        functools.partial(reduce_kernel, plans, steps),
        in_specs=[in_vmem] * len(operands),
        out_specs=[in_vmem] * len(outs),
        out_shape=outs,
        scratch_shapes=[
            *sends,
            *arrivals,
            pltpu.SemaphoreType.DMA((len(groups), most)),
            pltpu.SemaphoreType.DMA((len(groups), most)),
        ],
        compiler_params=pltpu.CompilerParams(
            collective_id=2, has_side_effects=True, vmem_limit_bytes=58 << 20
        ),
        cost_estimate=pl.CostEstimate(
            flops=10**11,
            bytes_accessed=4 * sum(operand.size for operand in operands),
            transcendentals=0,
        ),
    )(*operands)


def attend_kernel(
    raw_ref, cosine_ref, sine_ref, expand_ref, keys_ref, bias_ref,
    nope_ref, queries_ref, weights_ref, mixed_ref, out_ref,
):
    rows = raw_ref.shape[0]
    width = HEAD + ROPE
    cosine, sine = cosine_ref[...], sine_ref[...]
    for h in range(2):
        raw = raw_ref[:, h * width : (h + 1) * width]
        nope = raw[:, :HEAD].astype(BF)
        first = raw[:, HEAD : HEAD + ROPE // 2]
        second = raw[:, HEAD + ROPE // 2 :]
        turned = jnp.concatenate(
            [first * cosine - second * sine, second * cosine + first * sine], -1
        )
        nope_ref[:, h * HEAD : (h + 1) * HEAD] = nope
        latent = dot_t(nope, expand_ref[:, 2 * h * HEAD : (2 * h + 1) * HEAD])
        queries_ref[h * rows : (h + 1) * rows, :RANK] = latent.astype(BF)
        queries_ref[h * rows : (h + 1) * rows, RANK:] = turned.astype(BF)
    bias = bias_ref[...]
    for h in range(2):
        part = slice(h * rows, (h + 1) * rows)
        scores = dot_t(queries_ref[part, :], keys_ref[...]) * (HEAD + ROPE) ** -0.5 + bias
        shifted = jnp.exp(scores - jnp.max(scores, -1, keepdims=True))
        total = jnp.sum(shifted, -1, keepdims=True)
        weights_ref[part, :] = (shifted * (1.0 / total)).astype(BF)
    mixed_ref[...] = dot(weights_ref[...], keys_ref[:, :RANK]).astype(BF)
    for h in range(2):
        out_ref[:, h * VHEAD : (h + 1) * VHEAD] = dot(
            mixed_ref[h * rows : (h + 1) * rows, :],
            expand_ref[:, (2 * h + 1) * HEAD : (2 * h + 2) * HEAD],
        ).astype(BF)


def attend(query_raw, cosine, sine, expand, keys, bias):
    rows, slot = bias.shape
    steps = HEADS // 2
    whole = lambda *shape: pl.BlockSpec(shape, lambda i: (0,) * len(shape))
    return pl.pallas_call(
        attend_kernel,
        grid=(steps,),
        in_specs=[
            pl.BlockSpec((rows, 2 * (HEAD + ROPE)), lambda i: (0, i)),
            whole(rows, ROPE // 2),
            whole(rows, ROPE // 2),
            pl.BlockSpec((RANK, 4 * HEAD), lambda i: (0, i)),
            whole(slot, RANK + ROPE),
            whole(rows, slot),
        ],
        out_specs=[
            pl.BlockSpec((rows, 2 * HEAD), lambda i: (0, i)),
            pl.BlockSpec((2 * rows, RANK + ROPE), lambda i: (i, 0)),
            pl.BlockSpec((2 * rows, slot), lambda i: (i, 0)),
            pl.BlockSpec((2 * rows, RANK), lambda i: (i, 0)),
            pl.BlockSpec((rows, 2 * VHEAD), lambda i: (0, i)),
        ],
        out_shape=[
            jax.ShapeDtypeStruct((rows, HEADS * HEAD), BF),
            jax.ShapeDtypeStruct((HEADS * rows, RANK + ROPE), BF),
            jax.ShapeDtypeStruct((HEADS * rows, slot), BF),
            jax.ShapeDtypeStruct((HEADS * rows, RANK), BF),
            jax.ShapeDtypeStruct((rows, HEADS * VHEAD), BF),
        ],
        compiler_params=pltpu.CompilerParams(vmem_limit_bytes=40 << 20),
        cost_estimate=pl.CostEstimate(
            flops=2 * HEADS * rows * slot * (2 * RANK + ROPE),
            bytes_accessed=2 * HEADS * rows * slot,
            transcendentals=HEADS * rows * slot,
        ),
    )(query_raw, cosine, sine, expand, keys, bias)


def attend_back_kernel(
    order_ref, grad_ref, expand_ref, keys_ref, weights_ref, queries_ref, mixed_ref, nope_ref, cosine_ref,
    sine_ref, query_grad_ref, expand_grad_ref, key_out_ref, key_grad_ref, latent_ref, scores_ref,
):
    rows = grad_ref.shape[0]
    width = HEAD + ROPE
    scale = (HEAD + ROPE) ** -0.5

    @pl.when(pl.program_id(0) == 0)
    def _():
        key_grad_ref[...] = jnp.zeros_like(key_grad_ref)

    for h in range(2):
        part = slice(h * rows, (h + 1) * rows)
        grad = grad_ref[:, h * VHEAD : (h + 1) * VHEAD]
        latent_ref[part, :] = dot_t(
            grad, expand_ref[:, (2 * h + 1) * HEAD : (2 * h + 2) * HEAD]
        ).astype(BF)
        arrived = dot_t(latent_ref[part, :], keys_ref[:, :RANK])
        weights = weights_ref[part, :].astype(F32)
        mean = jnp.sum(weights * arrived, -1, keepdims=True)
        scores_ref[part, :] = (weights * (arrived - mean) * scale).astype(BF)
    key_grad_ref[...] += t_dot(queries_ref[...], scores_ref[...])
    key_grad_ref[:RANK, :] += t_dot(latent_ref[...], weights_ref[...])
    cosine, sine = cosine_ref[...], sine_ref[...]
    for h in range(2):
        part = slice(h * rows, (h + 1) * rows)
        query_grad = dot(scores_ref[part, :], keys_ref[...])
        latent = query_grad[:, :RANK].astype(BF)
        key_part = slice(2 * h * HEAD, (2 * h + 1) * HEAD)
        value_part = slice((2 * h + 1) * HEAD, (2 * h + 2) * HEAD)
        nope = dot(latent, expand_ref[:, key_part])
        first = query_grad[:, RANK : RANK + ROPE // 2]
        second = query_grad[:, RANK + ROPE // 2 :]
        query_grad_ref[:, h * width : (h + 1) * width] = jnp.concatenate(
            [nope, first * cosine + second * sine, second * cosine - first * sine], -1
        ).astype(BF)
        key_grad = t_dot(latent, nope_ref[:, h * HEAD : (h + 1) * HEAD]).astype(BF)
        value_grad = t_dot(
            mixed_ref[part, :], grad_ref[:, h * VHEAD : (h + 1) * VHEAD]
        ).astype(BF)
        count = order_ref.shape[0]
        height = RANK // count
        for j in range(count):
            target = pl.ds(pl.multiple_of(order_ref[j] * height, height), height)
            source = slice(j * height, (j + 1) * height)
            expand_grad_ref[target, key_part] = key_grad[source, :]
            expand_grad_ref[target, value_part] = value_grad[source, :]

    @pl.when(pl.program_id(0) == pl.num_programs(0) - 1)
    def _():
        key_out_ref[...] = key_grad_ref[...].T.astype(BF)


def attend_back(grad_out, expand, keys, weights, queries, mixed, nope, cosine, sine, order):
    rows = grad_out.shape[0]
    slot = keys.shape[0]
    whole = lambda *shape: pl.BlockSpec(shape, lambda i, order: (0,) * len(shape))
    return pl.pallas_call(
        attend_back_kernel,
        grid_spec=pltpu.PrefetchScalarGridSpec(
            num_scalar_prefetch=1,
            grid=(HEADS // 2,),
            in_specs=[
            pl.BlockSpec((rows, 2 * VHEAD), lambda i, order: (0, i)),
            pl.BlockSpec((RANK, 4 * HEAD), lambda i, order: (0, i)),
            whole(slot, RANK + ROPE),
            pl.BlockSpec((2 * rows, slot), lambda i, order: (i, 0)),
            pl.BlockSpec((2 * rows, RANK + ROPE), lambda i, order: (i, 0)),
            pl.BlockSpec((2 * rows, RANK), lambda i, order: (i, 0)),
            pl.BlockSpec((rows, 2 * HEAD), lambda i, order: (0, i)),
            whole(rows, ROPE // 2),
            whole(rows, ROPE // 2),
        ],
        out_specs=[
            pl.BlockSpec((rows, 2 * (HEAD + ROPE)), lambda i, order: (0, i)),
            pl.BlockSpec((RANK, 4 * HEAD), lambda i, order: (0, i)),
            whole(slot, RANK + ROPE),
        ],
        scratch_shapes=[
            pltpu.VMEM((RANK + ROPE, slot), F32),
            pltpu.VMEM((2 * rows, RANK), BF),
            pltpu.VMEM((2 * rows, slot), BF),
        ],
        ),
        out_shape=[
            jax.ShapeDtypeStruct((rows, HEADS * (HEAD + ROPE)), BF),
            jax.ShapeDtypeStruct((RANK, 2 * HEADS * HEAD), BF),
            jax.ShapeDtypeStruct((slot, RANK + ROPE), BF),
        ],
        compiler_params=pltpu.CompilerParams(vmem_limit_bytes=48 << 20),
        cost_estimate=pl.CostEstimate(
            flops=2 * HEADS * rows * slot * (3 * RANK + 2 * (RANK + ROPE)),
            bytes_accessed=2 * HEADS * rows * slot,
            transcendentals=0,
        ),
    )(order, grad_out, expand, keys, weights, queries, mixed, nope, cosine, sine)


def expert_kernel(sources, here_ref, rows_ref, router_ref, *refs):
    weights = refs[: 2 * sources]
    (
        row_grad_ref, units_ref, back_ref, gate_ref, logit_grad_ref, total_ref, probs_ref, share_ref,
    ) = refs[2 * sources :]
    step = pl.program_id(0)
    chunks = pl.num_programs(0) // sources

    @pl.when(step == 0)
    def _():
        logits = dot_t(router_ref[...], rows_ref[...])
        powers = jnp.exp(logits - jnp.max(logits, 0, keepdims=True))
        probs = powers / jnp.sum(powers, 0, keepdims=True)
        own = lax.broadcasted_iota(jnp.int32, probs.shape, 0) == here_ref[0]
        probs_ref[...] = probs
        gate_ref[...] = jnp.sum(jnp.where(own, probs, 0.0), 0, keepdims=True)
        share_ref[...] = jnp.zeros_like(share_ref)
        total_ref[...] = jnp.zeros_like(total_ref)

    def work(in_ref, slopes_ref):
        gate = dot_t(in_ref[0], rows_ref[...])
        up = dot_t(in_ref[1], rows_ref[...])
        back = slopes_ref[...]
        sigma = 1.0 / (1.0 + jnp.exp(-gate))
        act = gate * sigma
        units = (act * up).astype(BF)
        units_ref[...] = units
        share_ref[...] += jnp.sum(back * units.astype(F32), 0, keepdims=True)
        back = back * gate_ref[...]
        back_ref[0] = (back * up * (sigma * (1.0 + gate * (1.0 - sigma)))).astype(BF)
        back_ref[1] = (back * act).astype(BF)
        total_ref[...] += t_dot(back_ref[0], in_ref[0])
        total_ref[...] += t_dot(back_ref[1], in_ref[1])

    for k in range(sources):

        @pl.when(step // chunks == k)
        def _(k=k):
            work(weights[2 * k], weights[2 * k + 1])

    @pl.when(step == pl.num_programs(0) - 1)
    def _():
        probs = probs_ref[...]
        own = lax.broadcasted_iota(jnp.int32, probs.shape, 0) == here_ref[0]
        grad = probs * (own.astype(F32) - gate_ref[...]) * share_ref[...]
        logit_grad_ref[...] = grad.astype(BF)
        row_grad_ref[...] = (
            total_ref[...] + t_dot(logit_grad_ref[...], router_ref[...])
        ).astype(BF)


def expert_pass(here, rows, router, weights):
    count, width = rows.shape
    experts = router.shape[0]
    sources = len(weights)
    units = weights[0][1].shape[0]
    tile = next(t for t in (352, 176, 88, 64, 32, 16, units) if units % t == 0)
    chunks = units // tile
    once = pl.Buffered(1)
    in_specs = [
        pl.BlockSpec((count, width), lambda i, h: (0, 0), pipeline_mode=once),
        pl.BlockSpec((experts, width), lambda i, h: (0, 0)),
    ]
    for k in range(sources):
        at = lambda i, k=k: jnp.clip(i - k * chunks, 0, chunks - 1)
        in_specs.append(pl.BlockSpec((2, tile, width), lambda i, h, at=at: (0, at(i), 0)))
        in_specs.append(pl.BlockSpec((tile, count), lambda i, h, at=at: (at(i), 0)))
    return pl.pallas_call(
        functools.partial(expert_kernel, sources),
        grid_spec=pltpu.PrefetchScalarGridSpec(
            num_scalar_prefetch=1,
            grid=(sources * chunks,),
            in_specs=in_specs,
            out_specs=[
                pl.BlockSpec((count, width), lambda i, h: (0, 0), pipeline_mode=once),
                pl.BlockSpec((tile, count), lambda i, h: (i, 0)),
                pl.BlockSpec(
                    (None, 2, tile, count), lambda i, h: (i // chunks, 0, i % chunks, 0)
                ),
                pl.BlockSpec((1, count), lambda i, h: (0, 0)),
                pl.BlockSpec((experts, count), lambda i, h: (0, 0)),
            ],
            scratch_shapes=[
                pltpu.VMEM((count, width), F32),
                pltpu.VMEM((experts, count), F32),
                pltpu.VMEM((1, count), F32),
            ],
        ),
        out_shape=[
            jax.ShapeDtypeStruct((count, width), BF),
            jax.ShapeDtypeStruct((sources * units, count), BF),
            jax.ShapeDtypeStruct((sources, 2, units, count), BF),
            jax.ShapeDtypeStruct((1, count), F32),
            jax.ShapeDtypeStruct((experts, count), BF),
        ],
        compiler_params=pltpu.CompilerParams(vmem_limit_bytes=58 << 20),
        cost_estimate=pl.CostEstimate(
            flops=8 * count * width * sources * units,
            bytes_accessed=4 * (count + sources * units) * width,
            transcendentals=count * sources * units,
        ),
    )(here, rows, router, *[piece for pair in weights for piece in pair])


def per_device(
    tokens,
    lengths,
    routes,
    attn_gain,
    query_weight,
    latent_weight,
    latent_gain,
    expand_weight,
    output_weight,
    ffn_gain,
    router_weight,
    shared_in,
    shared_out,
    expert_in,
    expert_out,
    cotangent,
):
    local_rows = tokens.shape[1]
    model_width = tokens.shape[2]
    owners, shards = lax.axis_size("expert"), lax.axis_size("shard")
    experts_all = router_weight.shape[1]
    assert experts_all == owners
    topk_count = routes.shape[2]
    capacity = max(2, 9 * local_rows * topk_count // (8 * experts_all))
    capacity = -(-capacity // 8) * 8
    here = lax.axis_index("expert")

    query_blocks = row_blocks(query_weight)
    latent_blocks = row_blocks(latent_weight)
    gains = jnp.concatenate([attn_gain, ffn_gain, latent_gain])[None]
    gains = (
        jnp.where(
            lax.axis_index("shard") == 0,
            jnp.concatenate([gains, swap(gains)], 0),
            jnp.concatenate([swap(gains), gains], 0),
        )
        if shards == 2
        else lax.all_gather(gains, "shard", axis=0, tiled=True)
    ).astype(F32)
    cut = attn_gain.shape[0]
    gain_attn = gains[:, :cut].reshape(-1)
    gain_ffn = gains[:, cut : 2 * cut].reshape(-1)
    gain_latent = gains[:, 2 * cut :].reshape(-1)
    expand = whole_rows(expand_weight)
    here_index = here * local_rows + jnp.arange(local_rows, dtype=jnp.int32)
    query_segment, query_position, query_valid = layout(lengths[0], here_index)
    cosine, sine_table = rope_tables(query_position)
    live_rows = query_valid.astype(F32)[:, None]
    grad_out = cotangent[0].astype(F32) * live_rows
    grad_out_low = grad_out.astype(BF)

    expert_ids = jnp.arange(experts_all, dtype=jnp.int32)
    member = jnp.any(routes[0].T[None] == expert_ids[:, None, None], 1)
    token_ids = jnp.arange(local_rows, dtype=jnp.int32)
    earlier = (token_ids[:, None] < token_ids[None, :]).astype(BF)
    rank = dot(member.astype(BF), earlier).astype(jnp.int32)
    place_ids = jnp.arange(capacity, dtype=jnp.int32)
    spread = (
        (member[:, None, :] & (rank[:, None, :] == place_ids[None, :, None]))
        .reshape(experts_all * capacity, local_rows)
        .astype(BF)
    )

    def exchange(rows):
        return lax.all_to_all(
            rows.reshape(owners, capacity, model_width),
            "expert",
            split_axis=0,
            concat_axis=0,
            tiled=True,
        ).reshape(owners * capacity, model_width)


    inputs = tokens[0].astype(F32)
    inverse_attn = rms_scale(inputs)
    normed_attn = inputs * inverse_attn
    attn_in = (normed_attn * gain_attn).astype(BF)
    latent_raw = times(attn_in, latent_blocks)
    latent = latent_raw[:, :RANK]
    inverse_latent = rms_scale(latent)
    normed_latent = latent * inverse_latent
    latent_in = (normed_latent * gain_latent).astype(BF)
    key_rope = rotate(latent_raw[:, RANK:], cosine, sine_table).astype(BF)
    own_keys = jnp.concatenate([latent_in, key_rope], -1)
    expert_in_rows, expert_out_rows = expert_in[0].transpose(1, 2, 0), expert_out[0]
    (
        own_keys, output_weight, router_weight, shared_in, shared_out, expert_in_rows, expert_out_rows,
    ) = together(
        own_keys, output_weight, router_weight, shared_in, shared_out, expert_in_rows, expert_out_rows,
    )
    output_blocks = row_blocks(output_weight)
    router = whole_rows(router_weight)
    shared_out_blocks = row_blocks(shared_out)
    shared_in_blocks = row_blocks(shared_in)
    if shards == 2:
        expert_weights = [
            (expert_in_rows, expert_out_rows),
            (swap(expert_in_rows), swap(expert_out_rows)),
        ]
    else:
        expert_weights = [
            (
                lax.all_gather(expert_in_rows, "shard", axis=1, tiled=True),
                lax.all_gather(expert_out_rows, "shard", axis=0, tiled=True),
            )
        ]

    sent_grads = dot(spread, grad_out_low).astype(BF)
    keys, sent_grads = together(gather_slot(own_keys), sent_grads)
    received_grads = exchange(sent_grads)
    keys = keys.reshape(-1, RANK + ROPE)
    key_index = (
        (here ^ jnp.arange(owners, dtype=jnp.int32))[:, None] * local_rows
        + jnp.arange(local_rows, dtype=jnp.int32)[None, :]
    ).reshape(-1)

    query_raw = times(attn_in, query_blocks)
    key_segment = layout(lengths[0], key_index)[0]
    allowed = (query_segment[:, None] == key_segment[None, :]) & (
        key_index[None, :] <= here_index[:, None]
    )
    bias = jnp.where(allowed, 0.0, MASK_FILL).astype(F32)
    query_nope, queries, attention, mixed_latent, mixed_heads = attend(
        query_raw, cosine, sine_table, expand, keys, bias
    )
    (
        mixed_heads, received_grads, output_blocks, router, shared_in_blocks, shared_out_blocks,
        expert_weights,
    ) = together(
        mixed_heads, received_grads, output_blocks, router, shared_in_blocks, shared_out_blocks,
        expert_weights,
    )
    hidden_state = inputs + times(mixed_heads, output_blocks)
    inverse_ffn = rms_scale(hidden_state)
    normed_ffn = hidden_state * inverse_ffn
    ffn_in = (normed_ffn * gain_ffn).astype(BF)

    received = exchange(dot(spread, ffn_in).astype(BF))
    shared_both = times(ffn_in, shared_in_blocks)
    shared_act, shared_slope = silu_parts(shared_both[:, :FF_S])
    shared_up = shared_both[:, FF_S:]
    shared_hidden = (shared_act * shared_up).astype(BF)
    shared_result = times(shared_hidden, shared_out_blocks)
    grad_shared_hidden = times_back(grad_out_low, shared_out_blocks)
    grad_shared_gate = (grad_shared_hidden * shared_up * shared_slope).astype(BF)
    grad_shared_up = (grad_shared_hidden * shared_act).astype(BF)
    grad_ffn_in = times_back(
        jnp.concatenate([grad_shared_gate, grad_shared_up], -1), shared_in_blocks
    )
    out_slopes = [dot_t(weight_out, received_grads) for _, weight_out in expert_weights]
    out_message = jnp.concatenate([shared_hidden, grad_out_low], 1)
    in_message = jnp.concatenate([ffn_in, grad_shared_gate, grad_shared_up], 1)
    received, shared_result, grad_ffn_in, out_slopes, out_message, in_message = together(
        received, shared_result, grad_ffn_in, out_slopes, out_message, in_message
    )

    early_message = jnp.concatenate([attn_in, mixed_heads], 1)
    received, early_message = together(received, early_message)
    arrived = cross(out_message, 1), cross(in_message, 4), cross(early_message, 2)
    expert_results = expert_pass(
        here[None],
        received,
        router.T,
        [(weight_in, slopes) for (weight_in, _), slopes in zip(expert_weights, out_slopes)],
    )
    row_grads, hidden, hidden_grads, row_gate, row_grad_logits = expert_results

    returned_grads = exchange(row_grads)
    units = expert_weights[0][1].shape[0]
    row_gate = row_gate.reshape(-1, 1)
    weighted_grads = (row_gate * received_grads.astype(F32)).astype(BF)

    def expert_grads(j):
        return (
            dot(hidden_grads[j].reshape(2 * units, -1), received).reshape(2, units, -1),
            dot(hidden[j * units : (j + 1) * units], weighted_grads),
        )

    other_parts = [part.astype(BF) for part in expert_grads(len(expert_weights) - 1)]
    other_parts, arrived = together(other_parts, arrived)
    out_messages = group_messages(out_message, arrived[0])
    in_messages = group_messages(in_message, arrived[1])
    early_messages = group_messages(early_message, arrived[2])
    cut = 4096
    shared_halves = [
        product_halves(messages, left_part, messages, right_part, order)[:2]
        for messages, left_part, right_part, order in (
            (out_messages, (0, FF_S), (FF_S, model_width), (2, 8, 4)),
            (in_messages, (0, model_width), (model_width, cut), (1, 2, 8)),
            (in_messages, (0, model_width), (model_width + cut, 2 * FF_S - cut), (2, 1, 8)),
        )
    ]
    hidden, hidden_grads, shared_halves, early_messages = together(
        hidden, hidden_grads, shared_halves, early_messages
    )
    shared_sums = [
        [kept, cross(sent, bit)] for (kept, sent), bit in zip(shared_halves, (2, 1, 2))
    ]
    row_out = 0.0
    for j, (_, weight) in enumerate(expert_weights):
        row_out = row_out + t_dot(hidden[j * units : (j + 1) * units], weight)
    row_out = (row_gate * row_out).astype(BF)
    if shards == 2:
        hidden, hidden_grads, other_parts = together(
            hidden, hidden_grads, [swap(part) for part in other_parts]
        )
        grad_expert_in, grad_expert_out = [
            own + other.astype(F32) for own, other in zip(expert_grads(0), other_parts)
        ]
    else:
        grad_expert_in, grad_expert_out = [
            lax.psum_scatter(part, "shard", scatter_dimension=part.ndim - 2, tiled=True).astype(F32)
            for part in other_parts
        ]
    grad_router = dot(row_grad_logits, received)
    returned_grads, row_out, grad_expert_in, grad_expert_out, grad_router = together(
        returned_grads, row_out, grad_expert_in, grad_expert_out, grad_router
    )
    grad_expert_in = grad_expert_in.transpose(2, 0, 1)[None]
    grad_expert_out = grad_expert_out[None]
    returned = exchange(row_out)
    grad_ffn_in = grad_ffn_in + t_dot(spread, returned_grads)
    grad_gain_ffn = jnp.sum(grad_ffn_in * normed_ffn, 0)
    grad_hidden_state = grad_out + norm_back(grad_ffn_in * gain_ffn, normed_ffn, inverse_ffn)

    grad_attn_out = grad_hidden_state.astype(BF)
    grad_mixed = times_back(grad_attn_out, output_blocks).astype(BF)
    grad_mixed, grad_attn_out = together(grad_mixed, grad_attn_out)
    out_arrived = cross(grad_attn_out, 2)
    expand_order = (2, 1, 4, 8)
    if shards == 2:
        differs = here ^ jnp.arange(owners, dtype=jnp.int32)
        place = sum((differs // bit % 2) << (3 - k) for k, bit in enumerate(expand_order))
        other = lax.axis_index("shard") ^ jnp.arange(2, dtype=jnp.int32)
        block_order = (other[None, :] * owners + place[:, None]).reshape(-1).astype(jnp.int32)
    else:
        block_order = jnp.zeros((1,), jnp.int32)
    attention_grads = attend_back(
        grad_mixed,
        expand,
        keys,
        attention,
        queries,
        mixed_latent,
        query_nope,
        cosine,
        sine_table,
        block_order,
    )
    attention_grads, shared_sums, out_arrived = together(
        attention_grads, shared_sums, out_arrived
    )
    grad_query_raw, grad_expand, grad_keys = attention_grads

    query_arrived = cross(grad_query_raw, 2)
    own_query = grad_query_raw
    if shards == 2:
        half_rank = RANK // 2
        expand_pair = [swap(grad_expand[half_rank:]), grad_expand]
    else:
        expand_pair = pair_partial(grad_expand, expand_order)
    grad_own_keys, returned, query_arrived, grad_query_raw, expand_pair = together(
        scatter_slot(grad_keys.reshape(owners, local_rows, -1)),
        returned,
        query_arrived,
        grad_query_raw,
        expand_pair,
    )
    grad_latent_in = grad_own_keys[:, :RANK]
    grad_gain_latent = jnp.sum(grad_latent_in * normed_latent, 0)
    grad_latent = norm_back(grad_latent_in * gain_latent, normed_latent, inverse_latent)
    grad_latent_raw = jnp.concatenate(
        [grad_latent, rotate_back(grad_own_keys[:, RANK:], cosine, sine_table)], -1
    ).astype(BF)
    latent_message = jnp.pad(grad_latent_raw, ((0, 0), (0, -grad_latent_raw.shape[1] % 128)))
    latent_messages = group_messages(latent_message, cross(latent_message, 2))
    query_messages = group_messages(own_query, query_arrived)
    out_messages = group_messages(grad_attn_out, out_arrived)
    in_part, heads_part = (0, model_width), (model_width, HEADS * VHEAD)
    whole_part = lambda array: (0, array.shape[1])
    *query_halves, picked = product_halves(
        early_messages, in_part, query_messages, whole_part(grad_query_raw), (1, 4, 8)
    )
    output_halves = product_halves(
        early_messages, heads_part, out_messages, whole_part(grad_attn_out), (4, 1, 8)
    )[:2]
    latent_product = dot(picked, jnp.concatenate(latent_messages, 0)).astype(BF)
    latent_halves = jnp.split(latent_product, 2, 0)
    grad_attn_in = times_back(grad_latent_raw, latent_blocks) + times_back(
        grad_query_raw, query_blocks
    )
    grad_gain_attn = jnp.sum(grad_attn_in * normed_attn, 0)
    tokens_grad = grad_hidden_state + norm_back(grad_attn_in * gain_attn, normed_attn, inverse_attn)
    devices = owners * shards
    rows = model_width // devices
    small = jnp.concatenate(
        [
            vector.reshape(devices, -1)
            for vector in (grad_router.T, grad_gain_attn, grad_gain_ffn, grad_gain_latent)
        ],
        1,
    )
    cuts = [rows * experts_all, rows * (experts_all + 1), rows * (experts_all + 2)]
    small = jnp.pad(small, ((0, 0), (0, -small.shape[1] % 2048))).reshape(devices * 16, -1)
    small_pair = pair_partial(small.astype(BF), expand_order)
    sums = reduce_all(
        [
            ((1, 4, 8), [latent_halves[0]], latent_halves[1]),
            ((8, 4), shared_sums[0], None),
            (expand_order, expand_pair, None),
            ((1, 4, 8), [query_halves[0]], query_halves[1]),
            ((2, 8), shared_sums[1], None),
            ((4, 1, 8), [output_halves[0]], output_halves[1]),
            ((1, 8), shared_sums[2], None),
            (expand_order, small_pair, None),
        ],
        REDUCE_STEPS,
    )
    grad_latent_weight = sums[0][:, : RANK + ROPE]
    grad_shared_out = sums[1][: FF_S // devices]
    grad_expand, grad_query = sums[2:4]
    grad_shared_in = jnp.concatenate([sums[4], sums[6]], 1)
    grad_output = sums[5]
    small = sums[7].reshape(-1)
    routed = t_dot(spread, returned)
    block_result = hidden_state + shared_result + routed
    return (
        block_result.astype(BF)[None],
        tokens_grad.astype(BF)[None],
        small[cuts[0] : cuts[1]],
        grad_query,
        grad_latent_weight,
        small[cuts[2] : cuts[2] + RANK // devices],
        grad_expand,
        grad_output,
        small[cuts[1] : cuts[2]],
        small[: cuts[0]].reshape(rows, experts_all),
        grad_shared_in,
        grad_shared_out,
        grad_expert_in,
        grad_expert_out,
    )


def solution(mesh):
    return jax.shard_map(
        per_device,
        mesh=mesh,
        in_specs=(
            P("shard", "expert", None),
            P("shard", None),
            P("shard", "expert", None),
            P("shard"),
            P("shard", None),
            P("shard", None),
            P("shard"),
            P("shard", None),
            P("shard", None),
            P("shard"),
            P("shard", None),
            P("shard", None),
            P("shard", None),
            P("expert", None, None, "shard"),
            P("expert", "shard", None),
            P("shard", "expert", None),
        ),
        out_specs=(
            P("shard", "expert", None),
            P("shard", "expert", None),
            P(("expert", "shard")),
            P(("expert", "shard"), None),
            P(("expert", "shard"), None),
            P(("expert", "shard")),
            P(("expert", "shard"), None),
            P(("expert", "shard"), None),
            P(("expert", "shard")),
            P(("expert", "shard"), None),
            P(("expert", "shard"), None),
            P(("expert", "shard"), None),
            P("expert", None, None, "shard"),
            P("expert", "shard", None),
        ),
        check_vma=False,
    )
```
